32 devices in a mesh: group: 2 (over y), expert: 4 (over x, core), shard: 4 (over z).
Axes of the slice: x: 2, y: 2, z: 4, core: 2. Of those that a mesh axis runs over, the one named last changes fastest.
Arguments:
- tokens: bfloat16 [8192, 2048], P(('group', 'expert', 'shard')), may hold values from -6 to 6
- cotangent: bfloat16 [8192, 2048], P(('group', 'expert', 'shard')), may hold values from -6 to 6
- gain_attn: float32 [2048], replicated, may hold values from 0.1 to 1.9
- w_query: bfloat16 [2048, 3072], P('shard'), may hold values from -0.125 to 0.125
- w_latent: bfloat16 [2048, 576], P('shard'), may hold values from -0.125 to 0.125
- gain_latent: float32 [512], replicated, may hold values from 0.1 to 1.9
- w_keyval: bfloat16 [512, 4096], P('shard'), may hold values from -0.25 to 0.25
- w_output: bfloat16 [2048, 2048], P('shard'), may hold values from -0.75 to 0.75
- gain_ffn: float32 [2048], replicated, may hold values from 0.1 to 1.9
- w_shared_gate: bfloat16 [2048, 2816], P('shard'), may hold values from -0.125 to 0.125
- w_shared_up: bfloat16 [2048, 2816], P('shard'), may hold values from -0.125 to 0.125
- w_shared_down: bfloat16 [2816, 2048], P('shard'), may hold values from -0.109375 to 0.109375
- w_router: bfloat16 [2048, 16], P('shard'), may hold values from -0.25 to 0.25
- expert_gate: bfloat16 [16, 2048, 1408], P(('expert', 'shard')), may hold values from -0.125 to 0.125
- expert_up: bfloat16 [16, 2048, 1408], P(('expert', 'shard')), may hold values from -0.125 to 0.125
- expert_down: bfloat16 [16, 1408, 2048], P(('expert', 'shard')), may hold values from -0.875 to 0.875
- segments: int32 [8192], P('group'), may hold values from 0 to 8, as said below
- positions: int32 [8192], P('group'), may hold values from 0 to 2303, as said below
- routes: int32 [8192, 6], P(('group', 'expert', 'shard')), may hold values from 0 to 15, all different within a row; in each aligned block of 256 rows (0 to 255, 256 to 511, ...) at most 144 rows name the same one
Outputs:
- output: bfloat16 [8192, 2048], P(('group', 'expert', 'shard'))
- grad_tokens: float32 [8192, 2048], P(('group', 'expert', 'shard'))
- grad_gain_attn: float32 [2048], P(('group', 'expert', 'shard'))
- grad_w_query: float32 [2048, 3072], P(('group', 'expert', 'shard'))
- grad_w_latent: float32 [2048, 576], P(('group', 'expert', 'shard'))
- grad_gain_latent: float32 [512], P(('group', 'expert', 'shard'))
- grad_w_keyval: float32 [512, 4096], P(('group', 'expert', 'shard'))
- grad_w_output: float32 [2048, 2048], P(('group', 'expert', 'shard'))
- grad_gain_ffn: float32 [2048], P(('group', 'expert', 'shard'))
- grad_w_shared_gate: float32 [2048, 2816], P(('group', 'expert', 'shard'))
- grad_w_shared_up: float32 [2048, 2816], P(('group', 'expert', 'shard'))
- grad_w_shared_down: float32 [2816, 2048], P(('group', 'expert', 'shard'))
- grad_w_router: float32 [2048, 16], P(('group', 'expert', 'shard'))
- grad_expert_gate: float32 [16, 2048, 1408], P(('expert', 'shard'), 'group')
- grad_expert_up: float32 [16, 2048, 1408], P(('expert', 'shard'), 'group')
- grad_expert_down: float32 [16, 1408, 2048], P(('expert', 'shard'), 'group')
The draws below stay inside these ranges and needn't reach their ends.
Inputs may be any that keep to these rules, and one draw needn't show every extreme that they name: `segments`: each aligned run of 256 tokens is one piece of one sequence: either 256 consecutive prompt positions starting at a multiple of 256, or a whole continuation. Each run of 4096 tokens holds 1 prompt group whole, in any order of pieces; a group's prompt has segment id group * (9) and its continuations group * 9 + 1 to group * 9 + 8. Prompt tokens have positions 0 to 2047 in order within each piece; a continuation's tokens have positions 2048 to 2303 in order. `routes`: each row names 6 different experts; among the 256 rows of one device no expert is named more than 144 times.
All inputs are finite; a program needn't handle non-finite values.
Results may differ from the reference program's by a relative error of at most 0.023.
Values may be sent and summed in bfloat16 or wider, within the bound.
No kernel may reach another device: no remote copies, remote signals or barrier semaphores. Data moves between devices by JAX's collectives and lax.ppermute only.
A program may use at most 576 MiB of HBM per device.

```python
import math
import jax
import jax.numpy as jnp
import numpy as np
from jax import lax

D = 2048
HEADS = 16
NOPE = 128
ROPE = 64
VDIM = 128
LATENT = 512
FFE = 1408
TOPK = 6
SHARED = 2816
BLOCK = 256
PROMPT = 2048
NCONT = 8
GROUP_TOK = 4096
ROW_DEV = 16
TOK_DEV = 256
ROWTOK = 4096
TOKENS = 8192
EXPERTS = 16
CAP = 144


def layout_blocks(key):
    run_blocks = ROWTOK // BLOCK
    group_blocks = GROUP_TOK // BLOCK
    prompt_blocks = PROMPT // BLOCK
    canonical = jnp.arange(run_blocks, dtype=jnp.int32)
    group_id = canonical // group_blocks
    inner_pos = canonical % group_blocks
    is_prompt = inner_pos < prompt_blocks
    block_seg = group_id * (NCONT + 1) + jnp.where(is_prompt, 0, inner_pos - prompt_blocks + 1)
    block_pos = jnp.where(is_prompt, inner_pos * BLOCK, PROMPT)
    row_count = TOKENS // ROWTOK
    row_keys = jax.random.split(jax.random.fold_in(key, 11), row_count)
    orders = jax.vmap(lambda row_key: jax.random.permutation(row_key, run_blocks))(row_keys)
    seg_grid = block_seg[orders][:, :, None] + jnp.zeros((1, 1, BLOCK), jnp.int32)
    pos_grid = block_pos[orders][:, :, None] + jnp.arange(BLOCK, dtype=jnp.int32)[None, None, :]
    return (seg_grid.reshape(TOKENS).astype(jnp.int32), pos_grid.reshape(TOKENS).astype(jnp.int32))


def draw_segments(key, part):
    return layout_blocks(key)[0]


def draw_positions(key, part):
    return layout_blocks(key)[1]


def shard_levels(own_key, dims, shards, smallest, largest):
    loudness = 1.0
    for position, blocks in shards:
        steps = jax.random.uniform(jax.random.fold_in(jax.random.fold_in(own_key, 6), position), (blocks,), jnp.float32, smallest / len(shards), largest / len(shards))
        loudness = loudness * jnp.repeat(jnp.exp(steps), dims[position] // blocks).reshape((-1,) + (1,) * (len(dims) - 1 - position))
    return loudness


def deal_out(own_key, own, number, rows, amount, top, bound, slope):
    sequence = jax.random.permutation(own_key, amount)
    heavy_load, ordinary = portions_of(amount, rows * top, bound, slope, True), portions_of(amount, rows * top, bound, slope, False)
    places = jnp.arange(amount)

    def named(lengths, offset_by):
        used = int((lengths > 0).sum())
        fixed = max(1, used // 4)
        shifted = fixed + (places - fixed + offset_by * (used - fixed)) % max(1, amount - fixed)
        return jnp.zeros((amount,), jnp.int32).at[sequence[jnp.where(places < fixed, places, shifted)]].set(jnp.asarray(lengths, jnp.int32))

    lengths = jnp.where(number % 4 == 0, named(heavy_load, number // 4), named(ordinary, number - number // 4 - 1))
    mixed = jax.random.permutation(jax.random.fold_in(own, 3), amount)
    source_of, taker = mixed[0:amount // 2 * 2:2], mixed[1:amount // 2 * 2:2]
    room = jnp.minimum(lengths[source_of] - 1, bound - lengths[taker]) // 2
    room = jnp.where((source_of == sequence[0]) | (taker == sequence[0]) | (lengths[taker] == 0), 0, jnp.maximum(room, 0))
    shifted = jax.random.randint(jax.random.fold_in(own, 4), (amount // 2,), 0, 1 << 20) % (room + 1)
    lengths = lengths.at[source_of].add(-shifted).at[taker].add(shifted)
    items = jnp.searchsorted(jnp.cumsum(lengths), jnp.arange(rows * top), side="right").astype(jnp.int32)
    grid = items.reshape(top, rows).T
    grid = grid[jax.random.permutation(jax.random.fold_in(own, 1), rows)]
    offset_by = jax.random.randint(jax.random.fold_in(own, 2), (rows, 1), 0, top)
    return jnp.take_along_axis(grid, (jnp.arange(top)[None, :] + offset_by) % top, axis=1)


def portions_of(number_of, total, most, skew, full):
    weights = [(1 << 20) // math.isqrt(standing ** skew) + 1 for standing in range(1, number_of + 1)]
    largest = most if full else min(most, max(-(-total // number_of), total * weights[0] // sum(weights)))
    least = 1 if total - largest >= number_of - 1 else 0
    given, spare = [largest] + [least] * (number_of - 1), total - largest - least * (number_of - 1)
    while spare > 0:
        candidates = [i for i in range(1, number_of) if given[i] < largest] or [i for i in range(1, number_of) if given[i] < most]
        whole, left = sum([weights[i] for i in candidates]), spare
        for i in candidates:
            more = min(most - given[i], max(1, left * weights[i] // whole), spare)
            given[i] = given[i] + more
            spare = spare - more
    return np.array(given)


def gaussian(own_key, shape, deviation, bound, pieces=(), kind=jnp.bfloat16):
    drawn = deviation * jax.random.normal(own_key, shape, jnp.float32)
    if pieces:
        drawn = drawn * shard_levels(own_key, shape, pieces, -0.22, 0.18)
    return jnp.clip(drawn, -bound, bound).astype(kind)


def setup_inputs(seed: int = 0) -> dict:
    key_of = jax.random.split(jax.random.key(seed), 20)
    tokens = gaussian(key_of[0], (TOKENS, D), 1.0, 6.0, ((0, 32),))
    cotangent = gaussian(key_of[1], (TOKENS, D), 1.0, 6.0, ((0, 32),))
    gain_attn = jnp.clip(1.0 + 0.18 * jax.random.normal(key_of[2], (D,), jnp.float32), 0.1, 1.9)
    w_query = gaussian(key_of[3], (D, HEADS * (NOPE + ROPE)), D ** -0.5, 0.125, ((0, 4),))
    w_latent = gaussian(key_of[4], (D, LATENT + ROPE), D ** -0.5, 0.125, ((0, 4),))
    gain_latent = jnp.clip(1.0 + 0.18 * jax.random.normal(key_of[5], (LATENT,), jnp.float32), 0.1, 1.9)
    w_keyval = gaussian(key_of[6], (LATENT, HEADS * (NOPE + VDIM)), LATENT ** -0.5, 0.25, ((0, 4),))
    w_output = gaussian(key_of[7], (HEADS * VDIM, D), (HEADS * VDIM // 32) ** -0.5, 0.75, ((0, 4),))
    gain_ffn = jnp.clip(1.0 + 0.18 * jax.random.normal(key_of[8], (D,), jnp.float32), 0.1, 1.9)
    w_shared_gate = gaussian(key_of[9], (D, SHARED), D ** -0.5, 0.125, ((0, 4),))
    w_shared_up = gaussian(key_of[10], (D, SHARED), D ** -0.5, 0.125, ((0, 4),))
    w_shared_down = gaussian(key_of[11], (SHARED, D), SHARED ** -0.5, 0.109375, ((0, 4),))
    w_router = gaussian(key_of[12], (D, EXPERTS), (D // 4) ** -0.5, 0.25, ((0, 4),))
    expert_gate = gaussian(key_of[13], (EXPERTS, D, FFE), D ** -0.5, 0.125, ((0, 16),))
    expert_up = gaussian(key_of[14], (EXPERTS, D, FFE), D ** -0.5, 0.125, ((0, 16),))
    expert_down = gaussian(key_of[15], (EXPERTS, FFE, D), (FFE // 32) ** -0.5, 0.875, ((0, 16),))
    segments = draw_segments(jax.random.fold_in(key_of[19], 71), 0)
    positions = draw_positions(jax.random.fold_in(key_of[19], 71), 0)
    routes_keys = jax.random.split(jax.random.fold_in(key_of[18], 1), TOKENS // TOK_DEV)
    routes_turns = jax.random.permutation(jax.random.fold_in(key_of[18], 3), TOKENS // TOK_DEV)
    routes = jax.vmap(lambda own, number: deal_out(jax.random.fold_in(key_of[18], 2), own, number, TOK_DEV, EXPERTS, TOPK, CAP, 2))(routes_keys, routes_turns).reshape((TOKENS, TOPK))
    return dict(tokens=tokens, cotangent=cotangent, gain_attn=gain_attn, w_query=w_query, w_latent=w_latent, gain_latent=gain_latent, w_keyval=w_keyval, w_output=w_output, gain_ffn=gain_ffn, w_shared_gate=w_shared_gate, w_shared_up=w_shared_up, w_shared_down=w_shared_down, w_router=w_router, expert_gate=expert_gate, expert_up=expert_up, expert_down=expert_down, segments=segments, positions=positions, routes=routes)


@jax.custom_vjp
def low(v):
    return lax.optimization_barrier(v.astype(jnp.bfloat16)).astype(jnp.float32)

@jax.custom_vjp
def low_back(v):
    return v

def low_keep(v):
    return (low(v), None)

def low_pass(kept, grad):
    return (grad,)

def back_keep(v):
    return (v, None)

def back_low(kept, grad):
    return (low(grad),)
low.defvjp(low_keep, low_pass)
low_back.defvjp(back_keep, back_low)
EPS = 1e-06
HIGH = lax.Precision.HIGHEST

def matmul(left, right):
    return jnp.dot(left, right, precision=HIGH, preferred_element_type=jnp.float32)

def norm_rows(values, gain):
    return values * lax.rsqrt(lax.optimization_barrier(jnp.mean(values * values, axis=-1, keepdims=True)) + EPS) * gain

def angles(pos_list, rot_width):
    half_width = rot_width // 2
    freq = 10000.0 ** (-2.0 * jnp.arange(half_width, dtype=jnp.float32) / rot_width)
    theta = pos_list.astype(jnp.float32)[:, None] * freq[None, :]
    return (jnp.cos(theta), jnp.sin(theta))

def rotate(values, cosine, sine):
    half_width = values.shape[-1] // 2
    first_half = values[..., :half_width]
    second_half = values[..., half_width:]
    return jnp.concatenate([first_half * cosine - second_half * sine, second_half * cosine + first_half * sine], axis=-1)

def route_places(row_routes):
    dev_routes = row_routes.reshape(ROW_DEV, TOK_DEV * TOPK)
    hot_table = (dev_routes[:, :, None] == jnp.arange(EXPERTS, dtype=jnp.int32)[None, None, :]).astype(jnp.int32)
    before = jnp.cumsum(hot_table, axis=1) - hot_table
    slot_num = lax.optimization_barrier(jnp.sum(before * hot_table, axis=2))
    device_num = jnp.arange(ROW_DEV, dtype=jnp.int32)[:, None]
    places = dev_routes * (ROW_DEV * CAP) + device_num * CAP + slot_num
    return places.reshape(ROWTOK, TOPK)

def forward(tokens, gain_attn, w_query, w_latent, gain_latent, w_keyval, w_output, gain_ffn, w_shared_gate, w_shared_up, w_shared_down, w_router, expert_gate, expert_up, expert_down, segments, positions, routes):
    all_rows = tokens.shape[0]
    row_count = all_rows // ROWTOK
    hidden1 = low(norm_rows(tokens, gain_attn))
    query_pre = low_back(matmul(hidden1, w_query)).reshape(all_rows, HEADS, NOPE + ROPE)
    cosine, sine = angles(positions, ROPE)
    query = low(jnp.concatenate([query_pre[..., :NOPE], rotate(query_pre[..., NOPE:], cosine[:, None, :], sine[:, None, :])], axis=-1))
    latent = low_back(matmul(hidden1, w_latent))
    compressed = low(norm_rows(latent[:, :LATENT], gain_latent))
    key_rope = low(rotate(latent[:, LATENT:], cosine, sine))
    keyval = low(matmul(compressed, w_keyval)).reshape(all_rows, HEADS, NOPE + VDIM)
    score_scale = 1.0 / math.sqrt(NOPE + ROPE)
    block_rows = min(512, ROWTOK)
    num_blocks = ROWTOK // block_rows

    def attend_row(pack):
        row_query, row_keyval, row_rope, row_seg, row_pos = pack
        key_nope = row_keyval[..., :NOPE]
        values = row_keyval[..., NOPE:]
        key_group = row_seg // (NCONT + 1)
        key_prompt = row_seg % (NCONT + 1) == 0

        def one_block(inner):
            blk_query, blk_seg, blk_pos = inner
            raw = jnp.einsum('qhn,khn->hqk', blk_query[..., :NOPE], key_nope, precision=HIGH)
            raw = raw + jnp.einsum('qhr,kr->hqk', blk_query[..., NOPE:], row_rope, precision=HIGH)
            scores = low_back(raw * score_scale)
            allowed = (key_group[None, :] == (blk_seg // (NCONT + 1))[:, None]) & (row_pos[None, :] <= blk_pos[:, None])
            allowed = allowed & (key_prompt[None, :] | (row_seg[None, :] == blk_seg[:, None]))
            allowed = allowed[None, :, :]
            top_score = lax.optimization_barrier(jnp.max(jnp.where(allowed, scores, -jnp.inf), axis=-1, keepdims=True))
            exp_terms = jnp.where(allowed, jnp.exp(jnp.where(allowed, scores, top_score) - top_score), 0.0)
            prob_attn = low(exp_terms / lax.optimization_barrier(jnp.sum(exp_terms, axis=-1, keepdims=True)))
            return jnp.einsum('hqk,khv->qhv', prob_attn, values, precision=HIGH)
        parts = lax.map(jax.checkpoint(one_block), (row_query.reshape(num_blocks, block_rows, HEADS, NOPE + ROPE), row_seg.reshape(num_blocks, block_rows), row_pos.reshape(num_blocks, block_rows)))
        return parts.reshape(ROWTOK, HEADS, VDIM)
    mixed = lax.map(attend_row, (query.reshape(row_count, ROWTOK, HEADS, NOPE + ROPE), keyval.reshape(row_count, ROWTOK, HEADS, NOPE + VDIM), key_rope.reshape(row_count, ROWTOK, ROPE), segments.reshape(row_count, ROWTOK), positions.reshape(row_count, ROWTOK)))
    mixed = low_back(low(mixed.reshape(all_rows, HEADS * VDIM)))
    after = tokens + low_back(matmul(mixed, w_output))
    hidden2 = low(norm_rows(after, gain_ffn))
    shared_gate = low_back(matmul(hidden2, w_shared_gate))
    shared_up = low_back(matmul(hidden2, w_shared_up))
    shared_mid = low(jax.nn.silu(shared_gate) * shared_up)
    shared = low_back(matmul(shared_mid, w_shared_down))
    logits = low_back(matmul(hidden2, w_router))
    logit_top = lax.optimization_barrier(jnp.max(logits, axis=-1, keepdims=True))
    logit_exp = jnp.exp(logits - logit_top)
    router_prob = logit_exp / lax.optimization_barrier(jnp.sum(logit_exp, axis=-1, keepdims=True))
    route_weight = jnp.take_along_axis(router_prob, routes, axis=1)

    def expert_row(pack):
        row_hidden, row_weight, row_routes = pack
        places = route_places(row_routes)
        token_num = jnp.arange(ROWTOK * TOPK, dtype=jnp.int32) // TOPK
        token_of = jnp.full((EXPERTS * ROW_DEV * CAP,), ROWTOK, jnp.int32).at[places.reshape(-1)].set(token_num)
        padded = jnp.concatenate([row_hidden, jnp.zeros((1, D), jnp.float32)], axis=0)
        sent = low_back(padded[token_of]).reshape(EXPERTS, ROW_DEV * CAP, D)
        gate_pre = low_back(jnp.einsum('erd,edf->erf', sent, expert_gate, precision=HIGH))
        up_pre = low_back(jnp.einsum('erd,edf->erf', sent, expert_up, precision=HIGH))
        middle = low(jax.nn.silu(gate_pre) * up_pre)
        result = low_back(low(jnp.einsum('erf,efd->erd', middle, expert_down, precision=HIGH)))
        picked = result.reshape(EXPERTS * ROW_DEV * CAP, D)[places]
        return jnp.einsum('tk,tkd->td', row_weight, picked, precision=HIGH)
    routed = lax.map(jax.checkpoint(expert_row), (hidden2.reshape(row_count, ROWTOK, D), route_weight.reshape(row_count, ROWTOK, TOPK), routes.reshape(row_count, ROWTOK, TOPK)))
    return after + shared + routed.reshape(all_rows, D)

def reference(tokens, cotangent, gain_attn, w_query, w_latent, gain_latent, w_keyval, w_output, gain_ffn, w_shared_gate, w_shared_up, w_shared_down, w_router, expert_gate, expert_up, expert_down, segments, positions, routes):
    floats = (tokens, gain_attn, w_query, w_latent, gain_latent, w_keyval, w_output, gain_ffn, w_shared_gate, w_shared_up, w_shared_down, w_router, expert_gate, expert_up, expert_down)
    floats = tuple((item.astype(jnp.float32) for item in floats))

    def run(*arrays):
        return forward(*arrays, segments, positions, routes)
    result, pullback = jax.vjp(run, *floats)
    grads = pullback(cotangent.astype(jnp.float32))
    return (result.astype(jnp.bfloat16), grads[0], grads[1], grads[2], grads[3], grads[4], grads[5], grads[6], grads[7], grads[8], grads[9], grads[10], grads[11], grads[12], grads[13], grads[14])
```

```python
import functools
import math

import jax
import jax.numpy as jnp
from jax import lax
from jax.experimental import pallas as pl
from jax.experimental.pallas import tpu as pltpu
from jax.sharding import PartitionSpec as P

HEADS = 16
NOPE = 128
ROPE = 64
VDIM = 128
LATENT = 512
BLOCK = 256
PROMPT = 2048
NCONT = 8
QDIM = NOPE + ROPE
KVDIM = NOPE + VDIM
GROUP_BLOCKS = PROMPT // BLOCK + NCONT
GROUP_TOK = GROUP_BLOCKS * BLOCK

EPS = 1e-06
ALL = ("group", "expert", "shard")
ROW = ("expert", "shard")
SCALE = 1.0 / math.sqrt(NOPE + ROPE)
F32 = jnp.float32
BF16 = jnp.bfloat16


def matmul(left, right):
    return jnp.dot(left, right, preferred_element_type=F32)


def matmul_nt(left, right):
    return lax.dot_general(left, right, (((1,), (1,)), ((), ())), preferred_element_type=F32)


def matmul_tn(left, right):
    return lax.dot_general(left, right, (((0,), (0,)), ((), ())), preferred_element_type=F32)


def rms_parts(values):
    inverse = lax.rsqrt(jnp.mean(values * values, axis=-1, keepdims=True) + EPS)
    return (values * inverse, inverse)


def norm_back(grad_in, normed, inverse, gain):
    scaled = grad_in * gain
    gain_grad = jnp.sum(grad_in * normed, axis=0)
    input_grad = inverse * (scaled - normed * jnp.mean(scaled * normed, axis=-1, keepdims=True))
    return (input_grad, gain_grad)


def angles(pos_list, rot_width):
    half_width = rot_width // 2
    freq = 10000.0 ** (-2.0 * jnp.arange(half_width, dtype=F32) / rot_width)
    theta = pos_list.astype(F32)[:, None] * freq[None, :]
    return (jnp.cos(theta), jnp.sin(theta))


def rotate(values, cosine, sine):
    half_width = values.shape[-1] // 2
    first_half = values[..., :half_width]
    second_half = values[..., half_width:]
    return jnp.concatenate(
        [first_half * cosine - second_half * sine, second_half * cosine + first_half * sine],
        axis=-1,
    )


def unrotate(grad_in, cosine, sine):
    return rotate(grad_in, cosine, -sine)


def silu_parts(values):
    sigmoid = jax.nn.sigmoid(values)
    return (values * sigmoid, sigmoid * (1.0 + values * (1.0 - sigmoid)))


def trade(buffer, axes):
    return lax.all_to_all(buffer, axes, split_axis=0, concat_axis=0, tiled=True)


def take_blocks(blocks, index):
    shape = blocks.shape[1:]

    def body(index_ref, src_ref, dst_ref):
        dst_ref[...] = src_ref[...]

    return pl.pallas_call(
        body,
        grid_spec=pltpu.PrefetchScalarGridSpec(
            num_scalar_prefetch=1,
            grid=(index.shape[0],),
            in_specs=[pl.BlockSpec((1,) + shape, lambda i, at: (at[i], 0, 0))],
            out_specs=pl.BlockSpec((1,) + shape, lambda i, at: (i, 0, 0)),
        ),
        out_shape=jax.ShapeDtypeStruct((index.shape[0],) + shape, blocks.dtype),
        name="take_blocks",
    )(index, blocks)


def causal(count):
    rows = lax.broadcasted_iota(jnp.int32, (count, count), 0)
    cols = lax.broadcasted_iota(jnp.int32, (count, count), 1)
    return cols <= rows


def attend(query, key, value):
    q_p, q_c = query[:PROMPT], query[PROMPT:]
    k_p, k_c = key[:PROMPT], key[PROMPT:]
    v_p, v_c = value[:PROMPT], value[PROMPT:]
    own = lambda a: a.reshape(NCONT, BLOCK, a.shape[-1])
    s_p = jnp.where(causal(PROMPT), matmul_nt(q_p, k_p) * SCALE, -jnp.inf)
    s_cp = matmul_nt(q_c, k_p) * SCALE
    s_cc = jnp.einsum("cqd,ckd->cqk", own(q_c), own(k_c), preferred_element_type=F32) * SCALE
    s_cc = jnp.where(causal(BLOCK)[None], s_cc, -jnp.inf)
    m_p = jnp.max(s_p, axis=-1, keepdims=True)
    e_p = jnp.exp(s_p - m_p)
    z_p = jnp.sum(e_p, axis=-1, keepdims=True)
    o_p = matmul((e_p / z_p).astype(BF16), v_p)
    m_c = jnp.maximum(
        jnp.max(s_cp, axis=-1, keepdims=True),
        jnp.max(s_cc, axis=-1, keepdims=True).reshape(NCONT * BLOCK, 1),
    )
    e_cp = jnp.exp(s_cp - m_c)
    e_cc = jnp.exp(s_cc - own(m_c))
    z_c = jnp.sum(e_cp, axis=-1, keepdims=True) + jnp.sum(e_cc, axis=-1, keepdims=True).reshape(
        NCONT * BLOCK, 1
    )
    o_c = matmul((e_cp / z_c).astype(BF16), v_p) + jnp.einsum(
        "cqk,ckd->cqd", (e_cc / own(z_c)).astype(BF16), own(v_c), preferred_element_type=F32
    ).reshape(NCONT * BLOCK, VDIM)
    total = jnp.concatenate([m_p + jnp.log(z_p), m_c + jnp.log(z_c)], axis=0)
    return jnp.concatenate([o_p, o_c], axis=0), total


def attend_back(query, key, value, mixed, total, grad_mixed):
    delta = jnp.sum(grad_mixed.astype(F32) * mixed, axis=-1, keepdims=True)
    own = lambda a: a.reshape(NCONT, BLOCK, a.shape[-1])
    flat = lambda a: a.reshape(NCONT * BLOCK, a.shape[-1])
    q_p, q_c = query[:PROMPT], query[PROMPT:]
    k_p, k_c = key[:PROMPT], key[PROMPT:]
    v_p, v_c = value[:PROMPT], value[PROMPT:]
    g_p, g_c = grad_mixed[:PROMPT], grad_mixed[PROMPT:]
    t_p, t_c = total[:PROMPT], total[PROMPT:]
    d_p, d_c = delta[:PROMPT], delta[PROMPT:]

    def part(q, k, v, g, t, d, mask):
        batch = "c" if q.ndim == 3 else ""
        prob = jnp.exp(
            jnp.einsum(f"{batch}qd,{batch}kd->{batch}qk", q, k, preferred_element_type=F32) * SCALE
            - t
        )
        if mask is not None:
            prob = jnp.where(mask, prob, 0.0)
        grad_p = jnp.einsum(f"{batch}qd,{batch}kd->{batch}qk", g, v, preferred_element_type=F32)
        grad_s = (prob * (grad_p - d)).astype(BF16)
        back = f"{batch}qk,{batch}qd->{batch}kd"
        grad_v = jnp.einsum(back, prob.astype(BF16), g, preferred_element_type=F32)
        grad_k = jnp.einsum(back, grad_s, q, preferred_element_type=F32) * SCALE
        grad_q = (
            jnp.einsum(f"{batch}qk,{batch}kd->{batch}qd", grad_s, k, preferred_element_type=F32)
            * SCALE
        )
        return grad_q, grad_k, grad_v

    gq_p, gk_p, gv_p = part(q_p, k_p, v_p, g_p, t_p, d_p, causal(PROMPT))
    gq_1, gk_1, gv_1 = part(q_c, k_p, v_p, g_c, t_c, d_c, None)
    gq_2, gk_2, gv_2 = part(
        own(q_c), own(k_c), own(v_c), own(g_c), own(t_c), own(d_c), causal(BLOCK)[None]
    )
    join = lambda a, b: jnp.concatenate([a, b], axis=0)
    return (
        join(gq_p, gq_1 + flat(gq_2)),
        join(gk_p + gk_1, flat(gk_2)),
        join(gv_p + gv_1, flat(gv_2)),
    )


def places_of(hit):
    grid = hit.reshape(-1, 128)
    rows = grid.shape[0]
    upper = (
        lax.broadcasted_iota(jnp.int32, (128, 128), 0)
        < lax.broadcasted_iota(jnp.int32, (128, 128), 1)
    ).astype(BF16)
    lower = (
        lax.broadcasted_iota(jnp.int32, (rows, rows), 1)
        < lax.broadcasted_iota(jnp.int32, (rows, rows), 0)
    ).astype(BF16)
    inside = matmul(grid.astype(BF16), upper)
    sums = jnp.sum(grid, axis=1, keepdims=True).astype(BF16)
    ahead = matmul(lower, sums)
    return (inside + ahead).astype(jnp.int32).reshape(-1)


def per_device(
    sizes,
    tokens,
    cotangent,
    gain_attn,
    w_query,
    w_latent,
    gain_latent,
    w_keyval,
    w_output,
    gain_ffn,
    w_shared_gate,
    w_shared_up,
    w_shared_down,
    w_router,
    expert_gate,
    expert_up,
    expert_down,
    segments,
    positions,
    routes,
):
    n_group, n_expert, n_shard = sizes
    n_row = n_expert * n_shard
    n_all = n_group * n_row
    tok_rows, width = tokens.shape
    row_tokens = segments.shape[0]
    n_prompt = row_tokens // GROUP_TOK
    e_per_prompt = n_expert // n_prompt
    group_at = lax.axis_index("group")
    expert_at = lax.axis_index("expert")
    shard_at = lax.axis_index("shard")
    row_at = expert_at * n_shard + shard_at
    prompt_at = expert_at // e_per_prompt
    head_group = expert_at % e_per_prompt

    seg_block = segments[::BLOCK]
    pos_block = positions[::BLOCK]
    prompt_of = seg_block // (NCONT + 1)
    prompt_of = prompt_of - jnp.min(prompt_of)
    cont_of = seg_block % (NCONT + 1)
    piece = jnp.where(cont_of == 0, pos_block // BLOCK, PROMPT // BLOCK - 1 + cont_of)
    slot_of = prompt_of * GROUP_BLOCKS + piece
    block_ids = jnp.arange(n_row, dtype=jnp.int32)
    block_at = jnp.sum(
        jnp.where(slot_of[None, :] == block_ids[:, None], block_ids[None, :], 0), axis=1
    )
    my_blocks = lax.dynamic_slice_in_dim(block_at, prompt_at * GROUP_BLOCKS, GROUP_BLOCKS)
    local_slot = slot_of - prompt_at * GROUP_BLOCKS
    mine = (local_slot >= 0) & (local_slot < GROUP_BLOCKS)
    local_slot = jnp.clip(local_slot, 0, GROUP_BLOCKS - 1)
    own_prompt = jnp.sum(jnp.where(block_ids == row_at, prompt_of, 0))

    def to_pieces(all_rows):
        return take_blocks(all_rows.reshape(n_row, BLOCK, -1), my_blocks).reshape(GROUP_TOK, -1)

    def from_pieces(rows, clear=False):
        picked = take_blocks(rows.reshape(GROUP_BLOCKS, BLOCK, -1), local_slot)
        if clear and n_prompt > 1:
            picked = jnp.where(mine[:, None, None], picked, jnp.zeros_like(picked))
        return picked

    def heads_home(rows):
        got = trade(from_pieces(rows), ROW)
        if n_prompt > 1:
            got = lax.dynamic_slice_in_dim(got, own_prompt * GROUP_BLOCKS, GROUP_BLOCKS)
        return jnp.swapaxes(got, 0, 1).reshape(BLOCK, -1)

    def heads_out(rows):
        split = jnp.swapaxes(rows.reshape(BLOCK, HEADS, -1), 0, 1)
        if n_prompt > 1:
            split = jnp.tile(split, (n_prompt, 1, 1))
            keep = (block_ids // GROUP_BLOCKS) == own_prompt
            split = jnp.where(keep[:, None, None], split, jnp.zeros_like(split))
        return to_pieces(trade(split, ROW))

    def head_columns(weight, per_head):
        cols = lax.dynamic_slice_in_dim(
            weight, head_group * (n_shard * per_head), n_shard * per_head, axis=1
        )
        cols = jnp.swapaxes(cols.reshape(-1, n_shard, per_head), 0, 1)
        return trade(cols, "shard").reshape(-1, per_head)

    def unit_columns(weight):
        units = weight.shape[1] // n_row
        cols = weight.reshape(weight.shape[0], n_shard, n_expert, units)
        cols = lax.dynamic_index_in_dim(cols, expert_at, axis=2, keepdims=False)
        return jnp.swapaxes(cols, 0, 1)

    def gather_rows(weight):
        part = weight.shape[0] // (n_group * n_expert)
        at = (group_at * n_expert + expert_at) * part
        return lax.all_gather(
            lax.dynamic_slice_in_dim(weight, at, part), ("shard", "group", "expert"), tiled=True
        )

    tok_all = lax.all_gather(tokens, ROW, axis=0, tiled=True)
    routes_all = lax.all_gather(routes, ROW, axis=0, tiled=True)
    w_l = lax.all_gather(w_latent, "shard", axis=0, tiled=True)
    w_r = lax.all_gather(w_router, "shard", axis=0, tiled=True)
    wq_h = head_columns(w_query, QDIM)
    wkv_h = head_columns(w_keyval, KVDIM)
    units = w_shared_gate.shape[1] // n_row
    w_gu = trade(
        jnp.concatenate([unit_columns(w_shared_gate), unit_columns(w_shared_up)], axis=-1), "shard"
    ).reshape(width, 2 * units)
    w_sd = lax.dynamic_slice_in_dim(w_shared_down, expert_at * units, units)
    w_o = gather_rows(w_output)
    c_all = lax.all_gather(cotangent, ROW, axis=0, tiled=True)
    w_q = gather_rows(w_query)

    expert_count = w_r.shape[1]
    top_count = routes.shape[1]
    capacity = n_row * (3 * tok_rows * top_count // (2 * expert_count))
    hit = jnp.any(routes_all == row_at, axis=1)
    place = places_of(hit.astype(F32))
    count = jnp.sum(hit.astype(jnp.int32))
    token_of = (
        jnp.zeros((capacity,), jnp.int32)
        .at[jnp.where(hit, place, capacity)]
        .set(jnp.arange(row_tokens, dtype=jnp.int32), mode="drop")
    )
    filled = jnp.arange(capacity, dtype=jnp.int32) < count
    place = jnp.where(hit, place, 0)

    tok_p = to_pieces(tok_all).astype(F32)
    hidden1 = (rms_parts(tok_p)[0] * gain_attn).astype(BF16)
    pos_p = jnp.arange(GROUP_TOK, dtype=jnp.int32)
    pos_p = jnp.where(pos_p < PROMPT, pos_p, PROMPT + pos_p % BLOCK)
    cos_p, sin_p = angles(pos_p, ROPE)
    joint = matmul(hidden1, jnp.concatenate([wq_h, w_l], axis=1))
    query_f, latent_f = joint[:, :QDIM], joint[:, QDIM:]
    query = jnp.concatenate(
        [query_f[:, :NOPE], rotate(query_f[:, NOPE:], cos_p, sin_p)], axis=1
    ).astype(BF16)
    comp = (rms_parts(latent_f[:, :LATENT])[0] * gain_latent).astype(BF16)
    key_rope = rotate(latent_f[:, LATENT:], cos_p, sin_p).astype(BF16)
    keyval = matmul(comp, wkv_h).astype(BF16)
    key = jnp.concatenate([keyval[:, :NOPE], key_rope], axis=1)
    value = keyval[:, NOPE:]
    mixed_h, total_h = attend(query, key, value)
    mixed = heads_home(mixed_h.astype(BF16))

    inputs = tokens.astype(F32)
    grad_out = cotangent.astype(F32)
    normed1, inverse1 = rms_parts(inputs)
    hidden1_own = (normed1 * gain_attn).astype(BF16)
    latent_own = matmul(hidden1_own, w_l)
    normed_c, inverse_c = rms_parts(latent_own[:, :LATENT])
    after = inputs + matmul(mixed, w_o)
    normed2, inverse2 = rms_parts(after)
    hidden2 = (normed2 * gain_ffn).astype(BF16)
    logits = matmul(hidden2, w_r)
    router_prob = jax.nn.softmax(logits, axis=-1)

    h2_all = lax.all_gather(hidden2, ROW, axis=0, tiled=True)
    wide = matmul(h2_all, jnp.concatenate([w_gu, w_r], axis=1))
    s_gate, s_up = wide[:, :units], wide[:, units : 2 * units]
    prob_all = jax.nn.softmax(wide[:, 2 * units :], axis=-1)
    my_col = (jnp.arange(expert_count) == row_at).astype(F32)
    weight_of = jnp.sum(prob_all * my_col[None, :], axis=1) * hit.astype(F32)
    s_act, s_slope = silu_parts(s_gate)
    s_mid = (s_act * s_up).astype(BF16)
    shared = matmul(s_mid, w_sd)
    rows = h2_all[token_of]
    c_rows = c_all[token_of]
    w_rows = jnp.where(filled, weight_of[token_of], 0.0)
    d_out = (w_rows[:, None] * c_rows.astype(F32)).astype(BF16)
    e_gate = matmul(rows, expert_gate[0])
    e_up = matmul(rows, expert_up[0])
    e_act, e_slope = silu_parts(e_gate)
    e_mid = (e_act * e_up).astype(BF16)
    e_out = matmul(e_mid, expert_down[0]).astype(BF16)
    picked = jnp.where(hit[:, None], e_out[place].astype(F32), 0.0)
    out_part = (weight_of[:, None] * picked + shared).astype(BF16)
    d_prob_col = jnp.sum(c_all.astype(F32) * picked, axis=1)
    ffn = lax.psum_scatter(out_part, ROW, scatter_dimension=0, tiled=True)
    output = (after + ffn.astype(F32)).astype(BF16)

    d_mid = matmul_nt(d_out, expert_down[0])
    d_gate = (d_mid * e_up * e_slope).astype(BF16)
    d_up = (d_mid * e_act).astype(BF16)
    d_rows = (matmul_nt(d_gate, expert_gate[0]) + matmul_nt(d_up, expert_up[0])).astype(BF16)
    ds_mid = matmul_nt(c_all, w_sd)
    ds_gate = (ds_mid * s_up * s_slope).astype(BF16)
    ds_up = (ds_mid * s_act).astype(BF16)
    ds_gu = jnp.concatenate([ds_gate, ds_up], axis=1)
    dh_part = jnp.where(hit[:, None], d_rows[place].astype(F32), 0.0) + matmul_nt(ds_gu, w_gu)
    d_h2 = lax.psum_scatter(dh_part.astype(BF16), ROW, scatter_dimension=0, tiled=True)
    d_prob = trade(d_prob_col.reshape(n_row, tok_rows), ROW).T
    route_hot = jnp.any(
        routes[:, :, None] == jnp.arange(expert_count, dtype=jnp.int32)[None, None, :], axis=1
    )
    d_prob = jnp.where(route_hot, d_prob, 0.0)
    d_logits = (
        router_prob * (d_prob - jnp.sum(router_prob * d_prob, axis=-1, keepdims=True))
    ).astype(BF16)
    grad_router = matmul_tn(hidden2, d_logits)

    def group_sum(left, right):
        whole = matmul_tn(left, right)
        half = whole.shape[0] // n_group
        if n_group != 2:
            return lax.psum_scatter(
                whole.astype(BF16), "group", scatter_dimension=0, tiled=True
            ).astype(F32)[None]
        send = lax.dynamic_slice_in_dim(whole, (1 - group_at) * half, half).astype(BF16)
        keep = lax.dynamic_slice_in_dim(whole, group_at * half, half)
        return (keep + lax.ppermute(send, "group", [(0, 1), (1, 0)]).astype(F32))[None]

    egrad_gate = group_sum(rows, d_gate)
    egrad_up = group_sum(rows, d_up)
    egrad_down = group_sum(e_mid, d_out)

    grad_gu = matmul_tn(h2_all, ds_gu).astype(BF16).reshape(n_all, width // n_all, 2 * units)
    got = trade(grad_gu, ALL).astype(F32)
    got = jnp.sum(got.reshape(n_group, n_expert, n_shard, -1, 2 * units), axis=0)
    got = jnp.transpose(got, (2, 1, 0, 3))
    grad_sg = got[..., :units].reshape(got.shape[0], -1)
    grad_su = got[..., units:].reshape(got.shape[0], -1)
    grad_sd_part = matmul_tn(s_mid, c_all).astype(BF16).reshape(n_group, units // n_group, width)
    grad_sd = 0.0
    for turn in range(n_group):
        piece_at = (group_at + turn) % n_group
        moves = []
        for g in range(n_group):
            for e in range(n_expert):
                for s in range(n_shard):
                    target = (s * n_expert + e) * n_group + (g + turn) % n_group
                    moves.append(((g * n_expert + e) * n_shard + s, target))
        sent = lax.dynamic_index_in_dim(grad_sd_part, piece_at, axis=0, keepdims=False)
        grad_sd = grad_sd + lax.ppermute(sent, ALL, moves).astype(F32)

    d_hidden2 = d_h2.astype(F32) + matmul_nt(d_logits, w_r)
    d_after, grad_gain_ffn = norm_back(d_hidden2, normed2, inverse2, gain_ffn)
    grad_after = grad_out + d_after
    grad_attn = grad_after.astype(BF16)
    d_mixed = matmul_nt(grad_attn, w_o).astype(BF16)
    d_mixed_h = heads_out(d_mixed)
    grad_wo = lax.psum_scatter(
        matmul_tn(mixed, grad_attn).astype(BF16), ALL, scatter_dimension=0, tiled=True
    ).astype(F32)

    d_query, d_key, d_value = attend_back(query, key, value, mixed_h, total_h, d_mixed_h)
    d_query = jnp.concatenate(
        [d_query[:, :NOPE], unrotate(d_query[:, NOPE:], cos_p, sin_p)], axis=1
    ).astype(BF16)
    d_keyval = jnp.concatenate([d_key[:, :NOPE], d_value], axis=1).astype(BF16)
    d_comp = matmul_nt(d_keyval, wkv_h)
    d_latent_part = jnp.concatenate([d_comp, d_key[:, NOPE:]], axis=1).astype(BF16)
    d_lat = lax.psum_scatter(
        from_pieces(d_latent_part, clear=True).reshape(row_tokens, LATENT + ROPE),
        ROW,
        scatter_dimension=0,
        tiled=True,
    ).astype(F32)
    d_query_own = heads_home(d_query)

    grad_wq_h = matmul_tn(hidden1, d_query).astype(BF16).reshape(n_all, width // n_all, QDIM)
    grad_wkv_h = matmul_tn(comp, d_keyval).astype(BF16)
    grad_wkv_h = grad_wkv_h.reshape(n_all, width // n_all, -1)
    got = trade(jnp.concatenate([grad_wq_h, grad_wkv_h], axis=-1), ALL).astype(F32)
    got = jnp.sum(got.reshape(n_group * n_prompt, HEADS, got.shape[1], got.shape[2]), axis=0)
    grad_wq = jnp.swapaxes(got[..., :QDIM], 0, 1).reshape(got.shape[1], -1)
    grad_wkv = jnp.swapaxes(
        got[..., QDIM:].reshape(HEADS, LATENT // n_all, KVDIM), 0, 1
    ).reshape(LATENT // n_all, -1)

    own_pos = lax.dynamic_slice_in_dim(positions, row_at * tok_rows, tok_rows)
    cosine, sine = angles(own_pos, ROPE)
    d_lat_c, grad_gain_latent = norm_back(d_lat[:, :LATENT], normed_c, inverse_c, gain_latent)
    d_latent = jnp.concatenate([d_lat_c, unrotate(d_lat[:, LATENT:], cosine, sine)], axis=1).astype(
        BF16
    )
    d_hidden1 = matmul_nt(d_query_own, w_q) + matmul_nt(d_latent, w_l)
    d_tok, grad_gain_attn = norm_back(d_hidden1, normed1, inverse1, gain_attn)
    grad_tokens = grad_after + d_tok
    grad_wl = lax.psum_scatter(
        matmul_tn(hidden1_own, d_latent).astype(BF16), ALL, scatter_dimension=0, tiled=True
    ).astype(F32)

    small = jnp.concatenate(
        [
            grad_router.reshape(n_all, -1),
            grad_gain_attn.reshape(n_all, -1),
            grad_gain_ffn.reshape(n_all, -1),
            grad_gain_latent.reshape(n_all, -1),
        ],
        axis=1,
    ).reshape(-1)
    small = lax.psum_scatter(small, ALL, scatter_dimension=0, tiled=True)
    own = width // n_all
    at = own * expert_count
    return (
        output,
        grad_tokens,
        small[at : at + own],
        grad_wq,
        grad_wl,
        small[at + 2 * own :],
        grad_wkv,
        grad_wo,
        small[at + own : at + 2 * own],
        grad_sg,
        grad_su,
        grad_sd,
        small[:at].reshape(own, expert_count),
        egrad_gate,
        egrad_up,
        egrad_down,
    )


def solution(mesh):
    sizes = tuple(mesh.shape[name] for name in ALL)
    return jax.shard_map(
        functools.partial(per_device, sizes),
        mesh=mesh,
        in_specs=(
            P(ALL, None),
            P(ALL, None),
            P(),
            P("shard", None),
            P("shard", None),
            P(),
            P("shard", None),
            P("shard", None),
            P(),
            P("shard", None),
            P("shard", None),
            P("shard", None),
            P("shard", None),
            P(ROW, None, None),
            P(ROW, None, None),
            P(ROW, None, None),
            P("group"),
            P("group"),
            P(ALL, None),
        ),
        out_specs=(
            P(ALL, None),
            P(ALL, None),
            P(ALL),
            P(ALL, None),
            P(ALL, None),
            P(ALL),
            P(ALL, None),
            P(ALL, None),
            P(ALL),
            P(ALL, None),
            P(ALL, None),
            P(ALL, None),
            P(ALL, None),
            P(ROW, "group", None),
            P(ROW, "group", None),
            P(ROW, "group", None),
        ),
        check_vma=False,
    )
```

```python
import functools
import math

import jax
import jax.numpy as jnp
from jax import lax
from jax.experimental import pallas as pl
from jax.experimental.pallas import tpu as pltpu
from jax.sharding import PartitionSpec as P

HEADS = 16
NOPE = 128
ROPE = 64
VDIM = 128
LATENT = 512
BLOCK = 256
PROMPT = 2048
NCONT = 8
QDIM = NOPE + ROPE
KVDIM = NOPE + VDIM
GROUP_BLOCKS = PROMPT // BLOCK + NCONT
GROUP_TOK = GROUP_BLOCKS * BLOCK

EPS = 1e-06
ALL = ("group", "expert", "shard")
ROW = ("expert", "shard")
SCALE = 1.0 / math.sqrt(NOPE + ROPE)
F32 = jnp.float32
BF16 = jnp.bfloat16


def matmul(left, right):
    return jnp.dot(left, right, preferred_element_type=F32)


def matmul_nt(left, right):
    return lax.dot_general(left, right, (((1,), (1,)), ((), ())), preferred_element_type=F32)


def matmul_tn(left, right):
    return lax.dot_general(left, right, (((0,), (0,)), ((), ())), preferred_element_type=F32)


def rms_parts(values):
    inverse = lax.rsqrt(jnp.mean(values * values, axis=-1, keepdims=True) + EPS)
    return (values * inverse, inverse)


def norm_back(grad_in, normed, inverse, gain):
    scaled = grad_in * gain
    gain_grad = jnp.sum(grad_in * normed, axis=0)
    input_grad = inverse * (scaled - normed * jnp.mean(scaled * normed, axis=-1, keepdims=True))
    return (input_grad, gain_grad)


def angles(pos_list, rot_width):
    half_width = rot_width // 2
    freq = 10000.0 ** (-2.0 * jnp.arange(half_width, dtype=F32) / rot_width)
    theta = pos_list.astype(F32)[:, None] * freq[None, :]
    return (jnp.cos(theta), jnp.sin(theta))


def rotate(values, cosine, sine):
    half_width = values.shape[-1] // 2
    first_half = values[..., :half_width]
    second_half = values[..., half_width:]
    return jnp.concatenate(
        [first_half * cosine - second_half * sine, second_half * cosine + first_half * sine],
        axis=-1,
    )


def unrotate(grad_in, cosine, sine):
    return rotate(grad_in, cosine, -sine)


def silu_parts(values):
    sigmoid = jax.nn.sigmoid(values)
    return (values * sigmoid, sigmoid * (1.0 + values * (1.0 - sigmoid)))


def trade(buffer, axes):
    return lax.all_to_all(buffer, axes, split_axis=0, concat_axis=0, tiled=True)


TILE = 2 * BLOCK
TILES = GROUP_TOK // TILE
PROMPT_TILES = PROMPT // TILE
NEG = -1e30


def dot(left, right, left_dim, right_dim):
    return lax.dot_general(
        left, right, (((left_dim,), (right_dim,)), ((), ())), preferred_element_type=F32
    )


def take_blocks(blocks, index):
    count = index.shape[0]
    shape = blocks.shape[1:]
    unroll = 8 if shape[-1] <= 256 else 4

    def body(index_ref, *refs):
        for i in range(unroll):
            refs[-1][i] = refs[i][0]

    return pl.pallas_call(
        body,
        grid_spec=pltpu.PrefetchScalarGridSpec(
            num_scalar_prefetch=1,
            grid=(count // unroll,),
            in_specs=[
                pl.BlockSpec((1,) + shape, lambda i, at, k=k: (at[i * unroll + k], 0, 0))
                for k in range(unroll)
            ],
            out_specs=pl.BlockSpec((unroll,) + shape, lambda i, at: (i, 0, 0)),
        ),
        out_shape=jax.ShapeDtypeStruct((count,) + shape, blocks.dtype),
        compiler_params=pltpu.CompilerParams(vmem_limit_bytes=40 << 20),
        cost_estimate=pl.CostEstimate(
            flops=0, bytes_accessed=4 * count * shape[0] * shape[1], transcendentals=0
        ),
        name="take_blocks",
    )(index, *([blocks] * unroll))


def project_body(
    at_ref, tok_a, tok_b, gain_ref, w_ref, gain_l_ref, wkv_ref, cos_ref, sin_ref,
    hid_ref, q_ref, k_ref, v_ref, comp_ref,
):
    gain = gain_ref[...]
    gain_l = gain_l_ref[...]
    for part, tok in enumerate((tok_a, tok_b)):
        rows = slice(part * BLOCK, (part + 1) * BLOCK)
        hidden = (rms_parts(tok[0].astype(F32))[0] * gain).astype(BF16)
        hid_ref[rows, :] = hidden
        joint = dot(hidden, w_ref[...], 1, 0)
        cosine, sine = cos_ref[rows, :], sin_ref[rows, :]
        at = NOPE + LATENT
        q_ref[rows, :NOPE] = joint[:, :NOPE].astype(BF16)
        q_ref[rows, NOPE:] = rotate(joint[:, at : at + ROPE], cosine, sine).astype(BF16)
        comp = (rms_parts(joint[:, NOPE:at])[0] * gain_l).astype(BF16)
        comp_ref[rows, :] = comp
        keyval = dot(comp, wkv_ref[...], 1, 0).astype(BF16)
        k_ref[rows, :NOPE] = keyval[:, :NOPE]
        k_ref[rows, NOPE:] = rotate(joint[:, at + ROPE :], cosine, sine).astype(BF16)
        v_ref[rows, :] = keyval[:, NOPE:]


def project(blocks, index, gain, weights, gain_l, wkv, cosine, sine):
    width = blocks.shape[-1]
    whole = lambda a: pl.BlockSpec(a.shape, lambda i, at: (0, 0))
    tiled = lambda cols: pl.BlockSpec((TILE, cols), lambda i, at: (i, 0))
    piece = lambda k: pl.BlockSpec((1, BLOCK, width), lambda i, at: (at[2 * i + k], 0, 0))
    widths = (width, QDIM, QDIM, VDIM, LATENT)
    gain, gain_l = gain.reshape(1, -1), gain_l.reshape(1, -1)
    return pl.pallas_call(
        project_body,
        grid_spec=pltpu.PrefetchScalarGridSpec(
            num_scalar_prefetch=1,
            grid=(TILES,),
            in_specs=[
                piece(0), piece(1), whole(gain), whole(weights), whole(gain_l), whole(wkv),
                tiled(ROPE // 2), tiled(ROPE // 2),
            ],
            out_specs=[tiled(cols) for cols in widths],
        ),
        out_shape=[jax.ShapeDtypeStruct((GROUP_TOK, cols), BF16) for cols in widths],
        compiler_params=pltpu.CompilerParams(vmem_limit_bytes=48 << 20),
        cost_estimate=pl.CostEstimate(
            flops=14_000_000_000, bytes_accessed=48_000_000, transcendentals=0
        ),
        name="project",
    )(index, blocks, blocks, gain, weights, gain_l, wkv, cosine, sine)


def own_mask(tile):
    k_at = lax.broadcasted_iota(jnp.int32, (TILE, TILE), 0)
    q_at = lax.broadcasted_iota(jnp.int32, (TILE, TILE), 1)
    piece = jnp.where(tile < PROMPT_TILES, TILE, BLOCK)
    lowest = jnp.where(q_at >= piece, piece, 0)
    return (k_at <= q_at) & (k_at >= lowest)


def attend_body(q_ref, k_ref, v_ref, o_ref, ob_ref, lse_ref, s_ref):
    tile = pl.program_id(0)
    q = q_ref[...]
    others = jnp.minimum(tile, PROMPT_TILES)

    def rows_of(at):
        return pl.ds(pl.multiple_of(at * TILE, TILE), TILE)

    def fold(values, op):
        return op(values.reshape(TILE // 8, 8, TILE), axis=0)

    own = jnp.where(own_mask(tile), dot(k_ref[rows_of(tile), :], q, 1, 1) * SCALE, NEG)
    s_ref[rows_of(PROMPT_TILES), :] = own

    def raw(at, top):
        s = dot(k_ref[rows_of(at), :], q, 1, 1) * SCALE
        s_ref[rows_of(at), :] = s
        return jnp.maximum(top, fold(s, jnp.max))

    top = lax.fori_loop(0, others, raw, fold(own, jnp.max))
    top = jnp.max(top, axis=0, keepdims=True)

    def mix(s_at, v_at, carry):
        total, out = carry
        p = jnp.exp(s_ref[rows_of(s_at), :] - top)
        return total + fold(p, jnp.sum), out + dot(p.astype(BF16), v_ref[rows_of(v_at), :], 0, 0)

    carry = (jnp.zeros((8, TILE), F32), jnp.zeros((TILE, VDIM), F32))
    carry = mix(PROMPT_TILES, tile, carry)
    total, out = lax.fori_loop(0, others, lambda at, c: mix(at, at, c), carry)
    total = jnp.sum(total, axis=0, keepdims=True)
    lse_ref[...] = top + jnp.log(total)
    scale = jnp.transpose(jnp.broadcast_to(1.0 / total, (VDIM, TILE)))
    out = out * scale
    o_ref[...] = out
    ob_ref[...] = out.astype(BF16)


def attend(query, key, value):
    whole = lambda cols: pl.BlockSpec((GROUP_TOK, cols), lambda i: (0, 0))
    tiled = lambda cols: pl.BlockSpec((TILE, cols), lambda i: (i, 0))
    return pl.pallas_call(
        attend_body,
        grid=(TILES,),
        in_specs=[tiled(QDIM), whole(QDIM), whole(VDIM)],
        out_specs=[tiled(VDIM), tiled(VDIM), pl.BlockSpec((1, TILE), lambda i: (0, i))],
        out_shape=[
            jax.ShapeDtypeStruct((GROUP_TOK, VDIM), F32),
            jax.ShapeDtypeStruct((GROUP_TOK, VDIM), BF16),
            jax.ShapeDtypeStruct((1, GROUP_TOK), F32),
        ],
        scratch_shapes=[pltpu.VMEM((PROMPT + TILE, TILE), F32)],
        compiler_params=pltpu.CompilerParams(vmem_limit_bytes=40 << 20),
        cost_estimate=pl.CostEstimate(
            flops=6_000_000_000, bytes_accessed=10_000_000, transcendentals=8_000_000
        ),
        name="attend",
    )(query, key, value)


def attend_back_body(
    q_ref, k_ref, v_ref, g_ref, o_ref, lse_ref, cos_ref, sin_ref, dq_ref, dk_ref, dv_ref, acc_ref
):
    tile = pl.program_id(0)

    @pl.when(tile == 0)
    def _():
        dk_ref[...] = jnp.zeros_like(dk_ref)
        dv_ref[...] = jnp.zeros_like(dv_ref)

    q = q_ref[...]
    g = g_ref[...]
    lse = lse_ref[...]
    delta = jnp.sum(jnp.transpose(g.astype(F32) * o_ref[...]), axis=0, keepdims=True)

    def step(at, mask):
        rows = pl.ds(pl.multiple_of(at * TILE, TILE), TILE)
        k = k_ref[rows, :]
        p = jnp.exp(dot(k, q, 1, 1) * SCALE - lse)
        if mask is not None:
            p = jnp.where(mask, p, 0.0)
        ds = (p * (dot(v_ref[rows, :], g, 1, 1) - delta)).astype(BF16)
        dv_ref[rows, :] += dot(p.astype(BF16), g, 1, 0)
        dk_ref[rows, :] += dot(ds, q, 1, 0) * SCALE
        return dot(ds, k, 0, 0)

    acc_ref[...] = step(tile, own_mask(tile))

    @pl.loop(0, jnp.minimum(tile, PROMPT_TILES))
    def _(at):
        acc_ref[...] += step(at, None)

    dq = acc_ref[...] * SCALE
    dq_ref[:, :NOPE] = dq[:, :NOPE].astype(BF16)
    dq_ref[:, NOPE:] = rotate(dq[:, NOPE:], cos_ref[...], -sin_ref[...]).astype(BF16)


def attend_back(query, key, value, mixed, lse, grad, cosine, sine):
    whole = lambda cols: pl.BlockSpec((GROUP_TOK, cols), lambda i: (0, 0))
    tiled = lambda cols: pl.BlockSpec((TILE, cols), lambda i: (i, 0))
    return pl.pallas_call(
        attend_back_body,
        grid=(TILES,),
        in_specs=[
            tiled(QDIM), whole(QDIM), whole(VDIM), tiled(VDIM), tiled(VDIM),
            pl.BlockSpec((1, TILE), lambda i: (0, i)), tiled(ROPE // 2), tiled(ROPE // 2),
        ],
        out_specs=[tiled(QDIM), whole(QDIM), whole(VDIM)],
        out_shape=[
            jax.ShapeDtypeStruct((GROUP_TOK, QDIM), BF16),
            jax.ShapeDtypeStruct((GROUP_TOK, QDIM), F32),
            jax.ShapeDtypeStruct((GROUP_TOK, VDIM), F32),
        ],
        scratch_shapes=[pltpu.VMEM((TILE, QDIM), F32)],
        compiler_params=pltpu.CompilerParams(vmem_limit_bytes=48 << 20),
        cost_estimate=pl.CostEstimate(
            flops=16_000_000_000, bytes_accessed=20_000_000, transcendentals=8_000_000
        ),
        name="attend_back",
    )(query, key, value, grad, mixed, lse, cosine, sine)


def latent_back_body(slot_ref, mine_ref, dk_ref, dv_ref, w_ref, dkv_ref, lat_ref):
    kv = jnp.concatenate([dk_ref[:, :NOPE], dv_ref[...]], axis=1).astype(BF16)
    dkv_ref[...] = kv
    keep = mine_ref[pl.program_id(0)] != 0
    comp = jnp.where(keep, dot(kv, w_ref[...], 1, 1), 0.0)
    lat_ref[:, :LATENT] = comp.astype(BF16)
    lat_ref[:, LATENT:] = jnp.where(keep, dk_ref[:, NOPE:], 0.0).astype(BF16)


def latent_back(d_key, d_value, wkv, slot, mine):
    count = slot.shape[0]
    tiled = lambda cols: pl.BlockSpec((BLOCK, cols), lambda i, at, m: (at[i], 0))
    return pl.pallas_call(
        latent_back_body,
        grid_spec=pltpu.PrefetchScalarGridSpec(
            num_scalar_prefetch=2,
            grid=(count,),
            in_specs=[
                tiled(QDIM), tiled(VDIM), pl.BlockSpec(wkv.shape, lambda i, at, m: (0, 0)),
            ],
            out_specs=[
                tiled(KVDIM), pl.BlockSpec((BLOCK, LATENT + ROPE), lambda i, at, m: (i, 0)),
            ],
        ),
        out_shape=[
            jax.ShapeDtypeStruct((GROUP_TOK, KVDIM), BF16),
            jax.ShapeDtypeStruct((count * BLOCK, LATENT + ROPE), BF16),
        ],
        cost_estimate=pl.CostEstimate(
            flops=1_100_000_000, bytes_accessed=14_000_000, transcendentals=0
        ),
        name="latent_back",
    )(slot, mine.astype(jnp.int32), d_key, d_value, wkv)

def line_gather(part, axis, count):
    up = [(i, i + 1) for i in range(count - 1)]
    down = [(i + 1, i) for i in range(count - 1)]
    right, left = [part], [part]
    for _ in range(count - 1):
        right.append(lax.ppermute(right[-1], axis, up))
        left.append(lax.ppermute(left[-1], axis, down))
    line = jnp.stack(right[:0:-1] + left)
    return lax.dynamic_slice_in_dim(line, count - 1 - lax.axis_index(axis), count)


def pair_gather(part, axis, count, flip, bit):
    other = lax.ppermute(part, axis, [(i, i ^ flip) for i in range(count)])
    return lax.dynamic_slice_in_dim(jnp.stack([part, other, part]), bit, 2)


def chunks_of(total, size):
    return [slice(at, min(at + size, total)) for at in range(0, total, size)]


def experts_body(
    groups, units, count, me_ref, place_ref, h_ref, c_ref, wg_ref, wu_ref, wd_ref, ws_ref, wsd_ref,
    outa_ref, outb_ref, dh_ref, dprob_ref, rows_ref, dout_ref, mid_ref, dg_ref, du_ref, smid_ref, ds_ref,
    crow_ref,
):
    width, hidden = wg_ref.shape
    padded = wsd_ref.shape[0]
    h, c = h_ref[...], c_ref[...]

    wide = dot(h, ws_ref[...], 1, 0)
    s_gate, s_up = wide[:, :padded], wide[:, padded:]
    first = units - (padded - 128)
    logits = jnp.transpose(s_gate[:, padded - 128 :])[first : first + count, :]
    powers = jnp.exp(logits - jnp.max(logits, axis=0, keepdims=True))
    mine = lax.broadcasted_iota(jnp.int32, powers.shape, 0) == me_ref[0]
    weight = jnp.sum(jnp.where(mine, powers, 0.0), axis=0, keepdims=True) / jnp.sum(
        powers, axis=0, keepdims=True
    )
    s_act, s_slope = silu_parts(s_gate)
    smid_ref[...] = (s_act * s_up).astype(BF16)
    ds_mid = dot(c, wsd_ref[...], 1, 1)
    ds_ref[:, :padded] = (ds_mid * s_up * s_slope).astype(BF16)
    ds_ref[:, padded:] = (ds_mid * s_act).astype(BF16)

    picks, weights = [], []
    for rows, toks in groups:
        shape = (rows.stop - rows.start, toks.stop - toks.start)
        here = lax.broadcasted_iota(jnp.int32, shape, 0) + rows.start == place_ref[0, :, toks]
        pick = jnp.where(here, 1.0, 0.0).astype(BF16)
        scale = jnp.sum(jnp.where(here, weight[:, toks], 0.0), axis=1, keepdims=True)
        for cols in chunks_of(width, 512):
            rows_ref[rows, cols] = dot(pick, h[toks, cols], 1, 0).astype(BF16)
            c_rows = dot(pick, c[toks, cols], 1, 0)
            crow_ref[rows, cols] = c_rows.astype(BF16)
            dout_ref[rows, cols] = (scale * c_rows).astype(BF16)
        picks.append((rows, toks, here, pick))
        weights.append(scale)
    scale = jnp.concatenate(weights, axis=0) if len(weights) > 1 else weights[0]

    for cols in chunks_of(hidden, 512):
        gate = dot(rows_ref[...], wg_ref[:, cols], 1, 0)
        up = dot(rows_ref[...], wu_ref[:, cols], 1, 0)
        act, slope = silu_parts(gate)
        mid_ref[:, cols] = (act * up).astype(BF16)
        d_mid = dot(dout_ref[...], wd_ref[cols, :], 1, 1)
        dg_ref[:, cols] = (d_mid * up * slope).astype(BF16)
        du_ref[:, cols] = (d_mid * act).astype(BF16)

    d_prob = jnp.zeros(scale.shape, F32)
    for cols in chunks_of(width, 512):
        out = dot(mid_ref[...], wd_ref[:, cols], 1, 0).astype(BF16).astype(F32)
        d_prob = d_prob + jnp.sum(out * crow_ref[:, cols].astype(F32), axis=1, keepdims=True)
        out = (out * scale).astype(BF16)
        d_rows = dot(dg_ref[...], wg_ref[cols, :], 1, 1) + dot(du_ref[...], wu_ref[cols, :], 1, 1)
        d_rows = d_rows.astype(BF16)
        for rows, toks, here, pick in picks:
            shared = dot(smid_ref[toks, :], wsd_ref[:, cols], 1, 0)
            half_ref, at = (outa_ref, 0) if cols.start < width // 2 else (outb_ref, width // 2)
            half_ref[toks, cols.start - at : cols.stop - at] = (
                dot(pick, out[rows, :], 0, 0) + shared
            ).astype(BF16)
            shared = dot(ds_ref[toks, :], ws_ref[cols, :], 1, 1)
            dh_ref[toks, cols] = (dot(pick, d_rows[rows, :], 0, 0) + shared).astype(BF16)
    for rows, toks, here, pick in picks:
        dprob_ref[0, :, toks] = jnp.sum(
            jnp.where(here, d_prob[rows, :], 0.0), axis=0, keepdims=True
        )


def experts(
    me, place, capacity, hidden2, cotangent, w_gate, w_up, w_down, w_shared, w_sdown, units, count
):
    tokens, width = hidden2.shape
    hidden = w_gate.shape[1]
    padded = w_sdown.shape[0]
    blocks = 2
    step = blocks * BLOCK
    steps = tokens // step
    room = blocks * capacity
    if capacity % 16 == 0:
        groups = [
            (slice(b * capacity, (b + 1) * capacity), slice(b * BLOCK, (b + 1) * BLOCK))
            for b in range(blocks)
        ]
    else:
        groups = [(slice(0, room), slice(0, step))]
    once = lambda a: pl.BlockSpec(a.shape, lambda i, me: (0, 0), pipeline_mode=pl.Buffered(1))
    tiled = lambda rows, cols: pl.BlockSpec((rows, cols), lambda i, me: (i, 0))
    line = pl.BlockSpec((1, 1, step), lambda i, me: (i, 0, 0))
    shape = lambda rows, cols, kind=BF16: jax.ShapeDtypeStruct((rows, cols), kind)
    flops = 2 * steps * (6 * room * width * hidden + 6 * step * width * padded)
    return pl.pallas_call(
        functools.partial(experts_body, groups, units, count),
        grid_spec=pltpu.PrefetchScalarGridSpec(
            num_scalar_prefetch=1,
            grid=(steps,),
            in_specs=[
                line, tiled(step, width), tiled(step, width),
                once(w_gate), once(w_up), once(w_down), once(w_shared), once(w_sdown),
            ],
            out_specs=[
                tiled(step, width // 2), tiled(step, width // 2), tiled(step, width), line,
                tiled(room, width),
                tiled(room, width), tiled(room, hidden), tiled(room, hidden),
                tiled(room, hidden), tiled(step, padded), tiled(step, 2 * padded),
            ],
            scratch_shapes=[pltpu.VMEM((room, width), BF16)],
        ),
        out_shape=[
            shape(tokens, width // 2), shape(tokens, width // 2), shape(tokens, width),
            jax.ShapeDtypeStruct((steps, 1, step), F32),
            shape(steps * room, width), shape(steps * room, width), shape(steps * room, hidden),
            shape(steps * room, hidden), shape(steps * room, hidden), shape(tokens, padded),
            shape(tokens, 2 * padded),
        ],
        compiler_params=pltpu.CompilerParams(vmem_limit_bytes=62 << 20),
        cost_estimate=pl.CostEstimate(
            flops=flops, bytes_accessed=130_000_000, transcendentals=5_000_000
        ),
        name="experts",
    )(me, place, hidden2, cotangent, w_gate, w_up, w_down, w_shared, w_sdown)

def places_of(hit):
    count = hit.shape[1]
    upper = (
        lax.broadcasted_iota(jnp.int32, (count, count), 0)
        < lax.broadcasted_iota(jnp.int32, (count, count), 1)
    ).astype(BF16)
    return matmul(hit.astype(BF16), upper).astype(jnp.int32)


def per_device(
    sizes,
    tokens,
    cotangent,
    gain_attn,
    w_query,
    w_latent,
    gain_latent,
    w_keyval,
    w_output,
    gain_ffn,
    w_shared_gate,
    w_shared_up,
    w_shared_down,
    w_router,
    expert_gate,
    expert_up,
    expert_down,
    segments,
    positions,
    routes,
):
    n_group, n_expert, n_shard = sizes
    n_row = n_expert * n_shard
    n_all = n_group * n_row
    tok_rows, width = tokens.shape
    row_tokens = segments.shape[0]
    n_prompt = row_tokens // GROUP_TOK
    e_per_prompt = n_expert // n_prompt
    group_at = lax.axis_index("group")
    expert_at = lax.axis_index("expert")
    shard_at = lax.axis_index("shard")
    row_at = expert_at * n_shard + shard_at
    prompt_at = expert_at // e_per_prompt
    head_group = expert_at % e_per_prompt

    seg_block = segments[::BLOCK]
    pos_block = positions[::BLOCK]
    prompt_of = seg_block // (NCONT + 1)
    prompt_of = prompt_of - jnp.min(prompt_of)
    cont_of = seg_block % (NCONT + 1)
    piece = jnp.where(cont_of == 0, pos_block // BLOCK, PROMPT // BLOCK - 1 + cont_of)
    slot_of = prompt_of * GROUP_BLOCKS + piece
    block_ids = jnp.arange(n_row, dtype=jnp.int32)
    block_at = jnp.sum(
        jnp.where(slot_of[None, :] == block_ids[:, None], block_ids[None, :], 0), axis=1
    )
    my_blocks = lax.dynamic_slice_in_dim(block_at, prompt_at * GROUP_BLOCKS, GROUP_BLOCKS)
    local_slot = slot_of - prompt_at * GROUP_BLOCKS
    mine = (local_slot >= 0) & (local_slot < GROUP_BLOCKS)
    local_slot = jnp.clip(local_slot, 0, GROUP_BLOCKS - 1)
    own_prompt = jnp.sum(jnp.where(block_ids == row_at, prompt_of, 0))

    def to_pieces(all_rows):
        return take_blocks(all_rows.reshape(n_row, BLOCK, -1), my_blocks).reshape(GROUP_TOK, -1)

    def from_pieces(rows):
        return take_blocks(rows.reshape(GROUP_BLOCKS, BLOCK, -1), local_slot)

    def heads_home(rows):
        got = trade(from_pieces(rows), ROW)
        if n_prompt > 1:
            got = lax.dynamic_slice_in_dim(got, own_prompt * GROUP_BLOCKS, GROUP_BLOCKS)
        return jnp.swapaxes(got, 0, 1).reshape(BLOCK, -1)

    def heads_out(rows):
        split = jnp.swapaxes(rows.reshape(BLOCK, HEADS, -1), 0, 1)
        if n_prompt > 1:
            split = jnp.tile(split, (n_prompt, 1, 1))
            keep = (block_ids // GROUP_BLOCKS) == own_prompt
            split = jnp.where(keep[:, None, None], split, jnp.zeros_like(split))
        return to_pieces(trade(split, ROW))

    def head_parts(weight, per_head):
        cols = lax.dynamic_slice_in_dim(
            weight, head_group * (n_shard * per_head), n_shard * per_head, axis=1
        )
        return jnp.swapaxes(cols.reshape(-1, n_shard, per_head), 0, 1)

    def head_columns(weight, per_head):
        return trade(head_parts(weight, per_head), "shard").reshape(-1, per_head)

    def unit_columns(weight):
        units = weight.shape[1] // n_row
        cols = weight.reshape(weight.shape[0], n_shard, n_expert, units)
        cols = lax.dynamic_index_in_dim(cols, expert_at, axis=2, keepdims=False)
        return jnp.swapaxes(cols, 0, 1)

    paired = (n_group, n_expert) == (2, 4)
    x_at, core_at = expert_at // 2, expert_at % 2

    def sub_rows(weight):
        part = weight.shape[0] // (n_group * n_expert)
        at = (group_at * n_expert + expert_at) * part
        return lax.dynamic_slice_in_dim(weight, at, part)

    def gather_rows_at_once(weight):
        return lax.all_gather(sub_rows(weight), ("shard", "group", "expert"), tiled=True)

    def spread(part):
        return trade(jnp.broadcast_to(part, (n_shard,) + part.shape), "shard")

    def gather_rows(weight):
        if not paired:
            return gather_rows_at_once(weight)
        got = spread(sub_rows(weight))
        got = pair_gather(got, "expert", 4, 2, x_at)
        got = pair_gather(got, "group", 2, 1, group_at)
        got = pair_gather(got, "expert", 4, 1, core_at)
        return jnp.transpose(got, (3, 1, 2, 0, 4, 5)).reshape(width, -1)

    def scatter_rows(left, right, extra=None, pending=False):
        if not paired:
            whole = matmul_tn(left, right)
            if extra is not None:
                whole = jnp.concatenate([whole, extra], axis=1)
            return lax.psum_scatter(whole.astype(BF16), ALL, scatter_dimension=0, tiled=True).astype(
                F32
            )
        block = left.shape[1] // 8

        def half(core):
            cols = left.reshape(-1, 4, 2, block)
            cols = lax.dynamic_index_in_dim(cols, core, axis=2, keepdims=False)
            out = matmul_tn(cols.reshape(-1, 4 * block), right)
            if extra is not None:
                more = extra.reshape(4, 2, block, -1)
                more = lax.dynamic_index_in_dim(more, core, axis=1, keepdims=False)
                out = jnp.concatenate([out, more.reshape(4 * block, -1)], axis=1)
            return out

        def swap(rows, axis, count, flip):
            return lax.ppermute(
                rows.astype(BF16), axis, [(i, i ^ flip) for i in range(count)]
            ).astype(F32)

        rows = half(core_at) + swap(half(1 - core_at), "expert", 4, 1)
        for axis, count, flip, bit in (("group", 2, 1, group_at), ("expert", 4, 2, x_at)):
            size = rows.shape[0] // 2
            send = lax.dynamic_slice_in_dim(rows, (1 - bit) * size, size)
            keep = lax.dynamic_slice_in_dim(rows, bit * size, size)
            rows = keep + swap(send, axis, count, flip)
        rows = rows.astype(BF16).reshape(n_shard, -1, rows.shape[1])
        return rows if pending else over_shards(rows)

    def over_shards(rows):
        return jnp.sum(trade(rows, "shard").astype(F32), axis=0)

    expert_count = w_router.shape[1]
    top_count = routes.shape[1]
    route_hot = jnp.any(
        routes[:, :, None] == jnp.arange(expert_count, dtype=jnp.int32)[None, None, :], axis=1
    )
    pos_p = jnp.arange(GROUP_TOK, dtype=jnp.int32)
    pos_p = jnp.where(pos_p < PROMPT, pos_p, PROMPT + pos_p % BLOCK)
    cos_p, sin_p = angles(pos_p, ROPE)
    tok_all = lax.all_gather(tokens, ROW, axis=0, tiled=True)
    hit_b = trade(route_hot.T.astype(F32), ROW) > 0.5
    cotangent_late, cos_p, sin_p, hit_b = lax.optimization_barrier(
        (cotangent, cos_p, sin_p, hit_b)
    )
    c_all = lax.all_gather(cotangent_late, ROW, axis=0, tiled=True)
    units = w_shared_gate.shape[1] // n_row
    wq_h = head_columns(w_query, QDIM)
    wkv_h = head_columns(w_keyval, KVDIM)
    w_lr = gather_rows(jnp.concatenate([w_latent, w_router], axis=1))
    w_l, w_r = w_lr[:, : LATENT + ROPE], w_lr[:, LATENT + ROPE :]
    w_joint = jnp.concatenate([wq_h[:, :NOPE], w_l[:, :LATENT], wq_h[:, NOPE:], w_l[:, LATENT:]], 1)
    w_o_near = w_output
    if paired:
        w_o_near = pair_gather(spread(sub_rows(w_output)), "expert", 4, 2, x_at)
    w_joint, wkv_h, tok_all, w_o_near, w_gate_late, w_up_late = lax.optimization_barrier(
        (w_joint, wkv_h, tok_all, w_o_near, w_shared_gate, w_shared_up)
    )
    w_gu = trade(
        jnp.concatenate([unit_columns(w_gate_late), unit_columns(w_up_late)], axis=-1), "shard"
    ).reshape(width, 2 * units)
    if paired:
        w_o_near = pair_gather(w_o_near, "group", 2, 1, group_at)

    capacity = 3 * tok_rows * top_count // (2 * expert_count)
    ahead = capacity * (jnp.arange(n_row, dtype=jnp.int32)[:, None] % 2)
    place = jnp.where(hit_b, places_of(hit_b) + ahead, 1 << 20).reshape(-1, 1, 2 * tok_rows)

    hidden1, query, key, value, comp = project(
        tok_all.reshape(n_row, BLOCK, width),
        my_blocks,
        gain_attn,
        w_joint,
        gain_latent,
        wkv_h,
        cos_p,
        sin_p,
    )
    mixed_f, mixed_h, total_h = attend(query, key, value)
    mixed_h, w_o_near, w_gu = lax.optimization_barrier((mixed_h, w_o_near, w_gu))
    mixed = heads_home(mixed_h)
    if paired:
        w_o = pair_gather(w_o_near, "expert", 4, 1, core_at)
        w_o = jnp.transpose(w_o, (3, 1, 2, 0, 4, 5)).reshape(width, -1)
    else:
        w_o = gather_rows_at_once(w_o_near)
    padded = -(-(units + expert_count) // 128) * 128
    space = lambda cols: jnp.zeros((width, cols), BF16)
    w_sh = jnp.concatenate(
        [
            w_gu[:, :units],
            w_r,
            space(padded - units - expert_count),
            w_gu[:, units:],
            space(padded - units),
        ],
        axis=1,
    )
    w_sd = lax.dynamic_slice_in_dim(w_shared_down, expert_at * units, units)
    w_sd = jnp.pad(w_sd, ((0, padded - units), (0, 0)))

    inputs = tokens.astype(F32)
    grad_out = cotangent.astype(F32)
    normed1, inverse1 = rms_parts(inputs)
    hidden1_own = (normed1 * gain_attn).astype(BF16)
    latent_own = matmul(hidden1_own, w_l)
    normed_c, inverse_c = rms_parts(latent_own[:, :LATENT])
    after = inputs + matmul(mixed, w_o)
    normed2, inverse2 = rms_parts(after)
    hidden2 = (normed2 * gain_ffn).astype(BF16)
    logits = matmul(hidden2, w_r)
    router_prob = jax.nn.softmax(logits, axis=-1)

    hidden2, c_all = lax.optimization_barrier((hidden2, c_all))
    h2_all = lax.all_gather(hidden2, ROW, axis=0, tiled=True)
    h2_all, w_query = lax.optimization_barrier((h2_all, w_query))
    w_q = gather_rows_at_once(w_query)
    out_a, out_b, dh_part, d_prob_col, rows, d_out, e_mid, d_gate, d_up, s_mid, ds_gu = experts(
        row_at[None],
        place,
        capacity,
        h2_all,
        c_all,
        expert_gate[0],
        expert_up[0],
        expert_down[0],
        w_sh,
        w_sd,
        units,
        expert_count,
    )
    dh_part, w_q = lax.optimization_barrier((dh_part, w_q))
    d_h2 = lax.psum_scatter(dh_part, ROW, scatter_dimension=0, tiled=True)
    d_prob = trade(d_prob_col.reshape(n_row, tok_rows), ROW).T
    d_prob = jnp.where(route_hot, d_prob, 0.0)
    d_logits = (
        router_prob * (d_prob - jnp.sum(router_prob * d_prob, axis=-1, keepdims=True))
    ).astype(BF16)
    grad_router = matmul_tn(hidden2, d_logits)

    def share(whole):
        if n_group != 2:
            return lax.psum_scatter(
                whole.astype(BF16), "group", scatter_dimension=0, tiled=True
            ), None
        half = whole.shape[0] // 2
        send = lax.dynamic_slice_in_dim(whole, (1 - group_at) * half, half).astype(BF16)
        keep = lax.dynamic_slice_in_dim(whole, group_at * half, half)
        return lax.ppermute(send, "group", [(0, 1), (1, 0)]), keep

    whole_0 = matmul_tn(rows, d_gate)
    d_up, ds_gu, whole_0 = lax.optimization_barrier((d_up, ds_gu, whole_0))
    got_0, keep_0 = share(whole_0)
    whole_1 = matmul_tn(rows, d_up)
    grad_gu = matmul_tn(h2_all, ds_gu).astype(BF16)
    e_mid, s_mid, whole_1, got_0, grad_gu = lax.optimization_barrier(
        (e_mid, s_mid, whole_1, got_0, grad_gu)
    )
    got_1, keep_1 = share(whole_1)
    whole_2 = matmul_tn(e_mid, d_out)
    grad_sd_part = matmul_tn(s_mid, c_all)[:units].astype(BF16)
    whole_2, got_1, grad_sd_part = lax.optimization_barrier((whole_2, got_1, grad_sd_part))
    got_2, keep_2 = share(whole_2)
    grad_gu = jnp.concatenate(
        [grad_gu[:, :units], grad_gu[:, padded : padded + units]], axis=1
    ).reshape(n_all, width // n_all, 2 * units)
    grad_sd_part = grad_sd_part.reshape(n_group, units // n_group, width)
    d_h2, out_a, out_b, grad_gu, grad_sd_part = lax.optimization_barrier(
        (d_h2, out_a, out_b, grad_gu, grad_sd_part)
    )
    ffn_a = lax.psum_scatter(out_a, ROW, scatter_dimension=0, tiled=True)

    d_hidden2 = d_h2.astype(F32) + matmul_nt(d_logits, w_r)
    d_after, grad_gain_ffn = norm_back(d_hidden2, normed2, inverse2, gain_ffn)
    grad_after = grad_out + d_after
    grad_attn = grad_after.astype(BF16)
    d_mixed = matmul_nt(grad_attn, w_o).astype(BF16)
    d_mixed_h = heads_out(d_mixed)
    d_mixed_h, grad_gu, grad_sd_part = lax.optimization_barrier((d_mixed_h, grad_gu, grad_sd_part))
    gu_got = trade(grad_gu, ALL)
    sd_gots = []
    for turn in range(n_group):
        piece_at = (group_at + turn) % n_group
        moves = []
        for g in range(n_group):
            for e in range(n_expert):
                for s in range(n_shard):
                    target = (s * n_expert + e) * n_group + (g + turn) % n_group
                    moves.append(((g * n_expert + e) * n_shard + s, target))
        sent = lax.dynamic_index_in_dim(grad_sd_part, piece_at, axis=0, keepdims=False)
        sd_gots.append(lax.ppermute(sent, ALL, moves))

    d_query, d_key, d_value = attend_back(
        query, key, value, mixed_f, total_h, d_mixed_h, cos_p, sin_p
    )
    d_keyval, d_latent_part = latent_back(d_key, d_value, wkv_h, local_slot, mine)
    d_latent_part, ffn_a, got_2, gu_got, sd_gots, grad_attn_late = lax.optimization_barrier(
        (d_latent_part, ffn_a, got_2, gu_got, sd_gots, grad_attn)
    )
    d_lat = lax.psum_scatter(d_latent_part, ROW, scatter_dimension=0, tiled=True)
    d_query_own = heads_home(d_query)
    wo_rows = scatter_rows(mixed, grad_attn_late, pending=True)
    egrads = [
        (got.astype(F32) if keep is None else keep + got.astype(F32))[None]
        for got, keep in ((got_0, keep_0), (got_1, keep_1), (got_2, keep_2))
    ]
    d_lat, d_query_own, wo_rows, egrads, out_b, d_query, d_keyval = lax.optimization_barrier(
        (d_lat, d_query_own, wo_rows, egrads, out_b, d_query, d_keyval)
    )
    egrad_gate, egrad_up, egrad_down = egrads
    d_lat = d_lat.astype(F32)
    ffn_b = lax.psum_scatter(out_b, ROW, scatter_dimension=0, tiled=True)
    grad_wo = over_shards(wo_rows) if paired else wo_rows
    output = (after + jnp.concatenate([ffn_a, ffn_b], axis=1).astype(F32)).astype(BF16)
    got = gu_got.astype(F32)
    got = jnp.sum(got.reshape(n_group, n_expert, n_shard, -1, 2 * units), axis=0)
    got = jnp.transpose(got, (2, 1, 0, 3))
    grad_sg = got[..., :units].reshape(got.shape[0], -1)
    grad_su = got[..., units:].reshape(got.shape[0], -1)
    grad_sd = sum(got.astype(F32) for got in sd_gots)

    grad_wq_h = matmul_tn(hidden1, d_query).astype(BF16).reshape(n_all, width // n_all, QDIM)
    grad_wkv_h = matmul_tn(comp, d_keyval).astype(BF16)
    grad_wkv_h = grad_wkv_h.reshape(n_all, width // n_all, -1)
    got = trade(jnp.concatenate([grad_wq_h, grad_wkv_h], axis=-1), ALL).astype(F32)
    got = jnp.sum(got.reshape(n_group * n_prompt, HEADS, got.shape[1], got.shape[2]), axis=0)
    grad_wq = jnp.swapaxes(got[..., :QDIM], 0, 1).reshape(got.shape[1], -1)
    grad_wkv = jnp.swapaxes(
        got[..., QDIM:].reshape(HEADS, LATENT // n_all, KVDIM), 0, 1
    ).reshape(LATENT // n_all, -1)

    own_pos = lax.dynamic_slice_in_dim(positions, row_at * tok_rows, tok_rows)
    cosine, sine = angles(own_pos, ROPE)
    d_lat_c, grad_gain_latent = norm_back(d_lat[:, :LATENT], normed_c, inverse_c, gain_latent)
    d_latent = jnp.concatenate([d_lat_c, unrotate(d_lat[:, LATENT:], cosine, sine)], axis=1).astype(
        BF16
    )
    d_hidden1 = matmul_nt(d_query_own, w_q) + matmul_nt(d_latent, w_l)
    d_tok, grad_gain_attn = norm_back(d_hidden1, normed1, inverse1, gain_attn)
    grad_tokens = grad_after + d_tok
    own = width // n_all
    lat = LATENT // n_all
    gain_l = jnp.pad(grad_gain_latent.reshape(n_all, lat), ((0, 0), (0, own - lat)))
    beside = jnp.concatenate(
        [
            grad_router,
            grad_gain_attn[:, None],
            grad_gain_ffn[:, None],
            gain_l.reshape(width, 1),
        ],
        axis=1,
    )
    beside = jnp.pad(beside, ((0, 0), (0, -(LATENT + ROPE + expert_count + 3) % 128)))
    sums = scatter_rows(hidden1_own, d_latent, beside)
    grad_wl = sums[:, : LATENT + ROPE]
    at = LATENT + ROPE + expert_count
    grad_r, grad_ga, grad_gf, grad_gl = (
        sums[:, LATENT + ROPE : at],
        sums[:, at],
        sums[:, at + 1],
        sums[:lat, at + 2],
    )
    return (
        output,
        grad_tokens,
        grad_ga,
        grad_wq,
        grad_wl,
        grad_gl,
        grad_wkv,
        grad_wo,
        grad_gf,
        grad_sg,
        grad_su,
        grad_sd,
        grad_r,
        egrad_gate,
        egrad_up,
        egrad_down,
    )


def solution(mesh):
    sizes = tuple(mesh.shape[name] for name in ALL)
    return jax.shard_map(
        functools.partial(per_device, sizes),
        mesh=mesh,
        in_specs=(
            P(ALL, None),
            P(ALL, None),
            P(),
            P("shard", None),
            P("shard", None),
            P(),
            P("shard", None),
            P("shard", None),
            P(),
            P("shard", None),
            P("shard", None),
            P("shard", None),
            P("shard", None),
            P(ROW, None, None),
            P(ROW, None, None),
            P(ROW, None, None),
            P("group"),
            P("group"),
            P(ALL, None),
        ),
        out_specs=(
            P(ALL, None),
            P(ALL, None),
            P(ALL),
            P(ALL, None),
            P(ALL, None),
            P(ALL),
            P(ALL, None),
            P(ALL, None),
            P(ALL),
            P(ALL, None),
            P(ALL, None),
            P(ALL, None),
            P(ALL, None),
            P(ROW, "group", None),
            P(ROW, "group", None),
            P(ROW, "group", None),
        ),
        check_vma=False,
    )
```

```python
import functools
import math

import jax
import jax.numpy as jnp
from jax import lax
from jax.experimental import pallas as pl
from jax.experimental.pallas import tpu as pltpu
from jax.sharding import PartitionSpec as P

HEADS = 16
NOPE = 128
ROPE = 64
VDIM = 128
LATENT = 512
BLOCK = 256
PROMPT = 2048
NCONT = 8
QDIM = NOPE + ROPE
KVDIM = NOPE + VDIM
GROUP_BLOCKS = PROMPT // BLOCK + NCONT
GROUP_TOK = GROUP_BLOCKS * BLOCK
SIDE = 512

EPS = 1e-06
ALL = ("group", "expert", "shard")
ROW = ("expert", "shard")
SCALE = 1.0 / math.sqrt(NOPE + ROPE)
F32 = jnp.float32
BF16 = jnp.bfloat16


def matmul(left, right):
    return jnp.dot(left, right, preferred_element_type=F32)


def matmul_nt(left, right):
    return lax.dot_general(left, right, (((1,), (1,)), ((), ())), preferred_element_type=F32)


def matmul_tn(left, right):
    return lax.dot_general(left, right, (((0,), (0,)), ((), ())), preferred_element_type=F32)


def rms_parts(values):
    inverse = lax.rsqrt(jnp.mean(values * values, axis=-1, keepdims=True) + EPS)
    return (values * inverse, inverse)


def norm_back(grad_in, normed, inverse, gain):
    scaled = grad_in * gain
    gain_grad = jnp.sum(grad_in * normed, axis=0)
    input_grad = inverse * (scaled - normed * jnp.mean(scaled * normed, axis=-1, keepdims=True))
    return (input_grad, gain_grad)


def angles(pos_list, rot_width):
    half_width = rot_width // 2
    freq = 10000.0 ** (-2.0 * jnp.arange(half_width, dtype=F32) / rot_width)
    theta = pos_list.astype(F32)[:, None] * freq[None, :]
    return (jnp.cos(theta), jnp.sin(theta))


def rotate(values, cosine, sine):
    half_width = values.shape[-1] // 2
    first_half = values[..., :half_width]
    second_half = values[..., half_width:]
    return jnp.concatenate(
        [first_half * cosine - second_half * sine, second_half * cosine + first_half * sine],
        axis=-1,
    )


def unrotate(grad_in, cosine, sine):
    return rotate(grad_in, cosine, -sine)


def silu_parts(values):
    sigmoid = jax.nn.sigmoid(values)
    return (values * sigmoid, sigmoid * (1.0 + values * (1.0 - sigmoid)))


def trade(buffer, axes):
    return lax.all_to_all(buffer, axes, split_axis=0, concat_axis=0, tiled=True)


TILE = 2 * BLOCK
TILES = GROUP_TOK // TILE
PROMPT_TILES = PROMPT // TILE
NEG = -1e30


def dot(left, right, left_dim, right_dim):
    return lax.dot_general(
        left, right, (((left_dim,), (right_dim,)), ((), ())), preferred_element_type=F32
    )


def take_blocks(blocks, index):
    count = index.shape[0]
    shape = blocks.shape[1:]
    unroll = 8 if shape[-1] <= 256 else 4

    def body(index_ref, *refs):
        for i in range(unroll):
            refs[-1][i] = refs[i][0]

    return pl.pallas_call(
        body,
        grid_spec=pltpu.PrefetchScalarGridSpec(
            num_scalar_prefetch=1,
            grid=(count // unroll,),
            in_specs=[
                pl.BlockSpec((1,) + shape, lambda i, at, k=k: (at[i * unroll + k], 0, 0))
                for k in range(unroll)
            ],
            out_specs=pl.BlockSpec((unroll,) + shape, lambda i, at: (i, 0, 0)),
        ),
        out_shape=jax.ShapeDtypeStruct((count,) + shape, blocks.dtype),
        compiler_params=pltpu.CompilerParams(vmem_limit_bytes=40 << 20),
        cost_estimate=pl.CostEstimate(
            flops=0, bytes_accessed=4 * count * shape[0] * shape[1], transcendentals=0
        ),
        name="take_blocks",
    )(index, *([blocks] * unroll))


def project_body(
    at_ref, tok_a, tok_b, gain_ref, w_ref, gain_l_ref, wkv_ref, cos_ref, sin_ref,
    hid_ref, q_ref, k_ref, v_ref, comp_ref,
):
    gain = gain_ref[...]
    gain_l = gain_l_ref[...]
    for part, tok in enumerate((tok_a, tok_b)):
        rows = slice(part * BLOCK, (part + 1) * BLOCK)
        hidden = (rms_parts(tok[0].astype(F32))[0] * gain).astype(BF16)
        hid_ref[rows, :] = hidden
        joint = dot(hidden, w_ref[...], 1, 0)
        cosine, sine = cos_ref[rows, :], sin_ref[rows, :]
        at = NOPE + LATENT
        q_ref[rows, :NOPE] = joint[:, :NOPE].astype(BF16)
        q_ref[rows, NOPE:] = rotate(joint[:, at : at + ROPE], cosine, sine).astype(BF16)
        comp = (rms_parts(joint[:, NOPE:at])[0] * gain_l).astype(BF16)
        comp_ref[rows, :] = comp
        keyval = dot(comp, wkv_ref[...], 1, 0).astype(BF16)
        k_ref[rows, :NOPE] = keyval[:, :NOPE]
        k_ref[rows, NOPE:] = rotate(joint[:, at + ROPE :], cosine, sine).astype(BF16)
        v_ref[rows, :] = keyval[:, NOPE:]


def project(blocks, index, gain, weights, gain_l, wkv, cosine, sine):
    width = blocks.shape[-1]
    whole = lambda a: pl.BlockSpec(a.shape, lambda i, at: (0, 0))
    tiled = lambda cols: pl.BlockSpec((TILE, cols), lambda i, at: (i, 0))
    piece = lambda k: pl.BlockSpec((1, BLOCK, width), lambda i, at: (at[2 * i + k], 0, 0))
    widths = (width, QDIM, QDIM, VDIM, LATENT)
    gain, gain_l = gain.reshape(1, -1), gain_l.reshape(1, -1)
    return pl.pallas_call(
        project_body,
        grid_spec=pltpu.PrefetchScalarGridSpec(
            num_scalar_prefetch=1,
            grid=(TILES,),
            in_specs=[
                piece(0), piece(1), whole(gain), whole(weights), whole(gain_l), whole(wkv),
                tiled(ROPE // 2), tiled(ROPE // 2),
            ],
            out_specs=[tiled(cols) for cols in widths],
        ),
        out_shape=[jax.ShapeDtypeStruct((GROUP_TOK, cols), BF16) for cols in widths],
        compiler_params=pltpu.CompilerParams(vmem_limit_bytes=48 << 20),
        cost_estimate=pl.CostEstimate(
            flops=14_000_000_000, bytes_accessed=48_000_000, transcendentals=0
        ),
        name="project",
    )(index, blocks, blocks, gain, weights, gain_l, wkv, cosine, sine)


def own_mask(tile):
    k_at = lax.broadcasted_iota(jnp.int32, (TILE, TILE), 0)
    q_at = lax.broadcasted_iota(jnp.int32, (TILE, TILE), 1)
    piece = jnp.where(tile < PROMPT_TILES, TILE, BLOCK)
    lowest = jnp.where(q_at >= piece, piece, 0)
    return (k_at <= q_at) & (k_at >= lowest)


def attend_body(q_ref, k_ref, v_ref, o_ref, ob_ref, lse_ref, s_ref):
    tile = pl.program_id(0)
    q = q_ref[...]
    others = jnp.minimum(tile, PROMPT_TILES)

    def rows_of(at):
        return pl.ds(pl.multiple_of(at * TILE, TILE), TILE)

    def fold(values, op):
        return op(values.reshape(TILE // 8, 8, TILE), axis=0)

    own = jnp.where(own_mask(tile), dot(k_ref[rows_of(tile), :], q, 1, 1) * SCALE, NEG)
    s_ref[rows_of(PROMPT_TILES), :] = own

    def raw(at, top):
        s = dot(k_ref[rows_of(at), :], q, 1, 1) * SCALE
        s_ref[rows_of(at), :] = s
        return jnp.maximum(top, fold(s, jnp.max))

    top = lax.fori_loop(0, others, raw, fold(own, jnp.max))
    top = jnp.max(top, axis=0, keepdims=True)

    def mix(s_at, v_at, carry):
        total, out = carry
        p = jnp.exp(s_ref[rows_of(s_at), :] - top)
        return total + fold(p, jnp.sum), out + dot(p.astype(BF16), v_ref[rows_of(v_at), :], 0, 0)

    carry = (jnp.zeros((8, TILE), F32), jnp.zeros((TILE, VDIM), F32))
    carry = mix(PROMPT_TILES, tile, carry)
    total, out = lax.fori_loop(0, others, lambda at, c: mix(at, at, c), carry)
    total = jnp.sum(total, axis=0, keepdims=True)
    lse_ref[...] = top + jnp.log(total)
    scale = jnp.transpose(jnp.broadcast_to(1.0 / total, (VDIM, TILE)))
    out = out * scale
    o_ref[...] = out
    ob_ref[...] = out.astype(BF16)


def attend(query, key, value):
    whole = lambda cols: pl.BlockSpec((GROUP_TOK, cols), lambda i: (0, 0))
    tiled = lambda cols: pl.BlockSpec((TILE, cols), lambda i: (i, 0))
    return pl.pallas_call(
        attend_body,
        grid=(TILES,),
        in_specs=[tiled(QDIM), whole(QDIM), whole(VDIM)],
        out_specs=[tiled(VDIM), tiled(VDIM), pl.BlockSpec((1, TILE), lambda i: (0, i))],
        out_shape=[
            jax.ShapeDtypeStruct((GROUP_TOK, VDIM), F32),
            jax.ShapeDtypeStruct((GROUP_TOK, VDIM), BF16),
            jax.ShapeDtypeStruct((1, GROUP_TOK), F32),
        ],
        scratch_shapes=[pltpu.VMEM((PROMPT + TILE, TILE), F32)],
        compiler_params=pltpu.CompilerParams(vmem_limit_bytes=40 << 20),
        cost_estimate=pl.CostEstimate(
            flops=6_000_000_000, bytes_accessed=10_000_000, transcendentals=8_000_000
        ),
        name="attend",
    )(query, key, value)


def attend_back_body(
    q_ref, k_ref, v_ref, g_ref, o_ref, lse_ref, cos_ref, sin_ref, dq_ref, dk_ref, dv_ref, acc_ref
):
    tile = pl.program_id(0)

    @pl.when(tile == 0)
    def _():
        dk_ref[...] = jnp.zeros_like(dk_ref)
        dv_ref[...] = jnp.zeros_like(dv_ref)

    q = q_ref[...]
    g = g_ref[...]
    lse = lse_ref[...]
    delta = jnp.sum(jnp.transpose(g.astype(F32) * o_ref[...]), axis=0, keepdims=True)

    def step(at, mask):
        rows = pl.ds(pl.multiple_of(at * TILE, TILE), TILE)
        k = k_ref[rows, :]
        p = jnp.exp(dot(k, q, 1, 1) * SCALE - lse)
        if mask is not None:
            p = jnp.where(mask, p, 0.0)
        ds = (p * (dot(v_ref[rows, :], g, 1, 1) - delta)).astype(BF16)
        dv_ref[rows, :] += dot(p.astype(BF16), g, 1, 0)
        dk_ref[rows, :] += dot(ds, q, 1, 0) * SCALE
        return dot(ds, k, 0, 0)

    acc_ref[...] = step(tile, own_mask(tile))

    @pl.loop(0, jnp.minimum(tile, PROMPT_TILES))
    def _(at):
        acc_ref[...] += step(at, None)

    dq = acc_ref[...] * SCALE
    dq_ref[:, :NOPE] = dq[:, :NOPE].astype(BF16)
    dq_ref[:, NOPE:] = rotate(dq[:, NOPE:], cos_ref[...], -sin_ref[...]).astype(BF16)


def attend_back(query, key, value, mixed, lse, grad, cosine, sine):
    whole = lambda cols: pl.BlockSpec((GROUP_TOK, cols), lambda i: (0, 0))
    tiled = lambda cols: pl.BlockSpec((TILE, cols), lambda i: (i, 0))
    return pl.pallas_call(
        attend_back_body,
        grid=(TILES,),
        in_specs=[
            tiled(QDIM), whole(QDIM), whole(VDIM), tiled(VDIM), tiled(VDIM),
            pl.BlockSpec((1, TILE), lambda i: (0, i)), tiled(ROPE // 2), tiled(ROPE // 2),
        ],
        out_specs=[tiled(QDIM), whole(QDIM), whole(VDIM)],
        out_shape=[
            jax.ShapeDtypeStruct((GROUP_TOK, QDIM), BF16),
            jax.ShapeDtypeStruct((GROUP_TOK, QDIM), F32),
            jax.ShapeDtypeStruct((GROUP_TOK, VDIM), F32),
        ],
        scratch_shapes=[pltpu.VMEM((TILE, QDIM), F32)],
        compiler_params=pltpu.CompilerParams(vmem_limit_bytes=48 << 20),
        cost_estimate=pl.CostEstimate(
            flops=16_000_000_000, bytes_accessed=20_000_000, transcendentals=8_000_000
        ),
        name="attend_back",
    )(query, key, value, grad, mixed, lse, cosine, sine)


def latent_back_body(slot_ref, mine_ref, dk_ref, dv_ref, w_ref, dkv_ref, lat_ref):
    kv = jnp.concatenate([dk_ref[:, :NOPE], dv_ref[...]], axis=1).astype(BF16)
    dkv_ref[...] = kv
    keep = mine_ref[pl.program_id(0)] != 0
    comp = jnp.where(keep, dot(kv, w_ref[...], 1, 1), 0.0)
    lat_ref[:, :LATENT] = comp.astype(BF16)
    lat_ref[:, LATENT:] = jnp.where(keep, dk_ref[:, NOPE:], 0.0).astype(BF16)


def latent_back(d_key, d_value, wkv, slot, mine):
    count = slot.shape[0]
    tiled = lambda cols: pl.BlockSpec((BLOCK, cols), lambda i, at, m: (at[i], 0))
    return pl.pallas_call(
        latent_back_body,
        grid_spec=pltpu.PrefetchScalarGridSpec(
            num_scalar_prefetch=2,
            grid=(count,),
            in_specs=[
                tiled(QDIM), tiled(VDIM), pl.BlockSpec(wkv.shape, lambda i, at, m: (0, 0)),
            ],
            out_specs=[
                tiled(KVDIM), pl.BlockSpec((BLOCK, LATENT + ROPE), lambda i, at, m: (i, 0)),
            ],
        ),
        out_shape=[
            jax.ShapeDtypeStruct((GROUP_TOK, KVDIM), BF16),
            jax.ShapeDtypeStruct((count * BLOCK, LATENT + ROPE), BF16),
        ],
        cost_estimate=pl.CostEstimate(
            flops=1_100_000_000, bytes_accessed=14_000_000, transcendentals=0
        ),
        name="latent_back",
    )(slot, mine.astype(jnp.int32), d_key, d_value, wkv)

def line_gather(part, axis, count):
    up = [(i, i + 1) for i in range(count - 1)]
    down = [(i + 1, i) for i in range(count - 1)]
    right, left = [part], [part]
    for _ in range(count - 1):
        right.append(lax.ppermute(right[-1], axis, up))
        left.append(lax.ppermute(left[-1], axis, down))
    line = jnp.stack(right[:0:-1] + left)
    return lax.dynamic_slice_in_dim(line, count - 1 - lax.axis_index(axis), count)


def pair_gather(part, axis, count, flip, bit):
    other = lax.ppermute(part, axis, [(i, i ^ flip) for i in range(count)])
    return lax.dynamic_slice_in_dim(jnp.stack([part, other, part]), bit, 2)


def chunks_of(total, size):
    return [slice(at, min(at + size, total)) for at in range(0, total, size)]


def experts_body(
    groups, units, count, n_parts, me_ref, place_ref, h_ref, c_ref, wg_ref, wu_ref, wd_ref, ws_ref,
    wsd_ref, outa_ref, outb_ref, *refs,
):
    dh_refs = refs[:n_parts]
    dprob_ref, rows_ref, dout_ref, mid_ref, dg_ref, du_ref, smid_ref, ds_ref, crow_ref = refs[
        n_parts:
    ]
    width, hidden = wg_ref.shape
    padded = wsd_ref.shape[0]
    h, c = h_ref[...], c_ref[...]
    ends = [0]
    for ref in dh_refs:
        ends.append(ends[-1] + ref.shape[1])

    wide = dot(h, ws_ref[...], 1, 0)
    s_gate, s_up = wide[:, :padded], wide[:, padded:]
    first = units - (padded - 128)
    logits = jnp.transpose(s_gate[:, padded - 128 :])[first : first + count, :]
    powers = jnp.exp(logits - jnp.max(logits, axis=0, keepdims=True))
    mine = lax.broadcasted_iota(jnp.int32, powers.shape, 0) == me_ref[0]
    weight = jnp.sum(jnp.where(mine, powers, 0.0), axis=0, keepdims=True) / jnp.sum(
        powers, axis=0, keepdims=True
    )
    s_act, s_slope = silu_parts(s_gate)
    smid_ref[...] = (s_act * s_up).astype(BF16)
    ds_mid = dot(c, wsd_ref[...], 1, 1)
    ds_ref[:, :padded] = (ds_mid * s_up * s_slope).astype(BF16)
    ds_ref[:, padded:] = (ds_mid * s_act).astype(BF16)

    picks, weights = [], []
    for rows, toks in groups:
        shape = (rows.stop - rows.start, toks.stop - toks.start)
        here = lax.broadcasted_iota(jnp.int32, shape, 0) + rows.start == place_ref[0, :, toks]
        pick = jnp.where(here, 1.0, 0.0).astype(BF16)
        scale = jnp.sum(jnp.where(here, weight[:, toks], 0.0), axis=1, keepdims=True)
        for cols in chunks_of(width, 512):
            rows_ref[rows, cols] = dot(pick, h[toks, cols], 1, 0).astype(BF16)
            c_rows = dot(pick, c[toks, cols], 1, 0)
            crow_ref[rows, cols] = c_rows.astype(BF16)
            dout_ref[rows, cols] = (scale * c_rows).astype(BF16)
        picks.append((rows, toks, here, pick))
        weights.append(scale)
    scale = jnp.concatenate(weights, axis=0) if len(weights) > 1 else weights[0]

    for cols in chunks_of(hidden, 512):
        gate = dot(rows_ref[...], wg_ref[:, cols], 1, 0)
        up = dot(rows_ref[...], wu_ref[:, cols], 1, 0)
        act, slope = silu_parts(gate)
        mid_ref[:, cols] = (act * up).astype(BF16)
        d_mid = dot(dout_ref[...], wd_ref[cols, :], 1, 1)
        dg_ref[:, cols] = (d_mid * up * slope).astype(BF16)
        du_ref[:, cols] = (d_mid * act).astype(BF16)

    d_prob = jnp.zeros(scale.shape, F32)
    for cols in chunks_of(width, 512):
        out = dot(mid_ref[...], wd_ref[:, cols], 1, 0).astype(BF16).astype(F32)
        d_prob = d_prob + jnp.sum(out * crow_ref[:, cols].astype(F32), axis=1, keepdims=True)
        out = (out * scale).astype(BF16)
        d_rows = dot(dg_ref[...], wg_ref[cols, :], 1, 1) + dot(du_ref[...], wu_ref[cols, :], 1, 1)
        d_rows = d_rows.astype(BF16)
        for rows, toks, here, pick in picks:
            shared = dot(smid_ref[toks, :], wsd_ref[:, cols], 1, 0)
            half_ref, at = (outa_ref, 0) if cols.start < width // 2 else (outb_ref, width // 2)
            half_ref[toks, cols.start - at : cols.stop - at] = (
                dot(pick, out[rows, :], 0, 0) + shared
            ).astype(BF16)
            shared = dot(ds_ref[toks, :], ws_ref[cols, :], 1, 1)
            for ref, start, stop in zip(dh_refs, ends, ends[1:]):
                if start <= cols.start < stop:
                    ref[toks, cols.start - start : cols.stop - start] = (
                        dot(pick, d_rows[rows, :], 0, 0) + shared
                    ).astype(BF16)
    for rows, toks, here, pick in picks:
        dprob_ref[0, :, toks] = jnp.sum(
            jnp.where(here, d_prob[rows, :], 0.0), axis=0, keepdims=True
        )


def experts(
    me, place, capacity, hidden2, cotangent, w_gate, w_up, w_down, w_shared, w_sdown, units, count,
    widths,
):
    width, hidden = w_gate.shape
    tokens = cotangent.shape[0]
    n_parts = len(widths)
    padded = w_sdown.shape[0]
    blocks = 2
    step = blocks * BLOCK
    steps = tokens // step
    room = blocks * capacity
    if capacity % 16 == 0:
        groups = [
            (slice(b * capacity, (b + 1) * capacity), slice(b * BLOCK, (b + 1) * BLOCK))
            for b in range(blocks)
        ]
    else:
        groups = [(slice(0, room), slice(0, step))]
    once = lambda a: pl.BlockSpec(a.shape, lambda i, me: (0, 0), pipeline_mode=pl.Buffered(1))
    tiled = lambda rows, cols: pl.BlockSpec((rows, cols), lambda i, me: (i, 0))
    line = pl.BlockSpec((1, 1, step), lambda i, me: (i, 0, 0))
    shape = lambda rows, cols, kind=BF16: jax.ShapeDtypeStruct((rows, cols), kind)
    flops = 2 * steps * (6 * room * width * hidden + 6 * step * width * padded)
    outs = pl.pallas_call(
        functools.partial(experts_body, groups, units, count, n_parts),
        grid_spec=pltpu.PrefetchScalarGridSpec(
            num_scalar_prefetch=1,
            grid=(steps,),
            in_specs=[
                line, tiled(step, width), tiled(step, width),
                once(w_gate), once(w_up), once(w_down), once(w_shared), once(w_sdown),
            ],
            out_specs=[
                tiled(step, width // 2), tiled(step, width // 2),
                *[tiled(step, cols) for cols in widths], line,
                tiled(room, width),
                tiled(room, width), tiled(room, hidden), tiled(room, hidden),
                tiled(room, hidden), tiled(step, padded), tiled(step, 2 * padded),
            ],
            scratch_shapes=[pltpu.VMEM((room, width), BF16)],
        ),
        out_shape=[
            shape(tokens, width // 2), shape(tokens, width // 2),
            *[shape(tokens, cols) for cols in widths],
            jax.ShapeDtypeStruct((steps, 1, step), F32),
            shape(steps * room, width), shape(steps * room, width), shape(steps * room, hidden),
            shape(steps * room, hidden), shape(steps * room, hidden), shape(tokens, padded),
            shape(tokens, 2 * padded),
        ],
        compiler_params=pltpu.CompilerParams(vmem_limit_bytes=62 << 20),
        cost_estimate=pl.CostEstimate(
            flops=flops, bytes_accessed=130_000_000, transcendentals=5_000_000
        ),
        name="experts",
    )(me, place, hidden2, cotangent, w_gate, w_up, w_down, w_shared, w_sdown)
    return [*outs[:2], list(outs[2 : 2 + n_parts]), *outs[2 + n_parts :]]

def places_of(hit):
    count = hit.shape[1]
    upper = (
        lax.broadcasted_iota(jnp.int32, (count, count), 0)
        < lax.broadcasted_iota(jnp.int32, (count, count), 1)
    ).astype(BF16)
    return matmul(hit.astype(BF16), upper).astype(jnp.int32)


def per_device(
    sizes,
    tokens,
    cotangent,
    gain_attn,
    w_query,
    w_latent,
    gain_latent,
    w_keyval,
    w_output,
    gain_ffn,
    w_shared_gate,
    w_shared_up,
    w_shared_down,
    w_router,
    expert_gate,
    expert_up,
    expert_down,
    segments,
    positions,
    routes,
):
    n_group, n_expert, n_shard = sizes
    n_row = n_expert * n_shard
    n_all = n_group * n_row
    tok_rows, width = tokens.shape
    row_tokens = segments.shape[0]
    n_prompt = row_tokens // GROUP_TOK
    e_per_prompt = n_expert // n_prompt
    group_at = lax.axis_index("group")
    expert_at = lax.axis_index("expert")
    shard_at = lax.axis_index("shard")
    row_at = expert_at * n_shard + shard_at
    prompt_at = expert_at // e_per_prompt
    head_group = expert_at % e_per_prompt

    seg_block = segments[::BLOCK]
    pos_block = positions[::BLOCK]
    prompt_of = seg_block // (NCONT + 1)
    prompt_of = prompt_of - jnp.min(prompt_of)
    cont_of = seg_block % (NCONT + 1)
    piece = jnp.where(cont_of == 0, pos_block // BLOCK, PROMPT // BLOCK - 1 + cont_of)
    slot_of = prompt_of * GROUP_BLOCKS + piece
    block_ids = jnp.arange(n_row, dtype=jnp.int32)
    block_at = jnp.sum(
        jnp.where(slot_of[None, :] == block_ids[:, None], block_ids[None, :], 0), axis=1
    )
    my_blocks = lax.dynamic_slice_in_dim(block_at, prompt_at * GROUP_BLOCKS, GROUP_BLOCKS)
    local_slot = slot_of - prompt_at * GROUP_BLOCKS
    mine = (local_slot >= 0) & (local_slot < GROUP_BLOCKS)
    local_slot = jnp.clip(local_slot, 0, GROUP_BLOCKS - 1)
    own_prompt = jnp.sum(jnp.where(block_ids == row_at, prompt_of, 0))

    def to_pieces(all_rows):
        return take_blocks(all_rows.reshape(n_row, BLOCK, -1), my_blocks).reshape(GROUP_TOK, -1)

    def from_pieces(rows):
        return take_blocks(rows.reshape(GROUP_BLOCKS, BLOCK, -1), local_slot)

    def heads_home(rows):
        got = trade(from_pieces(rows), ROW)
        if n_prompt > 1:
            got = lax.dynamic_slice_in_dim(got, own_prompt * GROUP_BLOCKS, GROUP_BLOCKS)
        return jnp.swapaxes(got, 0, 1).reshape(BLOCK, -1)

    def heads_out(rows):
        split = jnp.swapaxes(rows.reshape(BLOCK, HEADS, -1), 0, 1)
        if n_prompt > 1:
            split = jnp.tile(split, (n_prompt, 1, 1))
            keep = (block_ids // GROUP_BLOCKS) == own_prompt
            split = jnp.where(keep[:, None, None], split, jnp.zeros_like(split))
        return to_pieces(trade(split, ROW))

    def head_parts(weight, per_head):
        cols = lax.dynamic_slice_in_dim(
            weight, head_group * (n_shard * per_head), n_shard * per_head, axis=1
        )
        return jnp.swapaxes(cols.reshape(-1, n_shard, per_head), 0, 1)

    def head_columns(weight, per_head):
        return trade(head_parts(weight, per_head), "shard").reshape(-1, per_head)

    def unit_columns(weight):
        units = weight.shape[1] // n_row
        cols = weight.reshape(weight.shape[0], n_shard, n_expert, units)
        cols = lax.dynamic_index_in_dim(cols, expert_at, axis=2, keepdims=False)
        return jnp.swapaxes(cols, 0, 1)

    paired = (n_group, n_expert) == (2, 4)
    x_at, core_at = expert_at // 2, expert_at % 2

    def sub_rows(weight):
        part = weight.shape[0] // (n_group * n_expert)
        at = (group_at * n_expert + expert_at) * part
        return lax.dynamic_slice_in_dim(weight, at, part)

    def gather_rows_at_once(weight):
        return lax.all_gather(sub_rows(weight), ("shard", "group", "expert"), tiled=True)

    def spread(part):
        return trade(jnp.broadcast_to(part, (n_shard,) + part.shape), "shard")

    def scatter_rows_of_row(part):
        part = part.reshape(2, 2, n_shard * tok_rows, -1)

        def halve(rows, axis, bit, flip):
            send = lax.dynamic_index_in_dim(rows, 1 - bit, axis, keepdims=False)
            keep = lax.dynamic_index_in_dim(rows, bit, axis, keepdims=False)
            got = lax.ppermute(send, "expert", [(i, i ^ flip) for i in range(4)])
            return (keep.astype(F32) + got.astype(F32)).astype(BF16)

        part = halve(halve(part, 1, core_at, 1), 0, x_at, 2)
        return over_shards(part.reshape(n_shard, tok_rows, -1))

    def gather_rows(weight):
        if not paired:
            return gather_rows_at_once(weight)
        got = spread(sub_rows(weight))
        got = pair_gather(got, "expert", 4, 2, x_at)
        got = pair_gather(got, "group", 2, 1, group_at)
        got = pair_gather(got, "expert", 4, 1, core_at)
        return jnp.transpose(got, (3, 1, 2, 0, 4, 5)).reshape(width, -1)

    def swap(rows, axis, count, flip):
        return lax.ppermute(
            rows.astype(BF16), axis, [(i, i ^ flip) for i in range(count)]
        ).astype(F32)

    def scatter_start(left, right, extra=None):
        if not paired:
            whole = matmul_tn(left, right)
            if extra is not None:
                whole = jnp.concatenate([whole, extra], axis=1)
            return whole
        block = left.shape[1] // 8

        def half(core):
            cols = left.reshape(-1, 4, 2, block)
            cols = lax.dynamic_index_in_dim(cols, core, axis=2, keepdims=False)
            out = matmul_tn(cols.reshape(-1, 4 * block), right)
            if extra is not None:
                more = extra.reshape(4, 2, block, -1)
                more = lax.dynamic_index_in_dim(more, core, axis=1, keepdims=False)
                out = jnp.concatenate([out, more.reshape(4 * block, -1)], axis=1)
            return out

        return half(core_at) + swap(half(1 - core_at), "expert", 4, 1)

    def scatter_step(rows, axis, count, flip, bit):
        if not paired:
            return rows
        size = rows.shape[0] // 2
        send = lax.dynamic_slice_in_dim(rows, (1 - bit) * size, size)
        return lax.dynamic_slice_in_dim(rows, bit * size, size) + swap(send, axis, count, flip)

    def scatter_y(rows):
        return scatter_step(rows, "group", 2, 1, group_at)

    def scatter_x(rows):
        return scatter_step(rows, "expert", 4, 2, x_at)

    def scatter_end(rows):
        if not paired:
            return lax.psum_scatter(rows.astype(BF16), ALL, scatter_dimension=0, tiled=True).astype(
                F32
            )
        return over_shards(rows.astype(BF16).reshape(n_shard, -1, rows.shape[1]))

    def over_shards(rows):
        return jnp.sum(trade(rows, "shard").astype(F32), axis=0)

    expert_count = w_router.shape[1]
    top_count = routes.shape[1]
    route_hot = jnp.any(
        routes[:, :, None] == jnp.arange(expert_count, dtype=jnp.int32)[None, None, :], axis=1
    )
    pos_p = jnp.arange(GROUP_TOK, dtype=jnp.int32)
    pos_p = jnp.where(pos_p < PROMPT, pos_p, PROMPT + pos_p % BLOCK)
    cos_p, sin_p = angles(pos_p, ROPE)
    tok_all = lax.all_gather(tokens, ROW, axis=0, tiled=True)
    hit_b = trade(route_hot.T.astype(F32), ROW) > 0.5
    cotangent_late, cos_p, sin_p, hit_b = lax.optimization_barrier(
        (cotangent, cos_p, sin_p, hit_b)
    )
    c_all = lax.all_gather(cotangent_late, ROW, axis=0, tiled=True)
    units = w_shared_gate.shape[1] // n_row
    wq_h = head_columns(w_query, QDIM)
    wkv_h = head_columns(w_keyval, KVDIM)
    w_lr = gather_rows(jnp.concatenate([w_latent, w_router], axis=1))
    w_l, w_r = w_lr[:, : LATENT + ROPE], w_lr[:, LATENT + ROPE :]
    w_joint = jnp.concatenate([wq_h[:, :NOPE], w_l[:, :LATENT], wq_h[:, NOPE:], w_l[:, LATENT:]], 1)
    w_o_near = w_output
    if paired:
        w_o_near = pair_gather(spread(sub_rows(w_output)), "expert", 4, 2, x_at)
    gu_parts = jnp.concatenate([unit_columns(w_shared_gate), unit_columns(w_shared_up)], axis=-1)
    w_joint, wkv_h, tok_all, w_o_near, gu_parts = lax.optimization_barrier(
        (w_joint, wkv_h, tok_all, w_o_near, gu_parts)
    )
    w_gu = trade(gu_parts, "shard").reshape(width, 2 * units)
    if paired:
        w_o_near = pair_gather(w_o_near, "group", 2, 1, group_at)

    capacity = 3 * tok_rows * top_count // (2 * expert_count)
    ahead = capacity * (jnp.arange(n_row, dtype=jnp.int32)[:, None] % 2)
    place = jnp.where(hit_b, places_of(hit_b) + ahead, 1 << 20).reshape(-1, 1, 2 * tok_rows)

    hidden1, query, key, value, comp = project(
        tok_all.reshape(n_row, BLOCK, width),
        my_blocks,
        gain_attn,
        w_joint,
        gain_latent,
        wkv_h,
        cos_p,
        sin_p,
    )
    mixed_f, mixed_h, total_h = attend(query, key, value)
    mixed_h, w_o_near, w_gu = lax.optimization_barrier((mixed_h, w_o_near, w_gu))
    mixed = heads_home(mixed_h)
    if paired:
        w_o = pair_gather(w_o_near, "expert", 4, 1, core_at)
        w_o = jnp.transpose(w_o, (3, 1, 2, 0, 4, 5)).reshape(width, -1)
    else:
        w_o = gather_rows_at_once(w_o_near)
    padded = -(-(units + expert_count) // 128) * 128
    space = lambda cols: jnp.zeros((width, cols), BF16)
    w_sh = jnp.concatenate(
        [
            w_gu[:, :units],
            w_r,
            space(padded - units - expert_count),
            w_gu[:, units:],
            space(padded - units),
        ],
        axis=1,
    )
    w_sd = lax.dynamic_slice_in_dim(w_shared_down, expert_at * units, units)
    w_sd = jnp.pad(w_sd, ((0, padded - units), (0, 0)))

    inputs = tokens.astype(F32)
    grad_out = cotangent.astype(F32)
    normed1, inverse1 = rms_parts(inputs)
    hidden1_own = (normed1 * gain_attn).astype(BF16)
    latent_own = matmul(hidden1_own, w_l)
    normed_c, inverse_c = rms_parts(latent_own[:, :LATENT])
    after = inputs + matmul(mixed, w_o)
    normed2, inverse2 = rms_parts(after)
    hidden2 = (normed2 * gain_ffn).astype(BF16)
    logits = matmul(hidden2, w_r)
    router_prob = jax.nn.softmax(logits, axis=-1)

    hidden2, c_all, w_sh = lax.optimization_barrier((hidden2, c_all, w_sh))
    h2_all = lax.all_gather(hidden2, ROW, axis=0, tiled=True)
    h2_all, w_query = lax.optimization_barrier((h2_all, w_query))
    w_q = gather_rows_at_once(w_query)
    out_a, out_b, dh_parts, d_prob_col, rows, d_out, e_mid, d_gate, d_up, s_mid, ds_gu = experts(
        row_at[None],
        place,
        capacity,
        h2_all,
        c_all,
        expert_gate[0],
        expert_up[0],
        expert_down[0],
        w_sh,
        w_sd,
        units,
        expert_count,
        [width - SIDE, SIDE] if paired else [width],
    )
    d_prob = trade(d_prob_col.reshape(n_row, tok_rows), ROW).T
    dh_parts, w_q = lax.optimization_barrier((dh_parts, w_q))
    d_h2 = lax.psum_scatter(dh_parts[0], ROW, scatter_dimension=0, tiled=True).astype(F32)
    if paired:
        d_h2 = jnp.concatenate([d_h2, scatter_rows_of_row(dh_parts[1])], axis=1)
    d_prob = jnp.where(route_hot, d_prob, 0.0)
    d_logits = (
        router_prob * (d_prob - jnp.sum(router_prob * d_prob, axis=-1, keepdims=True))
    ).astype(BF16)
    grad_router = matmul_tn(hidden2, d_logits)

    def share(whole):
        if n_group != 2:
            return lax.psum_scatter(
                whole.astype(BF16), "group", scatter_dimension=0, tiled=True
            ), None
        half = whole.shape[0] // 2
        send = lax.dynamic_slice_in_dim(whole, (1 - group_at) * half, half).astype(BF16)
        keep = lax.dynamic_slice_in_dim(whole, group_at * half, half)
        return lax.ppermute(send, "group", [(0, 1), (1, 0)]), keep

    whole_0 = matmul_tn(rows, d_gate)
    d_up, ds_gu, whole_0 = lax.optimization_barrier((d_up, ds_gu, whole_0))
    got_0, keep_0 = share(whole_0)
    whole_1 = matmul_tn(rows, d_up)
    grad_gu = matmul_tn(h2_all, ds_gu).astype(BF16)
    e_mid, s_mid, whole_1, got_0, grad_gu = lax.optimization_barrier(
        (e_mid, s_mid, whole_1, got_0, grad_gu)
    )
    got_1, keep_1 = share(whole_1)
    whole_2 = matmul_tn(e_mid, d_out)
    grad_sd_part = matmul_tn(s_mid, c_all)[:units].astype(BF16)
    d_h2, whole_2, grad_sd_part = lax.optimization_barrier((d_h2, whole_2, grad_sd_part))
    whole_2, _ = lax.optimization_barrier((whole_2, got_1))
    got_2, keep_2 = share(whole_2)
    grad_gu = jnp.concatenate(
        [grad_gu[:, :units], grad_gu[:, padded : padded + units]], axis=1
    ).reshape(n_all, width // n_all, 2 * units)
    grad_sd_part = grad_sd_part.reshape(n_group, units // n_group, width)
    d_h2, out_a, out_b, grad_gu, grad_sd_part, grad_router, d_logits = lax.optimization_barrier(
        (d_h2, out_a, out_b, grad_gu, grad_sd_part, grad_router, d_logits)
    )
    ffn_a = lax.psum_scatter(out_a, ROW, scatter_dimension=0, tiled=True)

    d_hidden2 = d_h2 + matmul_nt(d_logits, w_r)
    d_after, grad_gain_ffn = norm_back(d_hidden2, normed2, inverse2, gain_ffn)
    grad_after = grad_out + d_after
    grad_attn = grad_after.astype(BF16)
    d_mixed = matmul_nt(grad_attn, w_o).astype(BF16)
    d_mixed_h = heads_out(d_mixed)
    wo_rows = scatter_start(mixed, grad_attn)
    d_mixed_h, grad_gu, grad_sd_part, got_1, wo_rows = lax.optimization_barrier(
        (d_mixed_h, grad_gu, grad_sd_part, got_1, wo_rows)
    )
    wo_rows = scatter_y(wo_rows)
    gu_got = trade(grad_gu, ALL)
    sd_gots = []
    for turn in range(n_group):
        piece_at = (group_at + turn) % n_group
        moves = []
        for g in range(n_group):
            for e in range(n_expert):
                for s in range(n_shard):
                    target = (s * n_expert + e) * n_group + (g + turn) % n_group
                    moves.append(((g * n_expert + e) * n_shard + s, target))
        sent = lax.dynamic_index_in_dim(grad_sd_part, piece_at, axis=0, keepdims=False)
        sd_gots.append(lax.ppermute(sent, ALL, moves))

    d_query, d_key, d_value = attend_back(
        query, key, value, mixed_f, total_h, d_mixed_h, cos_p, sin_p
    )
    d_keyval, d_latent_part = latent_back(d_key, d_value, wkv_h, local_slot, mine)
    own_pos = lax.dynamic_slice_in_dim(positions, row_at * tok_rows, tok_rows)
    cosine, sine = angles(own_pos, ROPE)
    d_latent_part, ffn_a, gu_got, sd_gots, wo_rows, cosine, sine = lax.optimization_barrier(
        (d_latent_part, ffn_a, gu_got, sd_gots, wo_rows, cosine, sine)
    )
    d_lat = lax.psum_scatter(d_latent_part, ROW, scatter_dimension=0, tiled=True)
    d_query_own = heads_home(d_query)
    grad_wq_h = matmul_tn(hidden1, d_query).astype(BF16).reshape(n_all, width // n_all, QDIM)
    grad_wkv_h = matmul_tn(comp, d_keyval).astype(BF16)
    grad_wkv_h = grad_wkv_h.reshape(n_all, width // n_all, -1)
    head_got = trade(jnp.concatenate([grad_wq_h, grad_wkv_h], axis=-1), ALL)
    wo_rows = scatter_x(wo_rows)
    egrads = [
        (got.astype(F32) if keep is None else keep + got.astype(F32))[None]
        for got, keep in ((got_0, keep_0), (got_1, keep_1), (got_2, keep_2))
    ]
    d_lat, d_query_own, wo_rows, egrads, out_b, head_got = lax.optimization_barrier(
        (d_lat, d_query_own, wo_rows, egrads, out_b, head_got)
    )
    egrad_gate, egrad_up, egrad_down = egrads
    d_lat = d_lat.astype(F32)
    ffn_b = lax.psum_scatter(out_b, ROW, scatter_dimension=0, tiled=True)
    grad_wo = scatter_end(wo_rows)
    output = (after + jnp.concatenate([ffn_a, ffn_b], axis=1).astype(F32)).astype(BF16)
    got = gu_got.astype(F32)
    got = jnp.sum(got.reshape(n_group, n_expert, n_shard, -1, 2 * units), axis=0)
    got = jnp.transpose(got, (2, 1, 0, 3))
    grad_sg = got[..., :units].reshape(got.shape[0], -1)
    grad_su = got[..., units:].reshape(got.shape[0], -1)
    grad_sd = sum(got.astype(F32) for got in sd_gots)

    got = head_got.astype(F32)
    got = jnp.sum(got.reshape(n_group * n_prompt, HEADS, got.shape[1], got.shape[2]), axis=0)
    grad_wq = jnp.swapaxes(got[..., :QDIM], 0, 1).reshape(got.shape[1], -1)
    grad_wkv = jnp.swapaxes(
        got[..., QDIM:].reshape(HEADS, LATENT // n_all, KVDIM), 0, 1
    ).reshape(LATENT // n_all, -1)

    d_lat_c, grad_gain_latent = norm_back(d_lat[:, :LATENT], normed_c, inverse_c, gain_latent)
    d_latent = jnp.concatenate([d_lat_c, unrotate(d_lat[:, LATENT:], cosine, sine)], axis=1).astype(
        BF16
    )
    d_hidden1 = matmul_nt(d_query_own, w_q) + matmul_nt(d_latent, w_l)
    d_tok, grad_gain_attn = norm_back(d_hidden1, normed1, inverse1, gain_attn)
    grad_tokens = grad_after + d_tok
    own = width // n_all
    lat = LATENT // n_all
    gain_l = jnp.pad(grad_gain_latent.reshape(n_all, lat), ((0, 0), (0, own - lat)))
    beside = jnp.concatenate(
        [
            grad_router,
            grad_gain_attn[:, None],
            grad_gain_ffn[:, None],
            gain_l.reshape(width, 1),
        ],
        axis=1,
    )
    beside = jnp.pad(beside, ((0, 0), (0, -(LATENT + ROPE + expert_count + 3) % 128)))
    sums = scatter_end(scatter_x(scatter_y(scatter_start(hidden1_own, d_latent, beside))))
    grad_wl = sums[:, : LATENT + ROPE]
    at = LATENT + ROPE + expert_count
    grad_r, grad_ga, grad_gf, grad_gl = (
        sums[:, LATENT + ROPE : at],
        sums[:, at],
        sums[:, at + 1],
        sums[:lat, at + 2],
    )
    return (
        output,
        grad_tokens,
        grad_ga,
        grad_wq,
        grad_wl,
        grad_gl,
        grad_wkv,
        grad_wo,
        grad_gf,
        grad_sg,
        grad_su,
        grad_sd,
        grad_r,
        egrad_gate,
        egrad_up,
        egrad_down,
    )


def solution(mesh):
    sizes = tuple(mesh.shape[name] for name in ALL)
    return jax.shard_map(
        functools.partial(per_device, sizes),
        mesh=mesh,
        in_specs=(
            P(ALL, None),
            P(ALL, None),
            P(),
            P("shard", None),
            P("shard", None),
            P(),
            P("shard", None),
            P("shard", None),
            P(),
            P("shard", None),
            P("shard", None),
            P("shard", None),
            P("shard", None),
            P(ROW, None, None),
            P(ROW, None, None),
            P(ROW, None, None),
            P("group"),
            P("group"),
            P(ALL, None),
        ),
        out_specs=(
            P(ALL, None),
            P(ALL, None),
            P(ALL),
            P(ALL, None),
            P(ALL, None),
            P(ALL),
            P(ALL, None),
            P(ALL, None),
            P(ALL),
            P(ALL, None),
            P(ALL, None),
            P(ALL, None),
            P(ALL, None),
            P(ROW, "group", None),
            P(ROW, "group", None),
            P(ROW, "group", None),
        ),
        check_vma=False,
    )
```

```python
import functools
import math

import jax
import jax.numpy as jnp
from jax import lax
from jax.experimental import pallas as pl
from jax.experimental.pallas import tpu as pltpu
from jax.sharding import PartitionSpec as P

HEADS = 16
NOPE = 128
ROPE = 64
VDIM = 128
LATENT = 512
BLOCK = 256
PROMPT = 2048
NCONT = 8
QDIM = NOPE + ROPE
KVDIM = NOPE + VDIM
GROUP_BLOCKS = PROMPT // BLOCK + NCONT
GROUP_TOK = GROUP_BLOCKS * BLOCK
SIDE = 512

EPS = 1e-06
ALL = ("group", "expert", "shard")
ROW = ("expert", "shard")
SCALE = 1.0 / math.sqrt(NOPE + ROPE)
F32 = jnp.float32
BF16 = jnp.bfloat16


def matmul(left, right):
    return jnp.dot(left, right, preferred_element_type=F32)


def matmul_nt(left, right):
    return lax.dot_general(left, right, (((1,), (1,)), ((), ())), preferred_element_type=F32)


def matmul_tn(left, right):
    return lax.dot_general(left, right, (((0,), (0,)), ((), ())), preferred_element_type=F32)


def rms_parts(values):
    inverse = lax.rsqrt(jnp.mean(values * values, axis=-1, keepdims=True) + EPS)
    return (values * inverse, inverse)


def norm_back(grad_in, normed, inverse, gain):
    scaled = grad_in * gain
    gain_grad = jnp.sum(grad_in * normed, axis=0)
    input_grad = inverse * (scaled - normed * jnp.mean(scaled * normed, axis=-1, keepdims=True))
    return (input_grad, gain_grad)


def angles(pos_list, rot_width):
    half_width = rot_width // 2
    freq = 10000.0 ** (-2.0 * jnp.arange(half_width, dtype=F32) / rot_width)
    theta = pos_list.astype(F32)[:, None] * freq[None, :]
    return (jnp.cos(theta), jnp.sin(theta))


def rotate(values, cosine, sine):
    half_width = values.shape[-1] // 2
    first_half = values[..., :half_width]
    second_half = values[..., half_width:]
    return jnp.concatenate(
        [first_half * cosine - second_half * sine, second_half * cosine + first_half * sine],
        axis=-1,
    )


def unrotate(grad_in, cosine, sine):
    return rotate(grad_in, cosine, -sine)


def silu_parts(values):
    sigmoid = jax.nn.sigmoid(values)
    return (values * sigmoid, sigmoid * (1.0 + values * (1.0 - sigmoid)))


def trade(buffer, axes):
    return lax.all_to_all(buffer, axes, split_axis=0, concat_axis=0, tiled=True)


TILE = 2 * BLOCK
TILES = GROUP_TOK // TILE
PROMPT_TILES = PROMPT // TILE
NEG = -1e30


def dot(left, right, left_dim, right_dim):
    return lax.dot_general(
        left, right, (((left_dim,), (right_dim,)), ((), ())), preferred_element_type=F32
    )


def take_blocks(blocks, index):
    count = index.shape[0]
    shape = blocks.shape[1:]
    unroll = 8 if shape[-1] <= 256 else 4

    def body(index_ref, *refs):
        for i in range(unroll):
            refs[-1][i] = refs[i][0]

    return pl.pallas_call(
        body,
        grid_spec=pltpu.PrefetchScalarGridSpec(
            num_scalar_prefetch=1,
            grid=(count // unroll,),
            in_specs=[
                pl.BlockSpec((1,) + shape, lambda i, at, k=k: (at[i * unroll + k], 0, 0))
                for k in range(unroll)
            ],
            out_specs=pl.BlockSpec((unroll,) + shape, lambda i, at: (i, 0, 0)),
        ),
        out_shape=jax.ShapeDtypeStruct((count,) + shape, blocks.dtype),
        compiler_params=pltpu.CompilerParams(vmem_limit_bytes=40 << 20),
        cost_estimate=pl.CostEstimate(
            flops=0, bytes_accessed=4 * count * shape[0] * shape[1], transcendentals=0
        ),
        name="take_blocks",
    )(index, *([blocks] * unroll))


def project_body(
    at_ref, tok_a, tok_b, gain_ref, w_ref, gain_l_ref, wkv_ref, cos_ref, sin_ref,
    hid_ref, q_ref, k_ref, v_ref, comp_ref,
):
    gain = gain_ref[...]
    gain_l = gain_l_ref[...]
    for part, tok in enumerate((tok_a, tok_b)):
        rows = slice(part * BLOCK, (part + 1) * BLOCK)
        hidden = (rms_parts(tok[0].astype(F32))[0] * gain).astype(BF16)
        hid_ref[rows, :] = hidden
        joint = dot(hidden, w_ref[...], 1, 0)
        cosine, sine = cos_ref[rows, :], sin_ref[rows, :]
        at = NOPE + LATENT
        q_ref[rows, :NOPE] = joint[:, :NOPE].astype(BF16)
        q_ref[rows, NOPE:] = rotate(joint[:, at : at + ROPE], cosine, sine).astype(BF16)
        comp = (rms_parts(joint[:, NOPE:at])[0] * gain_l).astype(BF16)
        comp_ref[rows, :] = comp
        keyval = dot(comp, wkv_ref[...], 1, 0).astype(BF16)
        k_ref[rows, :NOPE] = keyval[:, :NOPE]
        k_ref[rows, NOPE:] = rotate(joint[:, at + ROPE :], cosine, sine).astype(BF16)
        v_ref[rows, :] = keyval[:, NOPE:]


def project(blocks, index, gain, weights, gain_l, wkv, cosine, sine):
    width = blocks.shape[-1]
    whole = lambda a: pl.BlockSpec(a.shape, lambda i, at: (0, 0))
    tiled = lambda cols: pl.BlockSpec((TILE, cols), lambda i, at: (i, 0))
    piece = lambda k: pl.BlockSpec((1, BLOCK, width), lambda i, at: (at[2 * i + k], 0, 0))
    widths = (width, QDIM, QDIM, VDIM, LATENT)
    gain, gain_l = gain.reshape(1, -1), gain_l.reshape(1, -1)
    return pl.pallas_call(
        project_body,
        grid_spec=pltpu.PrefetchScalarGridSpec(
            num_scalar_prefetch=1,
            grid=(TILES,),
            in_specs=[
                piece(0), piece(1), whole(gain), whole(weights), whole(gain_l), whole(wkv),
                tiled(ROPE // 2), tiled(ROPE // 2),
            ],
            out_specs=[tiled(cols) for cols in widths],
        ),
        out_shape=[jax.ShapeDtypeStruct((GROUP_TOK, cols), BF16) for cols in widths],
        compiler_params=pltpu.CompilerParams(vmem_limit_bytes=48 << 20),
        cost_estimate=pl.CostEstimate(
            flops=14_000_000_000, bytes_accessed=48_000_000, transcendentals=0
        ),
        name="project",
    )(index, blocks, blocks, gain, weights, gain_l, wkv, cosine, sine)


def own_mask(tile):
    k_at = lax.broadcasted_iota(jnp.int32, (TILE, TILE), 0)
    q_at = lax.broadcasted_iota(jnp.int32, (TILE, TILE), 1)
    piece = jnp.where(tile < PROMPT_TILES, TILE, BLOCK)
    lowest = jnp.where(q_at >= piece, piece, 0)
    return (k_at <= q_at) & (k_at >= lowest)


def attend_body(q_ref, k_ref, v_ref, o_ref, ob_ref, lse_ref, s_ref):
    tile = pl.program_id(0)
    q = q_ref[...]
    others = jnp.minimum(tile, PROMPT_TILES)

    def rows_of(at):
        return pl.ds(pl.multiple_of(at * TILE, TILE), TILE)

    def fold(values, op):
        return op(values.reshape(TILE // 8, 8, TILE), axis=0)

    own = jnp.where(own_mask(tile), dot(k_ref[rows_of(tile), :], q, 1, 1) * SCALE, NEG)
    s_ref[rows_of(PROMPT_TILES), :] = own

    def raw(at, top):
        s = dot(k_ref[rows_of(at), :], q, 1, 1) * SCALE
        s_ref[rows_of(at), :] = s
        return jnp.maximum(top, fold(s, jnp.max))

    top = lax.fori_loop(0, others, raw, fold(own, jnp.max))
    top = jnp.max(top, axis=0, keepdims=True)

    def mix(s_at, v_at, carry):
        total, out = carry
        p = jnp.exp(s_ref[rows_of(s_at), :] - top)
        return total + fold(p, jnp.sum), out + dot(p.astype(BF16), v_ref[rows_of(v_at), :], 0, 0)

    carry = (jnp.zeros((8, TILE), F32), jnp.zeros((TILE, VDIM), F32))
    carry = mix(PROMPT_TILES, tile, carry)
    total, out = lax.fori_loop(0, others, lambda at, c: mix(at, at, c), carry)
    total = jnp.sum(total, axis=0, keepdims=True)
    lse_ref[...] = top + jnp.log(total)
    scale = jnp.transpose(jnp.broadcast_to(1.0 / total, (VDIM, TILE)))
    out = out * scale
    o_ref[...] = out
    ob_ref[...] = out.astype(BF16)


def attend(query, key, value):
    whole = lambda cols: pl.BlockSpec((GROUP_TOK, cols), lambda i: (0, 0))
    tiled = lambda cols: pl.BlockSpec((TILE, cols), lambda i: (i, 0))
    return pl.pallas_call(
        attend_body,
        grid=(TILES,),
        in_specs=[tiled(QDIM), whole(QDIM), whole(VDIM)],
        out_specs=[tiled(VDIM), tiled(VDIM), pl.BlockSpec((1, TILE), lambda i: (0, i))],
        out_shape=[
            jax.ShapeDtypeStruct((GROUP_TOK, VDIM), F32),
            jax.ShapeDtypeStruct((GROUP_TOK, VDIM), BF16),
            jax.ShapeDtypeStruct((1, GROUP_TOK), F32),
        ],
        scratch_shapes=[pltpu.VMEM((PROMPT + TILE, TILE), F32)],
        compiler_params=pltpu.CompilerParams(vmem_limit_bytes=40 << 20),
        cost_estimate=pl.CostEstimate(
            flops=6_000_000_000, bytes_accessed=10_000_000, transcendentals=8_000_000
        ),
        name="attend",
    )(query, key, value)


def attend_back_body(
    q_ref, k_ref, v_ref, g_ref, o_ref, lse_ref, cos_ref, sin_ref, dq_ref, dk_ref, dv_ref, acc_ref
):
    tile = pl.program_id(0)

    @pl.when(tile == 0)
    def _():
        dk_ref[...] = jnp.zeros_like(dk_ref)
        dv_ref[...] = jnp.zeros_like(dv_ref)

    q = q_ref[...]
    g = g_ref[...]
    lse = lse_ref[...]
    delta = jnp.sum(jnp.transpose(g.astype(F32) * o_ref[...]), axis=0, keepdims=True)

    def step(at, mask):
        rows = pl.ds(pl.multiple_of(at * TILE, TILE), TILE)
        k = k_ref[rows, :]
        p = jnp.exp(dot(k, q, 1, 1) * SCALE - lse)
        if mask is not None:
            p = jnp.where(mask, p, 0.0)
        ds = (p * (dot(v_ref[rows, :], g, 1, 1) - delta)).astype(BF16)
        dv_ref[rows, :] += dot(p.astype(BF16), g, 1, 0)
        dk_ref[rows, :] += dot(ds, q, 1, 0) * SCALE
        return dot(ds, k, 0, 0)

    acc_ref[...] = step(tile, own_mask(tile))

    @pl.loop(0, jnp.minimum(tile, PROMPT_TILES))
    def _(at):
        acc_ref[...] += step(at, None)

    dq = acc_ref[...] * SCALE
    dq_ref[:, :NOPE] = dq[:, :NOPE].astype(BF16)
    dq_ref[:, NOPE:] = rotate(dq[:, NOPE:], cos_ref[...], -sin_ref[...]).astype(BF16)


def attend_back(query, key, value, mixed, lse, grad, cosine, sine):
    whole = lambda cols: pl.BlockSpec((GROUP_TOK, cols), lambda i: (0, 0))
    tiled = lambda cols: pl.BlockSpec((TILE, cols), lambda i: (i, 0))
    return pl.pallas_call(
        attend_back_body,
        grid=(TILES,),
        in_specs=[
            tiled(QDIM), whole(QDIM), whole(VDIM), tiled(VDIM), tiled(VDIM),
            pl.BlockSpec((1, TILE), lambda i: (0, i)), tiled(ROPE // 2), tiled(ROPE // 2),
        ],
        out_specs=[tiled(QDIM), whole(QDIM), whole(VDIM)],
        out_shape=[
            jax.ShapeDtypeStruct((GROUP_TOK, QDIM), BF16),
            jax.ShapeDtypeStruct((GROUP_TOK, QDIM), F32),
            jax.ShapeDtypeStruct((GROUP_TOK, VDIM), F32),
        ],
        scratch_shapes=[pltpu.VMEM((TILE, QDIM), F32)],
        compiler_params=pltpu.CompilerParams(vmem_limit_bytes=48 << 20),
        cost_estimate=pl.CostEstimate(
            flops=16_000_000_000, bytes_accessed=20_000_000, transcendentals=8_000_000
        ),
        name="attend_back",
    )(query, key, value, grad, mixed, lse, cosine, sine)


def latent_back_body(slot_ref, mine_ref, dk_ref, dv_ref, w_ref, dkv_ref, lat_ref):
    kv = jnp.concatenate([dk_ref[:, :NOPE], dv_ref[...]], axis=1).astype(BF16)
    dkv_ref[...] = kv
    keep = mine_ref[pl.program_id(0)] != 0
    comp = jnp.where(keep, dot(kv, w_ref[...], 1, 1), 0.0)
    lat_ref[:, :LATENT] = comp.astype(BF16)
    lat_ref[:, LATENT:] = jnp.where(keep, dk_ref[:, NOPE:], 0.0).astype(BF16)


def latent_back(d_key, d_value, wkv, slot, mine):
    count = slot.shape[0]
    tiled = lambda cols: pl.BlockSpec((BLOCK, cols), lambda i, at, m: (at[i], 0))
    return pl.pallas_call(
        latent_back_body,
        grid_spec=pltpu.PrefetchScalarGridSpec(
            num_scalar_prefetch=2,
            grid=(count,),
            in_specs=[
                tiled(QDIM), tiled(VDIM), pl.BlockSpec(wkv.shape, lambda i, at, m: (0, 0)),
            ],
            out_specs=[
                tiled(KVDIM), pl.BlockSpec((BLOCK, LATENT + ROPE), lambda i, at, m: (i, 0)),
            ],
        ),
        out_shape=[
            jax.ShapeDtypeStruct((GROUP_TOK, KVDIM), BF16),
            jax.ShapeDtypeStruct((count * BLOCK, LATENT + ROPE), BF16),
        ],
        cost_estimate=pl.CostEstimate(
            flops=1_100_000_000, bytes_accessed=14_000_000, transcendentals=0
        ),
        name="latent_back",
    )(slot, mine.astype(jnp.int32), d_key, d_value, wkv)

def line_gather(part, axis, count):
    up = [(i, i + 1) for i in range(count - 1)]
    down = [(i + 1, i) for i in range(count - 1)]
    right, left = [part], [part]
    for _ in range(count - 1):
        right.append(lax.ppermute(right[-1], axis, up))
        left.append(lax.ppermute(left[-1], axis, down))
    line = jnp.stack(right[:0:-1] + left)
    return lax.dynamic_slice_in_dim(line, count - 1 - lax.axis_index(axis), count)


def pair_gather(part, axis, count, flip, bit):
    other = lax.ppermute(part, axis, [(i, i ^ flip) for i in range(count)])
    return lax.dynamic_slice_in_dim(jnp.stack([part, other, part]), bit, 2)


def chunks_of(total, size):
    return [slice(at, min(at + size, total)) for at in range(0, total, size)]


def experts_body(
    groups, units, count, n_parts, me_ref, place_ref, h_ref, crow_ref, dmid_ref, dsmid_ref, wg_ref,
    wu_ref, wd_ref, ws_ref, wsd_ref, outa_ref, outb_ref, *refs,
):
    dh_refs = refs[:n_parts]
    dprob_ref, rows_ref, dout_ref, mid_ref, dg_ref, du_ref, smid_ref, ds_ref = refs[n_parts:]
    width, hidden = wg_ref.shape
    padded = wsd_ref.shape[0]
    h = h_ref[...]
    ends = [0]
    for ref in dh_refs:
        ends.append(ends[-1] + ref.shape[1])

    wide = dot(h, ws_ref[...], 1, 0)
    s_gate, s_up = wide[:, :padded], wide[:, padded:]
    first = units - (padded - 128)
    logits = jnp.transpose(s_gate[:, padded - 128 :])[first : first + count, :]
    powers = jnp.exp(logits - jnp.max(logits, axis=0, keepdims=True))
    mine = lax.broadcasted_iota(jnp.int32, powers.shape, 0) == me_ref[0]
    weight = jnp.sum(jnp.where(mine, powers, 0.0), axis=0, keepdims=True) / jnp.sum(
        powers, axis=0, keepdims=True
    )
    s_act, s_slope = silu_parts(s_gate)
    smid_ref[...] = (s_act * s_up).astype(BF16)
    ds_mid = dsmid_ref[...]
    ds_ref[:, :padded] = (ds_mid * s_up * s_slope).astype(BF16)
    ds_ref[:, padded:] = (ds_mid * s_act).astype(BF16)

    picks, weights = [], []
    for rows, toks in groups:
        shape = (rows.stop - rows.start, toks.stop - toks.start)
        here = lax.broadcasted_iota(jnp.int32, shape, 0) + rows.start == place_ref[0, :, toks]
        pick = jnp.where(here, 1.0, 0.0).astype(BF16)
        scale = jnp.sum(jnp.where(here, weight[:, toks], 0.0), axis=1, keepdims=True)
        for cols in chunks_of(width, 512):
            rows_ref[rows, cols] = dot(pick, h[toks, cols], 1, 0).astype(BF16)
            dout_ref[rows, cols] = (scale * crow_ref[rows, cols].astype(F32)).astype(BF16)
        picks.append((rows, toks, here, pick))
        weights.append(scale)
    scale = jnp.concatenate(weights, axis=0) if len(weights) > 1 else weights[0]

    for cols in chunks_of(hidden, 512):
        gate = dot(rows_ref[...], wg_ref[:, cols], 1, 0)
        up = dot(rows_ref[...], wu_ref[:, cols], 1, 0)
        act, slope = silu_parts(gate)
        mid_ref[:, cols] = (act * up).astype(BF16)
        d_mid = scale * dmid_ref[:, cols]
        dg_ref[:, cols] = (d_mid * up * slope).astype(BF16)
        du_ref[:, cols] = (d_mid * act).astype(BF16)

    d_prob = jnp.zeros(scale.shape, F32)
    for cols in chunks_of(width, 512):
        out = dot(mid_ref[...], wd_ref[:, cols], 1, 0).astype(BF16).astype(F32)
        d_prob = d_prob + jnp.sum(out * crow_ref[:, cols].astype(F32), axis=1, keepdims=True)
        out = (out * scale).astype(BF16)
        d_rows = dot(dg_ref[...], wg_ref[cols, :], 1, 1) + dot(du_ref[...], wu_ref[cols, :], 1, 1)
        d_rows = d_rows.astype(BF16)
        for rows, toks, here, pick in picks:
            shared = dot(smid_ref[toks, :], wsd_ref[:, cols], 1, 0)
            half_ref, at = (outa_ref, 0) if cols.start < width // 2 else (outb_ref, width // 2)
            half_ref[toks, cols.start - at : cols.stop - at] = (
                dot(pick, out[rows, :], 0, 0) + shared
            ).astype(BF16)
            shared = dot(ds_ref[toks, :], ws_ref[cols, :], 1, 1)
            for ref, start, stop in zip(dh_refs, ends, ends[1:]):
                if start <= cols.start < stop:
                    ref[toks, cols.start - start : cols.stop - start] = (
                        dot(pick, d_rows[rows, :], 0, 0) + shared
                    ).astype(BF16)
    for rows, toks, here, pick in picks:
        dprob_ref[0, :, toks] = jnp.sum(
            jnp.where(here, d_prob[rows, :], 0.0), axis=0, keepdims=True
        )


def groups_of(capacity, blocks):
    if capacity % 16 == 0:
        return [
            (slice(b * capacity, (b + 1) * capacity), slice(b * BLOCK, (b + 1) * BLOCK))
            for b in range(blocks)
        ]
    return [(slice(0, blocks * capacity), slice(0, blocks * BLOCK))]


def cotangent_body(groups, place_ref, c_ref, wd_ref, wsd_ref, crow_ref, dmid_ref, dsmid_ref):
    dsmid_ref[...] = dot(c_ref[...], wsd_ref[...], 1, 1)
    for rows, toks in groups:
        shape = (rows.stop - rows.start, toks.stop - toks.start)
        here = lax.broadcasted_iota(jnp.int32, shape, 0) + rows.start == place_ref[0, :, toks]
        pick = jnp.where(here, 1.0, 0.0).astype(BF16)
        for cols in chunks_of(c_ref.shape[1], 512):
            crow_ref[rows, cols] = dot(pick, c_ref[toks, cols], 1, 0).astype(BF16)
    for cols in chunks_of(wd_ref.shape[0], 512):
        dmid_ref[:, cols] = dot(crow_ref[...], wd_ref[cols, :], 1, 1)


def cotangent_rows(place, capacity, cotangent, w_down, w_sdown):
    tokens, width = cotangent.shape
    hidden, padded = w_down.shape[0], w_sdown.shape[0]
    step, room, steps = 2 * BLOCK, 2 * capacity, tokens // (2 * BLOCK)
    once = lambda a: pl.BlockSpec(a.shape, lambda i: (0, 0), pipeline_mode=pl.Buffered(1))
    tiled = lambda rows, cols: pl.BlockSpec((rows, cols), lambda i: (i, 0))
    return pl.pallas_call(
        functools.partial(cotangent_body, groups_of(capacity, 2)),
        grid=(steps,),
        in_specs=[
            pl.BlockSpec((1, 1, step), lambda i: (i, 0, 0)), tiled(step, width), once(w_down),
            once(w_sdown),
        ],
        out_specs=[tiled(room, width), tiled(room, hidden), tiled(step, padded)],
        out_shape=[
            jax.ShapeDtypeStruct((steps * room, width), BF16),
            jax.ShapeDtypeStruct((steps * room, hidden), F32),
            jax.ShapeDtypeStruct((tokens, padded), F32),
        ],
        compiler_params=pltpu.CompilerParams(vmem_limit_bytes=40 << 20),
        cost_estimate=pl.CostEstimate(
            flops=2 * steps * width * (room * hidden + step * padded + room * step),
            bytes_accessed=55_000_000,
            transcendentals=0,
        ),
        name="cotangent_rows",
    )(place, cotangent, w_down, w_sdown)


def experts(
    me, place, capacity, hidden2, c_kept, w_gate, w_up, w_down, w_shared, w_sdown, units, count,
    widths,
):
    width, hidden = w_gate.shape
    tokens = hidden2.shape[0]
    n_parts = len(widths)
    padded = w_sdown.shape[0]
    blocks = 2
    step = blocks * BLOCK
    steps = tokens // step
    room = blocks * capacity
    groups = groups_of(capacity, blocks)
    once = lambda a: pl.BlockSpec(a.shape, lambda i, me: (0, 0), pipeline_mode=pl.Buffered(1))
    tiled = lambda rows, cols: pl.BlockSpec((rows, cols), lambda i, me: (i, 0))
    line = pl.BlockSpec((1, 1, step), lambda i, me: (i, 0, 0))
    shape = lambda rows, cols, kind=BF16: jax.ShapeDtypeStruct((rows, cols), kind)
    flops = 2 * steps * (5 * room * width * hidden + 5 * step * width * padded)
    outs = pl.pallas_call(
        functools.partial(experts_body, groups, units, count, n_parts),
        grid_spec=pltpu.PrefetchScalarGridSpec(
            num_scalar_prefetch=1,
            grid=(steps,),
            in_specs=[
                line, tiled(step, width), tiled(room, width), tiled(room, hidden), tiled(step, padded),
                once(w_gate), once(w_up), once(w_down), once(w_shared), once(w_sdown),
            ],
            out_specs=[
                tiled(step, width // 2), tiled(step, width // 2),
                *[tiled(step, cols) for cols in widths], line,
                tiled(room, width),
                tiled(room, width), tiled(room, hidden), tiled(room, hidden),
                tiled(room, hidden), tiled(step, padded), tiled(step, 2 * padded),
            ],
        ),
        out_shape=[
            shape(tokens, width // 2), shape(tokens, width // 2),
            *[shape(tokens, cols) for cols in widths],
            jax.ShapeDtypeStruct((steps, 1, step), F32),
            shape(steps * room, width), shape(steps * room, width), shape(steps * room, hidden),
            shape(steps * room, hidden), shape(steps * room, hidden), shape(tokens, padded),
            shape(tokens, 2 * padded),
        ],
        compiler_params=pltpu.CompilerParams(vmem_limit_bytes=62 << 20),
        cost_estimate=pl.CostEstimate(
            flops=flops, bytes_accessed=130_000_000, transcendentals=5_000_000
        ),
        name="experts",
    )(me, place, hidden2, *c_kept, w_gate, w_up, w_down, w_shared, w_sdown)
    return [*outs[:2], list(outs[2 : 2 + n_parts]), *outs[2 + n_parts :]]

def places_of(hit):
    count = hit.shape[1]
    upper = (
        lax.broadcasted_iota(jnp.int32, (count, count), 0)
        < lax.broadcasted_iota(jnp.int32, (count, count), 1)
    ).astype(BF16)
    return matmul(hit.astype(BF16), upper).astype(jnp.int32)


def per_device(
    sizes,
    tokens,
    cotangent,
    gain_attn,
    w_query,
    w_latent,
    gain_latent,
    w_keyval,
    w_output,
    gain_ffn,
    w_shared_gate,
    w_shared_up,
    w_shared_down,
    w_router,
    expert_gate,
    expert_up,
    expert_down,
    segments,
    positions,
    routes,
):
    n_group, n_expert, n_shard = sizes
    n_row = n_expert * n_shard
    n_all = n_group * n_row
    tok_rows, width = tokens.shape
    row_tokens = segments.shape[0]
    n_prompt = row_tokens // GROUP_TOK
    e_per_prompt = n_expert // n_prompt
    group_at = lax.axis_index("group")
    expert_at = lax.axis_index("expert")
    shard_at = lax.axis_index("shard")
    row_at = expert_at * n_shard + shard_at
    prompt_at = expert_at // e_per_prompt
    head_group = expert_at % e_per_prompt

    seg_block = segments[::BLOCK]
    pos_block = positions[::BLOCK]
    prompt_of = seg_block // (NCONT + 1)
    prompt_of = prompt_of - jnp.min(prompt_of)
    cont_of = seg_block % (NCONT + 1)
    piece = jnp.where(cont_of == 0, pos_block // BLOCK, PROMPT // BLOCK - 1 + cont_of)
    slot_of = prompt_of * GROUP_BLOCKS + piece
    block_ids = jnp.arange(n_row, dtype=jnp.int32)
    block_at = jnp.sum(
        jnp.where(slot_of[None, :] == block_ids[:, None], block_ids[None, :], 0), axis=1
    )
    my_blocks = lax.dynamic_slice_in_dim(block_at, prompt_at * GROUP_BLOCKS, GROUP_BLOCKS)
    local_slot = slot_of - prompt_at * GROUP_BLOCKS
    mine = (local_slot >= 0) & (local_slot < GROUP_BLOCKS)
    local_slot = jnp.clip(local_slot, 0, GROUP_BLOCKS - 1)
    own_prompt = jnp.sum(jnp.where(block_ids == row_at, prompt_of, 0))

    def to_pieces(all_rows):
        return take_blocks(all_rows.reshape(n_row, BLOCK, -1), my_blocks).reshape(GROUP_TOK, -1)

    def from_pieces(rows):
        return take_blocks(rows.reshape(GROUP_BLOCKS, BLOCK, -1), local_slot)

    def heads_home(rows):
        got = trade(from_pieces(rows), ROW)
        if n_prompt > 1:
            got = lax.dynamic_slice_in_dim(got, own_prompt * GROUP_BLOCKS, GROUP_BLOCKS)
        return jnp.swapaxes(got, 0, 1).reshape(BLOCK, -1)

    def heads_out(rows):
        split = jnp.swapaxes(rows.reshape(BLOCK, HEADS, -1), 0, 1)
        if n_prompt > 1:
            split = jnp.tile(split, (n_prompt, 1, 1))
            keep = (block_ids // GROUP_BLOCKS) == own_prompt
            split = jnp.where(keep[:, None, None], split, jnp.zeros_like(split))
        return to_pieces(trade(split, ROW))

    def head_parts(weight, per_head):
        cols = lax.dynamic_slice_in_dim(
            weight, head_group * (n_shard * per_head), n_shard * per_head, axis=1
        )
        return jnp.swapaxes(cols.reshape(-1, n_shard, per_head), 0, 1)

    def head_columns(weight, per_head):
        return trade(head_parts(weight, per_head), "shard").reshape(-1, per_head)

    def unit_columns(weight):
        units = weight.shape[1] // n_row
        cols = weight.reshape(weight.shape[0], n_shard, n_expert, units)
        cols = lax.dynamic_index_in_dim(cols, expert_at, axis=2, keepdims=False)
        return jnp.swapaxes(cols, 0, 1)

    paired = (n_group, n_expert) == (2, 4)
    x_at, core_at = expert_at // 2, expert_at % 2

    def sub_rows(weight):
        part = weight.shape[0] // (n_group * n_expert)
        at = (group_at * n_expert + expert_at) * part
        return lax.dynamic_slice_in_dim(weight, at, part)

    def gather_rows_at_once(weight):
        return lax.all_gather(sub_rows(weight), ("shard", "group", "expert"), tiled=True)

    def spread(part):
        return trade(jnp.broadcast_to(part, (n_shard,) + part.shape), "shard")

    def scatter_rows_of_row(part):
        part = part.reshape(2, 2, n_shard * tok_rows, -1)

        def halve(rows, axis, bit, flip):
            send = lax.dynamic_index_in_dim(rows, 1 - bit, axis, keepdims=False)
            keep = lax.dynamic_index_in_dim(rows, bit, axis, keepdims=False)
            got = lax.ppermute(send, "expert", [(i, i ^ flip) for i in range(4)])
            return (keep.astype(F32) + got.astype(F32)).astype(BF16)

        part = halve(halve(part, 1, core_at, 1), 0, x_at, 2)
        return over_shards(part.reshape(n_shard, tok_rows, -1))

    def gather_rows(weight):
        if not paired:
            return gather_rows_at_once(weight)
        got = spread(sub_rows(weight))
        got = pair_gather(got, "expert", 4, 2, x_at)
        got = pair_gather(got, "group", 2, 1, group_at)
        got = pair_gather(got, "expert", 4, 1, core_at)
        return jnp.transpose(got, (3, 1, 2, 0, 4, 5)).reshape(width, -1)

    def swap(rows, axis, count, flip):
        return lax.ppermute(
            rows.astype(BF16), axis, [(i, i ^ flip) for i in range(count)]
        ).astype(F32)

    def scatter_start(left, right, extra=None):
        if not paired:
            whole = matmul_tn(left, right)
            if extra is not None:
                whole = jnp.concatenate([whole, extra], axis=1)
            return whole
        block = left.shape[1] // 8

        def half(core):
            cols = left.reshape(-1, 4, 2, block)
            cols = lax.dynamic_index_in_dim(cols, core, axis=2, keepdims=False)
            out = matmul_tn(cols.reshape(-1, 4 * block), right)
            if extra is not None:
                more = extra.reshape(4, 2, block, -1)
                more = lax.dynamic_index_in_dim(more, core, axis=1, keepdims=False)
                out = jnp.concatenate([out, more.reshape(4 * block, -1)], axis=1)
            return out

        return half(core_at) + swap(half(1 - core_at), "expert", 4, 1)

    def scatter_step(rows, axis, count, flip, bit):
        if not paired:
            return rows
        size = rows.shape[0] // 2
        send = lax.dynamic_slice_in_dim(rows, (1 - bit) * size, size)
        return lax.dynamic_slice_in_dim(rows, bit * size, size) + swap(send, axis, count, flip)

    def scatter_y(rows):
        return scatter_step(rows, "group", 2, 1, group_at)

    def scatter_x(rows):
        return scatter_step(rows, "expert", 4, 2, x_at)

    def scatter_end(rows):
        if not paired:
            return lax.psum_scatter(rows.astype(BF16), ALL, scatter_dimension=0, tiled=True).astype(
                F32
            )
        return over_shards(rows.astype(BF16).reshape(n_shard, -1, rows.shape[1]))

    def over_shards(rows):
        return jnp.sum(trade(rows, "shard").astype(F32), axis=0)

    expert_count = w_router.shape[1]
    top_count = routes.shape[1]
    route_hot = jnp.any(
        routes[:, :, None] == jnp.arange(expert_count, dtype=jnp.int32)[None, None, :], axis=1
    )
    pos_p = jnp.arange(GROUP_TOK, dtype=jnp.int32)
    pos_p = jnp.where(pos_p < PROMPT, pos_p, PROMPT + pos_p % BLOCK)
    cos_p, sin_p = angles(pos_p, ROPE)
    tok_all = lax.all_gather(tokens, ROW, axis=0, tiled=True)
    hit_b = trade(route_hot.T.astype(F32), ROW) > 0.5
    cotangent_late, cos_p, sin_p, hit_b = lax.optimization_barrier(
        (cotangent, cos_p, sin_p, hit_b)
    )
    c_all = lax.all_gather(cotangent_late, ROW, axis=0, tiled=True)
    units = w_shared_gate.shape[1] // n_row
    wq_h = head_columns(w_query, QDIM)
    wkv_h = head_columns(w_keyval, KVDIM)
    w_lr = gather_rows(jnp.concatenate([w_latent, w_router], axis=1))
    w_l, w_r = w_lr[:, : LATENT + ROPE], w_lr[:, LATENT + ROPE :]
    w_joint = jnp.concatenate([wq_h[:, :NOPE], w_l[:, :LATENT], wq_h[:, NOPE:], w_l[:, LATENT:]], 1)
    w_o_near = w_output
    if paired:
        w_o_near = pair_gather(spread(sub_rows(w_output)), "expert", 4, 2, x_at)
    gu_parts = jnp.concatenate([unit_columns(w_shared_gate), unit_columns(w_shared_up)], axis=-1)
    w_joint, wkv_h, tok_all, w_o_near, gu_parts = lax.optimization_barrier(
        (w_joint, wkv_h, tok_all, w_o_near, gu_parts)
    )
    w_gu = trade(gu_parts, "shard").reshape(width, 2 * units)
    if paired:
        w_o_near = pair_gather(w_o_near, "group", 2, 1, group_at)

    capacity = 3 * tok_rows * top_count // (2 * expert_count)
    ahead = capacity * (jnp.arange(n_row, dtype=jnp.int32)[:, None] % 2)
    place = jnp.where(hit_b, places_of(hit_b) + ahead, 1 << 20).reshape(-1, 1, 2 * tok_rows)

    hidden1, query, key, value, comp = project(
        tok_all.reshape(n_row, BLOCK, width),
        my_blocks,
        gain_attn,
        w_joint,
        gain_latent,
        wkv_h,
        cos_p,
        sin_p,
    )
    mixed_f, mixed_h, total_h = attend(query, key, value)
    mixed_h, w_o_near, w_gu = lax.optimization_barrier((mixed_h, w_o_near, w_gu))
    mixed = heads_home(mixed_h)
    if paired:
        w_o = pair_gather(w_o_near, "expert", 4, 1, core_at)
        w_o = jnp.transpose(w_o, (3, 1, 2, 0, 4, 5)).reshape(width, -1)
    else:
        w_o = gather_rows_at_once(w_o_near)
    padded = -(-(units + expert_count) // 128) * 128
    space = lambda cols: jnp.zeros((width, cols), BF16)
    w_sh = jnp.concatenate(
        [
            w_gu[:, :units],
            w_r,
            space(padded - units - expert_count),
            w_gu[:, units:],
            space(padded - units),
        ],
        axis=1,
    )
    w_sd = lax.dynamic_slice_in_dim(w_shared_down, expert_at * units, units)
    w_sd = jnp.pad(w_sd, ((0, padded - units), (0, 0)))

    inputs = tokens.astype(F32)
    grad_out = cotangent.astype(F32)
    normed1, inverse1 = rms_parts(inputs)
    hidden1_own = (normed1 * gain_attn).astype(BF16)
    latent_own = matmul(hidden1_own, w_l)
    normed_c, inverse_c = rms_parts(latent_own[:, :LATENT])
    after = inputs + matmul(mixed, w_o)
    normed2, inverse2 = rms_parts(after)
    hidden2 = (normed2 * gain_ffn).astype(BF16)
    logits = matmul(hidden2, w_r)
    router_prob = jax.nn.softmax(logits, axis=-1)

    hidden2, c_all, w_sh = lax.optimization_barrier((hidden2, c_all, w_sh))
    h2_all = lax.all_gather(hidden2, ROW, axis=0, tiled=True)
    c_kept = cotangent_rows(place, capacity, c_all, expert_down[0], w_sd)
    h2_all, w_query, c_kept = lax.optimization_barrier((h2_all, w_query, c_kept))
    w_q = gather_rows_at_once(w_query)
    out_a, out_b, dh_parts, d_prob_col, rows, d_out, e_mid, d_gate, d_up, s_mid, ds_gu = experts(
        row_at[None],
        place,
        capacity,
        h2_all,
        c_kept,
        expert_gate[0],
        expert_up[0],
        expert_down[0],
        w_sh,
        w_sd,
        units,
        expert_count,
        [width - SIDE, SIDE] if paired else [width],
    )
    d_prob = trade(d_prob_col.reshape(n_row, tok_rows), ROW).T
    dh_parts, w_q = lax.optimization_barrier((dh_parts, w_q))
    d_h2 = lax.psum_scatter(dh_parts[0], ROW, scatter_dimension=0, tiled=True).astype(F32)
    if paired:
        d_h2 = jnp.concatenate([d_h2, scatter_rows_of_row(dh_parts[1])], axis=1)
    d_prob = jnp.where(route_hot, d_prob, 0.0)
    d_logits = (
        router_prob * (d_prob - jnp.sum(router_prob * d_prob, axis=-1, keepdims=True))
    ).astype(BF16)
    grad_router = matmul_tn(hidden2, d_logits)

    def share(whole):
        if n_group != 2:
            return lax.psum_scatter(
                whole.astype(BF16), "group", scatter_dimension=0, tiled=True
            ), None
        half = whole.shape[0] // 2
        send = lax.dynamic_slice_in_dim(whole, (1 - group_at) * half, half).astype(BF16)
        keep = lax.dynamic_slice_in_dim(whole, group_at * half, half)
        return lax.ppermute(send, "group", [(0, 1), (1, 0)]), keep

    whole_0 = matmul_tn(rows, d_gate)
    d_up, ds_gu, whole_0 = lax.optimization_barrier((d_up, ds_gu, whole_0))
    got_0, keep_0 = share(whole_0)
    whole_1 = matmul_tn(rows, d_up)
    grad_gu = matmul_tn(h2_all, ds_gu).astype(BF16)
    e_mid, s_mid, whole_1, got_0, grad_gu = lax.optimization_barrier(
        (e_mid, s_mid, whole_1, got_0, grad_gu)
    )
    got_1, keep_1 = share(whole_1)
    whole_2 = matmul_tn(e_mid, d_out)
    grad_sd_part = matmul_tn(s_mid, c_all)[:units].astype(BF16)
    d_h2, whole_2, grad_sd_part = lax.optimization_barrier((d_h2, whole_2, grad_sd_part))
    whole_2, _ = lax.optimization_barrier((whole_2, got_1))
    got_2, keep_2 = share(whole_2)
    grad_gu = jnp.concatenate(
        [grad_gu[:, :units], grad_gu[:, padded : padded + units]], axis=1
    ).reshape(n_all, width // n_all, 2 * units)
    grad_sd_part = grad_sd_part.reshape(n_group, units // n_group, width)
    d_h2, out_a, out_b, grad_gu, grad_sd_part, grad_router, d_logits = lax.optimization_barrier(
        (d_h2, out_a, out_b, grad_gu, grad_sd_part, grad_router, d_logits)
    )
    ffn_a = lax.psum_scatter(out_a, ROW, scatter_dimension=0, tiled=True)

    d_hidden2 = d_h2 + matmul_nt(d_logits, w_r)
    d_after, grad_gain_ffn = norm_back(d_hidden2, normed2, inverse2, gain_ffn)
    grad_after = grad_out + d_after
    grad_attn = grad_after.astype(BF16)
    d_mixed = matmul_nt(grad_attn, w_o).astype(BF16)
    d_mixed_h = heads_out(d_mixed)
    wo_rows = scatter_start(mixed, grad_attn)
    d_mixed_h, grad_gu, grad_sd_part, got_1, wo_rows = lax.optimization_barrier(
        (d_mixed_h, grad_gu, grad_sd_part, got_1, wo_rows)
    )
    wo_rows = scatter_y(wo_rows)
    gu_got = trade(grad_gu, ALL)
    sd_gots = []
    for turn in range(n_group):
        piece_at = (group_at + turn) % n_group
        moves = []
        for g in range(n_group):
            for e in range(n_expert):
                for s in range(n_shard):
                    target = (s * n_expert + e) * n_group + (g + turn) % n_group
                    moves.append(((g * n_expert + e) * n_shard + s, target))
        sent = lax.dynamic_index_in_dim(grad_sd_part, piece_at, axis=0, keepdims=False)
        sd_gots.append(lax.ppermute(sent, ALL, moves))

    d_query, d_key, d_value = attend_back(
        query, key, value, mixed_f, total_h, d_mixed_h, cos_p, sin_p
    )
    d_keyval, d_latent_part = latent_back(d_key, d_value, wkv_h, local_slot, mine)
    own_pos = lax.dynamic_slice_in_dim(positions, row_at * tok_rows, tok_rows)
    cosine, sine = angles(own_pos, ROPE)
    d_latent_part, ffn_a, gu_got, sd_gots, wo_rows, cosine, sine = lax.optimization_barrier(
        (d_latent_part, ffn_a, gu_got, sd_gots, wo_rows, cosine, sine)
    )
    d_lat = lax.psum_scatter(d_latent_part, ROW, scatter_dimension=0, tiled=True)
    d_query_own = heads_home(d_query)
    grad_wq_h = matmul_tn(hidden1, d_query).astype(BF16).reshape(n_all, width // n_all, QDIM)
    grad_wkv_h = matmul_tn(comp, d_keyval).astype(BF16)
    grad_wkv_h = grad_wkv_h.reshape(n_all, width // n_all, -1)
    head_got = trade(jnp.concatenate([grad_wq_h, grad_wkv_h], axis=-1), ALL)
    wo_rows = scatter_x(wo_rows)
    egrads = [
        (got.astype(F32) if keep is None else keep + got.astype(F32))[None]
        for got, keep in ((got_0, keep_0), (got_1, keep_1), (got_2, keep_2))
    ]
    d_lat, d_query_own, wo_rows, egrads, out_b, head_got = lax.optimization_barrier(
        (d_lat, d_query_own, wo_rows, egrads, out_b, head_got)
    )
    egrad_gate, egrad_up, egrad_down = egrads
    d_lat = d_lat.astype(F32)
    ffn_b = lax.psum_scatter(out_b, ROW, scatter_dimension=0, tiled=True)
    grad_wo = scatter_end(wo_rows)
    output = (after + jnp.concatenate([ffn_a, ffn_b], axis=1).astype(F32)).astype(BF16)
    got = gu_got.astype(F32)
    got = jnp.sum(got.reshape(n_group, n_expert, n_shard, -1, 2 * units), axis=0)
    got = jnp.transpose(got, (2, 1, 0, 3))
    grad_sg = got[..., :units].reshape(got.shape[0], -1)
    grad_su = got[..., units:].reshape(got.shape[0], -1)
    grad_sd = sum(got.astype(F32) for got in sd_gots)

    got = head_got.astype(F32)
    got = jnp.sum(got.reshape(n_group * n_prompt, HEADS, got.shape[1], got.shape[2]), axis=0)
    grad_wq = jnp.swapaxes(got[..., :QDIM], 0, 1).reshape(got.shape[1], -1)
    grad_wkv = jnp.swapaxes(
        got[..., QDIM:].reshape(HEADS, LATENT // n_all, KVDIM), 0, 1
    ).reshape(LATENT // n_all, -1)

    d_lat_c, grad_gain_latent = norm_back(d_lat[:, :LATENT], normed_c, inverse_c, gain_latent)
    d_latent = jnp.concatenate([d_lat_c, unrotate(d_lat[:, LATENT:], cosine, sine)], axis=1).astype(
        BF16
    )
    d_hidden1 = matmul_nt(d_query_own, w_q) + matmul_nt(d_latent, w_l)
    d_tok, grad_gain_attn = norm_back(d_hidden1, normed1, inverse1, gain_attn)
    grad_tokens = grad_after + d_tok
    own = width // n_all
    lat = LATENT // n_all
    gain_l = jnp.pad(grad_gain_latent.reshape(n_all, lat), ((0, 0), (0, own - lat)))
    beside = jnp.concatenate(
        [
            grad_router,
            grad_gain_attn[:, None],
            grad_gain_ffn[:, None],
            gain_l.reshape(width, 1),
        ],
        axis=1,
    )
    beside = jnp.pad(beside, ((0, 0), (0, -(LATENT + ROPE + expert_count + 3) % 128)))
    sums = scatter_end(scatter_x(scatter_y(scatter_start(hidden1_own, d_latent, beside))))
    grad_wl = sums[:, : LATENT + ROPE]
    at = LATENT + ROPE + expert_count
    grad_r, grad_ga, grad_gf, grad_gl = (
        sums[:, LATENT + ROPE : at],
        sums[:, at],
        sums[:, at + 1],
        sums[:lat, at + 2],
    )
    return (
        output,
        grad_tokens,
        grad_ga,
        grad_wq,
        grad_wl,
        grad_gl,
        grad_wkv,
        grad_wo,
        grad_gf,
        grad_sg,
        grad_su,
        grad_sd,
        grad_r,
        egrad_gate,
        egrad_up,
        egrad_down,
    )


def solution(mesh):
    sizes = tuple(mesh.shape[name] for name in ALL)
    return jax.shard_map(
        functools.partial(per_device, sizes),
        mesh=mesh,
        in_specs=(
            P(ALL, None),
            P(ALL, None),
            P(),
            P("shard", None),
            P("shard", None),
            P(),
            P("shard", None),
            P("shard", None),
            P(),
            P("shard", None),
            P("shard", None),
            P("shard", None),
            P("shard", None),
            P(ROW, None, None),
            P(ROW, None, None),
            P(ROW, None, None),
            P("group"),
            P("group"),
            P(ALL, None),
        ),
        out_specs=(
            P(ALL, None),
            P(ALL, None),
            P(ALL),
            P(ALL, None),
            P(ALL, None),
            P(ALL),
            P(ALL, None),
            P(ALL, None),
            P(ALL),
            P(ALL, None),
            P(ALL, None),
            P(ALL, None),
            P(ALL, None),
            P(ROW, "group", None),
            P(ROW, "group", None),
            P(ROW, "group", None),
        ),
        check_vma=False,
    )
```

```python
import functools
import math

import jax
import jax.numpy as jnp
from jax import lax
from jax.experimental import pallas as pl
from jax.experimental.pallas import tpu as pltpu
from jax.sharding import PartitionSpec as P

HEADS = 16
NOPE = 128
ROPE = 64
VDIM = 128
LATENT = 512
BLOCK = 256
PROMPT = 2048
NCONT = 8
QDIM = NOPE + ROPE
KVDIM = NOPE + VDIM
GROUP_BLOCKS = PROMPT // BLOCK + NCONT
GROUP_TOK = GROUP_BLOCKS * BLOCK
SIDE = 512

EPS = 1e-06
ALL = ("group", "expert", "shard")
ROW = ("expert", "shard")
SCALE = 1.0 / math.sqrt(NOPE + ROPE)
F32 = jnp.float32
BF16 = jnp.bfloat16


def matmul(left, right):
    return jnp.dot(left, right, preferred_element_type=F32)


def matmul_nt(left, right):
    return lax.dot_general(left, right, (((1,), (1,)), ((), ())), preferred_element_type=F32)


def matmul_tn(left, right):
    return lax.dot_general(left, right, (((0,), (0,)), ((), ())), preferred_element_type=F32)


def rms_parts(values):
    inverse = lax.rsqrt(jnp.mean(values * values, axis=-1, keepdims=True) + EPS)
    return (values * inverse, inverse)


def norm_back(grad_in, normed, inverse, gain):
    scaled = grad_in * gain
    gain_grad = jnp.sum(grad_in * normed, axis=0)
    input_grad = inverse * (scaled - normed * jnp.mean(scaled * normed, axis=-1, keepdims=True))
    return (input_grad, gain_grad)


def angles(pos_list, rot_width):
    half_width = rot_width // 2
    freq = 10000.0 ** (-2.0 * jnp.arange(half_width, dtype=F32) / rot_width)
    theta = pos_list.astype(F32)[:, None] * freq[None, :]
    return (jnp.cos(theta), jnp.sin(theta))


def rotate(values, cosine, sine):
    half_width = values.shape[-1] // 2
    first_half = values[..., :half_width]
    second_half = values[..., half_width:]
    return jnp.concatenate(
        [first_half * cosine - second_half * sine, second_half * cosine + first_half * sine],
        axis=-1,
    )


def unrotate(grad_in, cosine, sine):
    return rotate(grad_in, cosine, -sine)


def silu_parts(values):
    sigmoid = jax.nn.sigmoid(values)
    return (values * sigmoid, sigmoid * (1.0 + values * (1.0 - sigmoid)))


def trade(buffer, axes):
    return lax.all_to_all(buffer, axes, split_axis=0, concat_axis=0, tiled=True)


TILE = 2 * BLOCK
TILES = GROUP_TOK // TILE
PROMPT_TILES = PROMPT // TILE
NEG = -1e30


def dot(left, right, left_dim, right_dim):
    return lax.dot_general(
        left, right, (((left_dim,), (right_dim,)), ((), ())), preferred_element_type=F32
    )


def take_blocks(blocks, index):
    count = index.shape[0]
    shape = blocks.shape[1:]
    unroll = 8 if shape[-1] <= 256 else 4

    def body(index_ref, *refs):
        for i in range(unroll):
            refs[-1][i] = refs[i][0]

    return pl.pallas_call(
        body,
        grid_spec=pltpu.PrefetchScalarGridSpec(
            num_scalar_prefetch=1,
            grid=(count // unroll,),
            in_specs=[
                pl.BlockSpec((1,) + shape, lambda i, at, k=k: (at[i * unroll + k], 0, 0))
                for k in range(unroll)
            ],
            out_specs=pl.BlockSpec((unroll,) + shape, lambda i, at: (i, 0, 0)),
        ),
        out_shape=jax.ShapeDtypeStruct((count,) + shape, blocks.dtype),
        compiler_params=pltpu.CompilerParams(vmem_limit_bytes=40 << 20),
        cost_estimate=pl.CostEstimate(
            flops=0, bytes_accessed=4 * count * shape[0] * shape[1], transcendentals=0
        ),
        name="take_blocks",
    )(index, *([blocks] * unroll))


def project_body(
    at_ref, tok_a, tok_b, gain_ref, w_ref, gain_l_ref, wkv_ref, cos_ref, sin_ref,
    hid_ref, q_ref, k_ref, v_ref, comp_ref,
):
    gain = gain_ref[...]
    gain_l = gain_l_ref[...]
    for part, tok in enumerate((tok_a, tok_b)):
        rows = slice(part * BLOCK, (part + 1) * BLOCK)
        hidden = (rms_parts(tok[0].astype(F32))[0] * gain).astype(BF16)
        hid_ref[rows, :] = hidden
        joint = dot(hidden, w_ref[...], 1, 0)
        cosine, sine = cos_ref[rows, :], sin_ref[rows, :]
        at = NOPE + LATENT
        q_ref[rows, :NOPE] = joint[:, :NOPE].astype(BF16)
        q_ref[rows, NOPE:] = rotate(joint[:, at : at + ROPE], cosine, sine).astype(BF16)
        comp = (rms_parts(joint[:, NOPE:at])[0] * gain_l).astype(BF16)
        comp_ref[rows, :] = comp
        keyval = dot(comp, wkv_ref[...], 1, 0).astype(BF16)
        k_ref[rows, :NOPE] = keyval[:, :NOPE]
        k_ref[rows, NOPE:] = rotate(joint[:, at + ROPE :], cosine, sine).astype(BF16)
        v_ref[rows, :] = keyval[:, NOPE:]


def project(blocks, index, gain, weights, gain_l, wkv, cosine, sine):
    width = blocks.shape[-1]
    whole = lambda a: pl.BlockSpec(a.shape, lambda i, at: (0, 0))
    tiled = lambda cols: pl.BlockSpec((TILE, cols), lambda i, at: (i, 0))
    piece = lambda k: pl.BlockSpec((1, BLOCK, width), lambda i, at: (at[2 * i + k], 0, 0))
    widths = (width, QDIM, QDIM, VDIM, LATENT)
    gain, gain_l = gain.reshape(1, -1), gain_l.reshape(1, -1)
    return pl.pallas_call(
        project_body,
        grid_spec=pltpu.PrefetchScalarGridSpec(
            num_scalar_prefetch=1,
            grid=(TILES,),
            in_specs=[
                piece(0), piece(1), whole(gain), whole(weights), whole(gain_l), whole(wkv),
                tiled(ROPE // 2), tiled(ROPE // 2),
            ],
            out_specs=[tiled(cols) for cols in widths],
        ),
        out_shape=[jax.ShapeDtypeStruct((GROUP_TOK, cols), BF16) for cols in widths],
        compiler_params=pltpu.CompilerParams(vmem_limit_bytes=48 << 20),
        cost_estimate=pl.CostEstimate(
            flops=14_000_000_000, bytes_accessed=48_000_000, transcendentals=0
        ),
        name="project",
    )(index, blocks, blocks, gain, weights, gain_l, wkv, cosine, sine)


def own_mask(tile):
    k_at = lax.broadcasted_iota(jnp.int32, (TILE, TILE), 0)
    q_at = lax.broadcasted_iota(jnp.int32, (TILE, TILE), 1)
    piece = jnp.where(tile < PROMPT_TILES, TILE, BLOCK)
    lowest = jnp.where(q_at >= piece, piece, 0)
    return (k_at <= q_at) & (k_at >= lowest)


def attend_body(q_ref, k_ref, v_ref, o_ref, ob_ref, lse_ref, s_ref):
    tile = pl.program_id(0)
    q = q_ref[...]
    others = jnp.minimum(tile, PROMPT_TILES)

    def rows_of(at):
        return pl.ds(pl.multiple_of(at * TILE, TILE), TILE)

    def fold(values, op):
        return op(values.reshape(TILE // 8, 8, TILE), axis=0)

    own = jnp.where(own_mask(tile), dot(k_ref[rows_of(tile), :], q, 1, 1) * SCALE, NEG)
    s_ref[rows_of(PROMPT_TILES), :] = own

    def raw(at, top):
        s = dot(k_ref[rows_of(at), :], q, 1, 1) * SCALE
        s_ref[rows_of(at), :] = s
        return jnp.maximum(top, fold(s, jnp.max))

    top = lax.fori_loop(0, others, raw, fold(own, jnp.max))
    top = jnp.max(top, axis=0, keepdims=True)

    def mix(s_at, v_at, carry):
        total, out = carry
        p = jnp.exp(s_ref[rows_of(s_at), :] - top)
        return total + fold(p, jnp.sum), out + dot(p.astype(BF16), v_ref[rows_of(v_at), :], 0, 0)

    carry = (jnp.zeros((8, TILE), F32), jnp.zeros((TILE, VDIM), F32))
    carry = mix(PROMPT_TILES, tile, carry)
    total, out = lax.fori_loop(0, others, lambda at, c: mix(at, at, c), carry)
    total = jnp.sum(total, axis=0, keepdims=True)
    lse_ref[...] = top + jnp.log(total)
    scale = jnp.transpose(jnp.broadcast_to(1.0 / total, (VDIM, TILE)))
    out = out * scale
    o_ref[...] = out
    ob_ref[...] = out.astype(BF16)


def attend(query, key, value):
    whole = lambda cols: pl.BlockSpec((GROUP_TOK, cols), lambda i: (0, 0))
    tiled = lambda cols: pl.BlockSpec((TILE, cols), lambda i: (i, 0))
    return pl.pallas_call(
        attend_body,
        grid=(TILES,),
        in_specs=[tiled(QDIM), whole(QDIM), whole(VDIM)],
        out_specs=[tiled(VDIM), tiled(VDIM), pl.BlockSpec((1, TILE), lambda i: (0, i))],
        out_shape=[
            jax.ShapeDtypeStruct((GROUP_TOK, VDIM), F32),
            jax.ShapeDtypeStruct((GROUP_TOK, VDIM), BF16),
            jax.ShapeDtypeStruct((1, GROUP_TOK), F32),
        ],
        scratch_shapes=[pltpu.VMEM((PROMPT + TILE, TILE), F32)],
        compiler_params=pltpu.CompilerParams(vmem_limit_bytes=40 << 20),
        cost_estimate=pl.CostEstimate(
            flops=6_000_000_000, bytes_accessed=10_000_000, transcendentals=8_000_000
        ),
        name="attend",
    )(query, key, value)


def attend_back_body(
    q_ref, k_ref, v_ref, g_ref, o_ref, lse_ref, cos_ref, sin_ref, dq_ref, dk_ref, dv_ref, acc_ref
):
    tile = pl.program_id(0)

    @pl.when(tile == 0)
    def _():
        dk_ref[...] = jnp.zeros_like(dk_ref)
        dv_ref[...] = jnp.zeros_like(dv_ref)

    q = q_ref[...]
    g = g_ref[...]
    lse = lse_ref[...]
    delta = jnp.sum(jnp.transpose(g.astype(F32) * o_ref[...]), axis=0, keepdims=True)

    def step(at, mask):
        rows = pl.ds(pl.multiple_of(at * TILE, TILE), TILE)
        k = k_ref[rows, :]
        p = jnp.exp(dot(k, q, 1, 1) * SCALE - lse)
        if mask is not None:
            p = jnp.where(mask, p, 0.0)
        ds = (p * (dot(v_ref[rows, :], g, 1, 1) - delta)).astype(BF16)
        dv_ref[rows, :] += dot(p.astype(BF16), g, 1, 0)
        dk_ref[rows, :] += dot(ds, q, 1, 0) * SCALE
        return dot(ds, k, 0, 0)

    acc_ref[...] = step(tile, own_mask(tile))

    @pl.loop(0, jnp.minimum(tile, PROMPT_TILES))
    def _(at):
        acc_ref[...] += step(at, None)

    dq = acc_ref[...] * SCALE
    dq_ref[:, :NOPE] = dq[:, :NOPE].astype(BF16)
    dq_ref[:, NOPE:] = rotate(dq[:, NOPE:], cos_ref[...], -sin_ref[...]).astype(BF16)


def attend_back(query, key, value, mixed, lse, grad, cosine, sine):
    whole = lambda cols: pl.BlockSpec((GROUP_TOK, cols), lambda i: (0, 0))
    tiled = lambda cols: pl.BlockSpec((TILE, cols), lambda i: (i, 0))
    return pl.pallas_call(
        attend_back_body,
        grid=(TILES,),
        in_specs=[
            tiled(QDIM), whole(QDIM), whole(VDIM), tiled(VDIM), tiled(VDIM),
            pl.BlockSpec((1, TILE), lambda i: (0, i)), tiled(ROPE // 2), tiled(ROPE // 2),
        ],
        out_specs=[tiled(QDIM), whole(QDIM), whole(VDIM)],
        out_shape=[
            jax.ShapeDtypeStruct((GROUP_TOK, QDIM), BF16),
            jax.ShapeDtypeStruct((GROUP_TOK, QDIM), F32),
            jax.ShapeDtypeStruct((GROUP_TOK, VDIM), F32),
        ],
        scratch_shapes=[pltpu.VMEM((TILE, QDIM), F32)],
        compiler_params=pltpu.CompilerParams(vmem_limit_bytes=48 << 20),
        cost_estimate=pl.CostEstimate(
            flops=16_000_000_000, bytes_accessed=20_000_000, transcendentals=8_000_000
        ),
        name="attend_back",
    )(query, key, value, grad, mixed, lse, cosine, sine)


def latent_back_body(slot_ref, mine_ref, dk_ref, dv_ref, w_ref, dkv_ref, lat_ref):
    kv = jnp.concatenate([dk_ref[:, :NOPE], dv_ref[...]], axis=1).astype(BF16)
    dkv_ref[...] = kv
    keep = mine_ref[pl.program_id(0)] != 0
    comp = jnp.where(keep, dot(kv, w_ref[...], 1, 1), 0.0)
    lat_ref[:, :LATENT] = comp.astype(BF16)
    lat_ref[:, LATENT:] = jnp.where(keep, dk_ref[:, NOPE:], 0.0).astype(BF16)


def latent_back(d_key, d_value, wkv, slot, mine):
    count = slot.shape[0]
    tiled = lambda cols: pl.BlockSpec((BLOCK, cols), lambda i, at, m: (at[i], 0))
    return pl.pallas_call(
        latent_back_body,
        grid_spec=pltpu.PrefetchScalarGridSpec(
            num_scalar_prefetch=2,
            grid=(count,),
            in_specs=[
                tiled(QDIM), tiled(VDIM), pl.BlockSpec(wkv.shape, lambda i, at, m: (0, 0)),
            ],
            out_specs=[
                tiled(KVDIM), pl.BlockSpec((BLOCK, LATENT + ROPE), lambda i, at, m: (i, 0)),
            ],
        ),
        out_shape=[
            jax.ShapeDtypeStruct((GROUP_TOK, KVDIM), BF16),
            jax.ShapeDtypeStruct((count * BLOCK, LATENT + ROPE), BF16),
        ],
        cost_estimate=pl.CostEstimate(
            flops=1_100_000_000, bytes_accessed=14_000_000, transcendentals=0
        ),
        name="latent_back",
    )(slot, mine.astype(jnp.int32), d_key, d_value, wkv)

def line_gather(part, axis, count):
    up = [(i, i + 1) for i in range(count - 1)]
    down = [(i + 1, i) for i in range(count - 1)]
    right, left = [part], [part]
    for _ in range(count - 1):
        right.append(lax.ppermute(right[-1], axis, up))
        left.append(lax.ppermute(left[-1], axis, down))
    line = jnp.stack(right[:0:-1] + left)
    return lax.dynamic_slice_in_dim(line, count - 1 - lax.axis_index(axis), count)


def pair_gather(part, axis, count, flip, bit):
    other = lax.ppermute(part, axis, [(i, i ^ flip) for i in range(count)])
    return lax.dynamic_slice_in_dim(jnp.stack([part, other, part]), bit, 2)


def chunks_of(total, size):
    return [slice(at, min(at + size, total)) for at in range(0, total, size)]


def experts_body(
    groups, units, count, n_parts, me_ref, place_ref, h_ref, crow_ref, dmid_ref, dsmid_ref, wg_hbm,
    wu_hbm, wd_hbm, ws_hbm, wsd_hbm, outa_ref, outb_ref, *refs,
):
    dh_refs = refs[:n_parts]
    dprob_ref, rows_ref, dout_ref, mid_ref, dg_ref, du_ref, smid_ref, ds_ref = refs[
        n_parts : n_parts + 8
    ]
    wg_ref, wu_ref, wd_ref, ws_ref, wsd_ref, sems = refs[n_parts + 8 :]
    copies = [
        pltpu.make_async_copy(source, target, sems.at[at])
        for at, (source, target) in enumerate(
            (
                (ws_hbm, ws_ref), (wg_hbm, wg_ref), (wu_hbm, wu_ref), (wd_hbm, wd_ref),
                (wsd_hbm, wsd_ref),
            )
        )
    ]
    opening = pl.program_id(0) == 0

    @pl.when(opening)
    def _():
        for copy in copies:
            copy.start()
        copies[0].wait()

    width, hidden = wg_ref.shape
    padded = wsd_ref.shape[0]
    h = h_ref[...]
    ends = [0]
    for ref in dh_refs:
        ends.append(ends[-1] + ref.shape[1])

    wide = dot(h, ws_ref[...], 1, 0)
    s_gate, s_up = wide[:, :padded], wide[:, padded:]
    first = units - (padded - 128)
    logits = jnp.transpose(s_gate[:, padded - 128 :])[first : first + count, :]
    powers = jnp.exp(logits - jnp.max(logits, axis=0, keepdims=True))
    mine = lax.broadcasted_iota(jnp.int32, powers.shape, 0) == me_ref[0]
    weight = jnp.sum(jnp.where(mine, powers, 0.0), axis=0, keepdims=True) / jnp.sum(
        powers, axis=0, keepdims=True
    )
    s_act, s_slope = silu_parts(s_gate)
    smid_ref[...] = (s_act * s_up).astype(BF16)
    ds_mid = dsmid_ref[...]
    ds_ref[:, :padded] = (ds_mid * s_up * s_slope).astype(BF16)
    ds_ref[:, padded:] = (ds_mid * s_act).astype(BF16)

    picks, weights = [], []
    for rows, toks in groups:
        shape = (rows.stop - rows.start, toks.stop - toks.start)
        here = lax.broadcasted_iota(jnp.int32, shape, 0) + rows.start == place_ref[0, :, toks]
        pick = jnp.where(here, 1.0, 0.0).astype(BF16)
        scale = jnp.sum(jnp.where(here, weight[:, toks], 0.0), axis=1, keepdims=True)
        for cols in chunks_of(width, 512):
            rows_ref[rows, cols] = dot(pick, h[toks, cols], 1, 0).astype(BF16)
            dout_ref[rows, cols] = (scale * crow_ref[rows, cols].astype(F32)).astype(BF16)
        picks.append((rows, toks, here, pick))
        weights.append(scale)
    scale = jnp.concatenate(weights, axis=0) if len(weights) > 1 else weights[0]

    @pl.when(opening)
    def _():
        copies[1].wait()
        copies[2].wait()

    for cols in chunks_of(hidden, 512):
        gate = dot(rows_ref[...], wg_ref[:, cols], 1, 0)
        up = dot(rows_ref[...], wu_ref[:, cols], 1, 0)
        act, slope = silu_parts(gate)
        mid_ref[:, cols] = (act * up).astype(BF16)
        d_mid = scale * dmid_ref[:, cols]
        dg_ref[:, cols] = (d_mid * up * slope).astype(BF16)
        du_ref[:, cols] = (d_mid * act).astype(BF16)

    @pl.when(opening)
    def _():
        copies[3].wait()
        copies[4].wait()

    d_prob = jnp.zeros(scale.shape, F32)
    for cols in chunks_of(width, 512):
        out = dot(mid_ref[...], wd_ref[:, cols], 1, 0).astype(BF16).astype(F32)
        d_prob = d_prob + jnp.sum(out * crow_ref[:, cols].astype(F32), axis=1, keepdims=True)
        out = (out * scale).astype(BF16)
        d_rows = dot(dg_ref[...], wg_ref[cols, :], 1, 1) + dot(du_ref[...], wu_ref[cols, :], 1, 1)
        d_rows = d_rows.astype(BF16)
        for rows, toks, here, pick in picks:
            shared = dot(smid_ref[toks, :], wsd_ref[:, cols], 1, 0)
            half_ref, at = (outa_ref, 0) if cols.start < width // 2 else (outb_ref, width // 2)
            half_ref[toks, cols.start - at : cols.stop - at] = (
                dot(pick, out[rows, :], 0, 0) + shared
            ).astype(BF16)
            shared = dot(ds_ref[toks, :], ws_ref[cols, :], 1, 1)
            for ref, start, stop in zip(dh_refs, ends, ends[1:]):
                if start <= cols.start < stop:
                    ref[toks, cols.start - start : cols.stop - start] = (
                        dot(pick, d_rows[rows, :], 0, 0) + shared
                    ).astype(BF16)
    for rows, toks, here, pick in picks:
        dprob_ref[0, :, toks] = jnp.sum(
            jnp.where(here, d_prob[rows, :], 0.0), axis=0, keepdims=True
        )


def groups_of(capacity, blocks):
    if capacity % 16 == 0:
        return [
            (slice(b * capacity, (b + 1) * capacity), slice(b * BLOCK, (b + 1) * BLOCK))
            for b in range(blocks)
        ]
    return [(slice(0, blocks * capacity), slice(0, blocks * BLOCK))]


def cotangent_body(groups, place_ref, c_ref, wd_ref, wsd_ref, crow_ref, dmid_ref, dsmid_ref):
    dsmid_ref[...] = dot(c_ref[...], wsd_ref[...], 1, 1)
    for rows, toks in groups:
        shape = (rows.stop - rows.start, toks.stop - toks.start)
        here = lax.broadcasted_iota(jnp.int32, shape, 0) + rows.start == place_ref[0, :, toks]
        pick = jnp.where(here, 1.0, 0.0).astype(BF16)
        for cols in chunks_of(c_ref.shape[1], 512):
            crow_ref[rows, cols] = dot(pick, c_ref[toks, cols], 1, 0).astype(BF16)
    for cols in chunks_of(wd_ref.shape[0], 512):
        dmid_ref[:, cols] = dot(crow_ref[...], wd_ref[cols, :], 1, 1)


def cotangent_rows(place, capacity, cotangent, w_down, w_sdown):
    tokens, width = cotangent.shape
    hidden, padded = w_down.shape[0], w_sdown.shape[0]
    step, room, steps = 2 * BLOCK, 2 * capacity, tokens // (2 * BLOCK)
    once = lambda a: pl.BlockSpec(a.shape, lambda i: (0, 0), pipeline_mode=pl.Buffered(1))
    tiled = lambda rows, cols: pl.BlockSpec((rows, cols), lambda i: (i, 0))
    return pl.pallas_call(
        functools.partial(cotangent_body, groups_of(capacity, 2)),
        grid=(steps,),
        in_specs=[
            pl.BlockSpec((1, 1, step), lambda i: (i, 0, 0)), tiled(step, width), once(w_down),
            once(w_sdown),
        ],
        out_specs=[tiled(room, width), tiled(room, hidden), tiled(step, padded)],
        out_shape=[
            jax.ShapeDtypeStruct((steps * room, width), BF16),
            jax.ShapeDtypeStruct((steps * room, hidden), F32),
            jax.ShapeDtypeStruct((tokens, padded), F32),
        ],
        compiler_params=pltpu.CompilerParams(vmem_limit_bytes=40 << 20),
        cost_estimate=pl.CostEstimate(
            flops=2 * steps * width * (room * hidden + step * padded + room * step),
            bytes_accessed=55_000_000,
            transcendentals=0,
        ),
        name="cotangent_rows",
    )(place, cotangent, w_down, w_sdown)


def experts(
    me, place, capacity, hidden2, c_kept, w_gate, w_up, w_down, w_shared, w_sdown, units, count,
    widths,
):
    width, hidden = w_gate.shape
    tokens = hidden2.shape[0]
    n_parts = len(widths)
    padded = w_sdown.shape[0]
    blocks = 2
    step = blocks * BLOCK
    steps = tokens // step
    room = blocks * capacity
    groups = groups_of(capacity, blocks)
    tiled = lambda rows, cols: pl.BlockSpec((rows, cols), lambda i, me: (i, 0))
    line = pl.BlockSpec((1, 1, step), lambda i, me: (i, 0, 0))
    shape = lambda rows, cols, kind=BF16: jax.ShapeDtypeStruct((rows, cols), kind)
    flops = 2 * steps * (5 * room * width * hidden + 5 * step * width * padded)
    outs = pl.pallas_call(
        functools.partial(experts_body, groups, units, count, n_parts),
        grid_spec=pltpu.PrefetchScalarGridSpec(
            num_scalar_prefetch=1,
            grid=(steps,),
            in_specs=[
                line, tiled(step, width), tiled(room, width), tiled(room, hidden), tiled(step, padded),
                *[pl.BlockSpec(memory_space=pl.ANY)] * 5,
            ],
            out_specs=[
                tiled(step, width // 2), tiled(step, width // 2),
                *[tiled(step, cols) for cols in widths], line,
                tiled(room, width),
                tiled(room, width), tiled(room, hidden), tiled(room, hidden),
                tiled(room, hidden), tiled(step, padded), tiled(step, 2 * padded),
            ],
            scratch_shapes=[
                *[pltpu.VMEM(w.shape, BF16) for w in (w_gate, w_up, w_down, w_shared, w_sdown)],
                pltpu.SemaphoreType.DMA((5,)),
            ],
        ),
        out_shape=[
            shape(tokens, width // 2), shape(tokens, width // 2),
            *[shape(tokens, cols) for cols in widths],
            jax.ShapeDtypeStruct((steps, 1, step), F32),
            shape(steps * room, width), shape(steps * room, width), shape(steps * room, hidden),
            shape(steps * room, hidden), shape(steps * room, hidden), shape(tokens, padded),
            shape(tokens, 2 * padded),
        ],
        compiler_params=pltpu.CompilerParams(vmem_limit_bytes=62 << 20),
        cost_estimate=pl.CostEstimate(
            flops=flops, bytes_accessed=130_000_000, transcendentals=5_000_000
        ),
        name="experts",
    )(me, place, hidden2, *c_kept, w_gate, w_up, w_down, w_shared, w_sdown)
    return [*outs[:2], list(outs[2 : 2 + n_parts]), *outs[2 + n_parts :]]

def places_of(hit):
    count = hit.shape[1]
    upper = (
        lax.broadcasted_iota(jnp.int32, (count, count), 0)
        < lax.broadcasted_iota(jnp.int32, (count, count), 1)
    ).astype(BF16)
    return matmul(hit.astype(BF16), upper).astype(jnp.int32)


def per_device(
    sizes,
    tokens,
    cotangent,
    gain_attn,
    w_query,
    w_latent,
    gain_latent,
    w_keyval,
    w_output,
    gain_ffn,
    w_shared_gate,
    w_shared_up,
    w_shared_down,
    w_router,
    expert_gate,
    expert_up,
    expert_down,
    segments,
    positions,
    routes,
):
    n_group, n_expert, n_shard = sizes
    n_row = n_expert * n_shard
    n_all = n_group * n_row
    tok_rows, width = tokens.shape
    row_tokens = segments.shape[0]
    n_prompt = row_tokens // GROUP_TOK
    e_per_prompt = n_expert // n_prompt
    group_at = lax.axis_index("group")
    expert_at = lax.axis_index("expert")
    shard_at = lax.axis_index("shard")
    row_at = expert_at * n_shard + shard_at
    prompt_at = expert_at // e_per_prompt
    head_group = expert_at % e_per_prompt

    seg_block = segments[::BLOCK]
    pos_block = positions[::BLOCK]
    prompt_of = seg_block // (NCONT + 1)
    prompt_of = prompt_of - jnp.min(prompt_of)
    cont_of = seg_block % (NCONT + 1)
    piece = jnp.where(cont_of == 0, pos_block // BLOCK, PROMPT // BLOCK - 1 + cont_of)
    slot_of = prompt_of * GROUP_BLOCKS + piece
    block_ids = jnp.arange(n_row, dtype=jnp.int32)
    block_at = jnp.sum(
        jnp.where(slot_of[None, :] == block_ids[:, None], block_ids[None, :], 0), axis=1
    )
    my_blocks = lax.dynamic_slice_in_dim(block_at, prompt_at * GROUP_BLOCKS, GROUP_BLOCKS)
    local_slot = slot_of - prompt_at * GROUP_BLOCKS
    mine = (local_slot >= 0) & (local_slot < GROUP_BLOCKS)
    local_slot = jnp.clip(local_slot, 0, GROUP_BLOCKS - 1)
    own_prompt = jnp.sum(jnp.where(block_ids == row_at, prompt_of, 0))

    def to_pieces(all_rows):
        return take_blocks(all_rows.reshape(n_row, BLOCK, -1), my_blocks).reshape(GROUP_TOK, -1)

    def from_pieces(rows):
        return take_blocks(rows.reshape(GROUP_BLOCKS, BLOCK, -1), local_slot)

    def heads_home(rows):
        got = trade(from_pieces(rows), ROW)
        if n_prompt > 1:
            got = lax.dynamic_slice_in_dim(got, own_prompt * GROUP_BLOCKS, GROUP_BLOCKS)
        return jnp.swapaxes(got, 0, 1).reshape(BLOCK, -1)

    def heads_out(rows):
        split = jnp.swapaxes(rows.reshape(BLOCK, HEADS, -1), 0, 1)
        if n_prompt > 1:
            split = jnp.tile(split, (n_prompt, 1, 1))
            keep = (block_ids // GROUP_BLOCKS) == own_prompt
            split = jnp.where(keep[:, None, None], split, jnp.zeros_like(split))
        return to_pieces(trade(split, ROW))

    def head_parts(weight, per_head):
        cols = lax.dynamic_slice_in_dim(
            weight, head_group * (n_shard * per_head), n_shard * per_head, axis=1
        )
        return jnp.swapaxes(cols.reshape(-1, n_shard, per_head), 0, 1)

    def head_columns(weight, per_head):
        return trade(head_parts(weight, per_head), "shard").reshape(-1, per_head)

    def unit_columns(weight):
        units = weight.shape[1] // n_row
        cols = weight.reshape(weight.shape[0], n_shard, n_expert, units)
        cols = lax.dynamic_index_in_dim(cols, expert_at, axis=2, keepdims=False)
        return jnp.swapaxes(cols, 0, 1)

    paired = (n_group, n_expert) == (2, 4)
    x_at, core_at = expert_at // 2, expert_at % 2

    def sub_rows(weight):
        part = weight.shape[0] // (n_group * n_expert)
        at = (group_at * n_expert + expert_at) * part
        return lax.dynamic_slice_in_dim(weight, at, part)

    def gather_rows_at_once(weight):
        return lax.all_gather(sub_rows(weight), ("shard", "group", "expert"), tiled=True)

    def spread(part):
        return trade(jnp.broadcast_to(part, (n_shard,) + part.shape), "shard")

    def scatter_rows_of_row(part):
        part = part.reshape(2, 2, n_shard * tok_rows, -1)

        def halve(rows, axis, bit, flip):
            send = lax.dynamic_index_in_dim(rows, 1 - bit, axis, keepdims=False)
            keep = lax.dynamic_index_in_dim(rows, bit, axis, keepdims=False)
            got = lax.ppermute(send, "expert", [(i, i ^ flip) for i in range(4)])
            return (keep.astype(F32) + got.astype(F32)).astype(BF16)

        part = halve(halve(part, 1, core_at, 1), 0, x_at, 2)
        return over_shards(part.reshape(n_shard, tok_rows, -1))

    def gather_rows(weight):
        if not paired:
            return gather_rows_at_once(weight)
        got = spread(sub_rows(weight))
        got = pair_gather(got, "expert", 4, 2, x_at)
        got = pair_gather(got, "group", 2, 1, group_at)
        got = pair_gather(got, "expert", 4, 1, core_at)
        return jnp.transpose(got, (3, 1, 2, 0, 4, 5)).reshape(width, -1)

    def swap(rows, axis, count, flip):
        return lax.ppermute(
            rows.astype(BF16), axis, [(i, i ^ flip) for i in range(count)]
        ).astype(F32)

    def scatter_start(left, right, extra=None):
        if not paired:
            whole = matmul_tn(left, right)
            if extra is not None:
                whole = jnp.concatenate([whole, extra], axis=1)
            return whole
        block = left.shape[1] // 8

        def half(core):
            cols = left.reshape(-1, 4, 2, block)
            cols = lax.dynamic_index_in_dim(cols, core, axis=2, keepdims=False)
            out = matmul_tn(cols.reshape(-1, 4 * block), right)
            if extra is not None:
                more = extra.reshape(4, 2, block, -1)
                more = lax.dynamic_index_in_dim(more, core, axis=1, keepdims=False)
                out = jnp.concatenate([out, more.reshape(4 * block, -1)], axis=1)
            return out

        return half(core_at) + swap(half(1 - core_at), "expert", 4, 1)

    def scatter_step(rows, axis, count, flip, bit):
        if not paired:
            return rows
        size = rows.shape[0] // 2
        send = lax.dynamic_slice_in_dim(rows, (1 - bit) * size, size)
        return lax.dynamic_slice_in_dim(rows, bit * size, size) + swap(send, axis, count, flip)

    def scatter_y(rows):
        return scatter_step(rows, "group", 2, 1, group_at)

    def scatter_x(rows):
        return scatter_step(rows, "expert", 4, 2, x_at)

    def scatter_end(rows):
        if not paired:
            return lax.psum_scatter(rows.astype(BF16), ALL, scatter_dimension=0, tiled=True).astype(
                F32
            )
        return over_shards(rows.astype(BF16).reshape(n_shard, -1, rows.shape[1]))

    def over_shards(rows):
        return jnp.sum(trade(rows, "shard").astype(F32), axis=0)

    expert_count = w_router.shape[1]
    top_count = routes.shape[1]
    route_hot = jnp.any(
        routes[:, :, None] == jnp.arange(expert_count, dtype=jnp.int32)[None, None, :], axis=1
    )
    pos_p = jnp.arange(GROUP_TOK, dtype=jnp.int32)
    pos_p = jnp.where(pos_p < PROMPT, pos_p, PROMPT + pos_p % BLOCK)
    cos_p, sin_p = angles(pos_p, ROPE)
    tok_all = lax.all_gather(tokens, ROW, axis=0, tiled=True)
    hit_b = trade(route_hot.T.astype(F32), ROW) > 0.5
    cotangent_late, cos_p, sin_p, hit_b = lax.optimization_barrier(
        (cotangent, cos_p, sin_p, hit_b)
    )
    c_all = lax.all_gather(cotangent_late, ROW, axis=0, tiled=True)
    units = w_shared_gate.shape[1] // n_row
    wq_h = head_columns(w_query, QDIM)
    wkv_h = head_columns(w_keyval, KVDIM)
    w_lr = gather_rows(jnp.concatenate([w_latent, w_router], axis=1))
    w_l, w_r = w_lr[:, : LATENT + ROPE], w_lr[:, LATENT + ROPE :]
    w_joint = jnp.concatenate([wq_h[:, :NOPE], w_l[:, :LATENT], wq_h[:, NOPE:], w_l[:, LATENT:]], 1)
    w_o_near = w_output
    if paired:
        w_o_near = pair_gather(spread(sub_rows(w_output)), "expert", 4, 2, x_at)
    gu_parts = jnp.concatenate([unit_columns(w_shared_gate), unit_columns(w_shared_up)], axis=-1)
    w_joint, wkv_h, tok_all, w_o_near, gu_parts = lax.optimization_barrier(
        (w_joint, wkv_h, tok_all, w_o_near, gu_parts)
    )
    w_gu = trade(gu_parts, "shard").reshape(width, 2 * units)
    if paired:
        w_o_near = pair_gather(w_o_near, "group", 2, 1, group_at)

    capacity = 3 * tok_rows * top_count // (2 * expert_count)
    ahead = capacity * (jnp.arange(n_row, dtype=jnp.int32)[:, None] % 2)
    place = jnp.where(hit_b, places_of(hit_b) + ahead, 1 << 20).reshape(-1, 1, 2 * tok_rows)

    hidden1, query, key, value, comp = project(
        tok_all.reshape(n_row, BLOCK, width),
        my_blocks,
        gain_attn,
        w_joint,
        gain_latent,
        wkv_h,
        cos_p,
        sin_p,
    )
    mixed_f, mixed_h, total_h = attend(query, key, value)
    mixed_h, w_o_near, w_gu = lax.optimization_barrier((mixed_h, w_o_near, w_gu))
    mixed = heads_home(mixed_h)
    if paired:
        w_o = pair_gather(w_o_near, "expert", 4, 1, core_at)
        w_o = jnp.transpose(w_o, (3, 1, 2, 0, 4, 5)).reshape(width, -1)
    else:
        w_o = gather_rows_at_once(w_o_near)
    padded = -(-(units + expert_count) // 128) * 128
    space = lambda cols: jnp.zeros((width, cols), BF16)
    w_sh = jnp.concatenate(
        [
            w_gu[:, :units],
            w_r,
            space(padded - units - expert_count),
            w_gu[:, units:],
            space(padded - units),
        ],
        axis=1,
    )
    w_sd = lax.dynamic_slice_in_dim(w_shared_down, expert_at * units, units)
    w_sd = jnp.pad(w_sd, ((0, padded - units), (0, 0)))

    inputs = tokens.astype(F32)
    grad_out = cotangent.astype(F32)
    normed1, inverse1 = rms_parts(inputs)
    hidden1_own = (normed1 * gain_attn).astype(BF16)
    latent_own = matmul(hidden1_own, w_l)
    normed_c, inverse_c = rms_parts(latent_own[:, :LATENT])
    after = inputs + matmul(mixed, w_o)
    normed2, inverse2 = rms_parts(after)
    hidden2 = (normed2 * gain_ffn).astype(BF16)
    logits = matmul(hidden2, w_r)
    router_prob = jax.nn.softmax(logits, axis=-1)

    hidden2, c_all, w_sh = lax.optimization_barrier((hidden2, c_all, w_sh))
    h2_all = lax.all_gather(hidden2, ROW, axis=0, tiled=True)
    c_kept = cotangent_rows(place, capacity, c_all, expert_down[0], w_sd)
    h2_all, w_query, c_kept = lax.optimization_barrier((h2_all, w_query, c_kept))
    w_q = gather_rows_at_once(w_query)
    out_a, out_b, dh_parts, d_prob_col, rows, d_out, e_mid, d_gate, d_up, s_mid, ds_gu = experts(
        row_at[None],
        place,
        capacity,
        h2_all,
        c_kept,
        expert_gate[0],
        expert_up[0],
        expert_down[0],
        w_sh,
        w_sd,
        units,
        expert_count,
        [width - SIDE, SIDE] if paired else [width],
    )
    d_prob = trade(d_prob_col.reshape(n_row, tok_rows), ROW).T
    dh_parts, w_q = lax.optimization_barrier((dh_parts, w_q))
    d_h2 = lax.psum_scatter(dh_parts[0], ROW, scatter_dimension=0, tiled=True).astype(F32)
    if paired:
        d_h2 = jnp.concatenate([d_h2, scatter_rows_of_row(dh_parts[1])], axis=1)
    d_prob = jnp.where(route_hot, d_prob, 0.0)
    d_logits = (
        router_prob * (d_prob - jnp.sum(router_prob * d_prob, axis=-1, keepdims=True))
    ).astype(BF16)
    grad_router = matmul_tn(hidden2, d_logits)

    def share(whole):
        if n_group != 2:
            return lax.psum_scatter(
                whole.astype(BF16), "group", scatter_dimension=0, tiled=True
            ), None
        half = whole.shape[0] // 2
        send = lax.dynamic_slice_in_dim(whole, (1 - group_at) * half, half).astype(BF16)
        keep = lax.dynamic_slice_in_dim(whole, group_at * half, half)
        return lax.ppermute(send, "group", [(0, 1), (1, 0)]), keep

    whole_0 = matmul_tn(rows, d_gate)
    d_up, ds_gu, whole_0 = lax.optimization_barrier((d_up, ds_gu, whole_0))
    got_0, keep_0 = share(whole_0)
    whole_1 = matmul_tn(rows, d_up)
    grad_gu = matmul_tn(h2_all, ds_gu).astype(BF16)
    e_mid, s_mid, whole_1, got_0, grad_gu = lax.optimization_barrier(
        (e_mid, s_mid, whole_1, got_0, grad_gu)
    )
    got_1, keep_1 = share(whole_1)
    whole_2 = matmul_tn(e_mid, d_out)
    grad_sd_part = matmul_tn(s_mid, c_all)[:units].astype(BF16)
    d_h2, whole_2, grad_sd_part = lax.optimization_barrier((d_h2, whole_2, grad_sd_part))
    whole_2, _ = lax.optimization_barrier((whole_2, got_1))
    got_2, keep_2 = share(whole_2)
    grad_gu = jnp.concatenate(
        [grad_gu[:, :units], grad_gu[:, padded : padded + units]], axis=1
    ).reshape(n_all, width // n_all, 2 * units)
    grad_sd_part = grad_sd_part.reshape(n_group, units // n_group, width)
    d_h2, out_a, out_b, grad_gu, grad_sd_part, grad_router, d_logits = lax.optimization_barrier(
        (d_h2, out_a, out_b, grad_gu, grad_sd_part, grad_router, d_logits)
    )
    ffn_a = lax.psum_scatter(out_a, ROW, scatter_dimension=0, tiled=True)

    d_hidden2 = d_h2 + matmul_nt(d_logits, w_r)
    d_after, grad_gain_ffn = norm_back(d_hidden2, normed2, inverse2, gain_ffn)
    grad_after = grad_out + d_after
    grad_attn = grad_after.astype(BF16)
    d_mixed = matmul_nt(grad_attn, w_o).astype(BF16)
    d_mixed_h = heads_out(d_mixed)
    wo_rows = scatter_start(mixed, grad_attn)
    d_mixed_h, grad_gu, grad_sd_part, got_1, wo_rows = lax.optimization_barrier(
        (d_mixed_h, grad_gu, grad_sd_part, got_1, wo_rows)
    )
    wo_rows = scatter_y(wo_rows)
    gu_got = trade(grad_gu, ALL)
    sd_gots = []
    for turn in range(n_group):
        piece_at = (group_at + turn) % n_group
        moves = []
        for g in range(n_group):
            for e in range(n_expert):
                for s in range(n_shard):
                    target = (s * n_expert + e) * n_group + (g + turn) % n_group
                    moves.append(((g * n_expert + e) * n_shard + s, target))
        sent = lax.dynamic_index_in_dim(grad_sd_part, piece_at, axis=0, keepdims=False)
        sd_gots.append(lax.ppermute(sent, ALL, moves))

    d_query, d_key, d_value = attend_back(
        query, key, value, mixed_f, total_h, d_mixed_h, cos_p, sin_p
    )
    d_keyval, d_latent_part = latent_back(d_key, d_value, wkv_h, local_slot, mine)
    own_pos = lax.dynamic_slice_in_dim(positions, row_at * tok_rows, tok_rows)
    cosine, sine = angles(own_pos, ROPE)
    d_latent_part, ffn_a, gu_got, sd_gots, wo_rows, cosine, sine = lax.optimization_barrier(
        (d_latent_part, ffn_a, gu_got, sd_gots, wo_rows, cosine, sine)
    )
    d_lat = lax.psum_scatter(d_latent_part, ROW, scatter_dimension=0, tiled=True)
    d_query_own = heads_home(d_query)
    grad_wq_h = matmul_tn(hidden1, d_query).astype(BF16).reshape(n_all, width // n_all, QDIM)
    grad_wkv_h = matmul_tn(comp, d_keyval).astype(BF16)
    grad_wkv_h = grad_wkv_h.reshape(n_all, width // n_all, -1)
    head_got = trade(jnp.concatenate([grad_wq_h, grad_wkv_h], axis=-1), ALL)
    wo_rows = scatter_x(wo_rows)
    egrads = [
        (got.astype(F32) if keep is None else keep + got.astype(F32))[None]
        for got, keep in ((got_0, keep_0), (got_1, keep_1), (got_2, keep_2))
    ]
    d_lat, d_query_own, wo_rows, egrads, out_b, head_got = lax.optimization_barrier(
        (d_lat, d_query_own, wo_rows, egrads, out_b, head_got)
    )
    egrad_gate, egrad_up, egrad_down = egrads
    d_lat = d_lat.astype(F32)
    ffn_b = lax.psum_scatter(out_b, ROW, scatter_dimension=0, tiled=True)
    grad_wo = scatter_end(wo_rows)
    output = (after + jnp.concatenate([ffn_a, ffn_b], axis=1).astype(F32)).astype(BF16)
    got = gu_got.astype(F32)
    got = jnp.sum(got.reshape(n_group, n_expert, n_shard, -1, 2 * units), axis=0)
    got = jnp.transpose(got, (2, 1, 0, 3))
    grad_sg = got[..., :units].reshape(got.shape[0], -1)
    grad_su = got[..., units:].reshape(got.shape[0], -1)
    grad_sd = sum(got.astype(F32) for got in sd_gots)

    got = head_got.astype(F32)
    got = jnp.sum(got.reshape(n_group * n_prompt, HEADS, got.shape[1], got.shape[2]), axis=0)
    grad_wq = jnp.swapaxes(got[..., :QDIM], 0, 1).reshape(got.shape[1], -1)
    grad_wkv = jnp.swapaxes(
        got[..., QDIM:].reshape(HEADS, LATENT // n_all, KVDIM), 0, 1
    ).reshape(LATENT // n_all, -1)

    d_lat_c, grad_gain_latent = norm_back(d_lat[:, :LATENT], normed_c, inverse_c, gain_latent)
    d_latent = jnp.concatenate([d_lat_c, unrotate(d_lat[:, LATENT:], cosine, sine)], axis=1).astype(
        BF16
    )
    d_hidden1 = matmul_nt(d_query_own, w_q) + matmul_nt(d_latent, w_l)
    d_tok, grad_gain_attn = norm_back(d_hidden1, normed1, inverse1, gain_attn)
    grad_tokens = grad_after + d_tok
    own = width // n_all
    lat = LATENT // n_all
    gain_l = jnp.pad(grad_gain_latent.reshape(n_all, lat), ((0, 0), (0, own - lat)))
    beside = jnp.concatenate(
        [
            grad_router,
            grad_gain_attn[:, None],
            grad_gain_ffn[:, None],
            gain_l.reshape(width, 1),
        ],
        axis=1,
    )
    beside = jnp.pad(beside, ((0, 0), (0, -(LATENT + ROPE + expert_count + 3) % 128)))
    sums = scatter_end(scatter_x(scatter_y(scatter_start(hidden1_own, d_latent, beside))))
    grad_wl = sums[:, : LATENT + ROPE]
    at = LATENT + ROPE + expert_count
    grad_r, grad_ga, grad_gf, grad_gl = (
        sums[:, LATENT + ROPE : at],
        sums[:, at],
        sums[:, at + 1],
        sums[:lat, at + 2],
    )
    return (
        output,
        grad_tokens,
        grad_ga,
        grad_wq,
        grad_wl,
        grad_gl,
        grad_wkv,
        grad_wo,
        grad_gf,
        grad_sg,
        grad_su,
        grad_sd,
        grad_r,
        egrad_gate,
        egrad_up,
        egrad_down,
    )


def solution(mesh):
    sizes = tuple(mesh.shape[name] for name in ALL)
    return jax.shard_map(
        functools.partial(per_device, sizes),
        mesh=mesh,
        in_specs=(
            P(ALL, None),
            P(ALL, None),
            P(),
            P("shard", None),
            P("shard", None),
            P(),
            P("shard", None),
            P("shard", None),
            P(),
            P("shard", None),
            P("shard", None),
            P("shard", None),
            P("shard", None),
            P(ROW, None, None),
            P(ROW, None, None),
            P(ROW, None, None),
            P("group"),
            P("group"),
            P(ALL, None),
        ),
        out_specs=(
            P(ALL, None),
            P(ALL, None),
            P(ALL),
            P(ALL, None),
            P(ALL, None),
            P(ALL),
            P(ALL, None),
            P(ALL, None),
            P(ALL),
            P(ALL, None),
            P(ALL, None),
            P(ALL, None),
            P(ALL, None),
            P(ROW, "group", None),
            P(ROW, "group", None),
            P(ROW, "group", None),
        ),
        check_vma=False,
    )
```
